32 devices in a mesh: dp: 8 (over z, x), mp: 4 (over y, core).
Axes of the slice: x: 2, y: 2, z: 4, core: 2. Of those that a mesh axis runs over, the one named last changes fastest.
Arguments:
- hidden_in: bfloat16 [16, 1024, 768], P(None, 'dp'), may hold values from -12 to 12
- cotangent: bfloat16 [16, 1024, 768], P(None, 'dp'), may hold values from -6 to 6
- lengths: int32 [16], replicated, may hold values from 1 to 1024, 9830 in all
- labels: int32 [16], replicated, may hold values from 0 to 13
- qkv_weight: bfloat16 [3, 768, 768], P(None, 'dp', 'mp'), may hold values from -0.15625 to 0.15625
- qv_bias: bfloat16 [12, 128], P('mp', 'dp'), may hold values from -1.796875 to 1.796875
- out_weight: bfloat16 [768, 768], P('mp', 'dp'), may hold values from -1.25 to 1.25
- out_bias: bfloat16 [768], P('dp'), may hold values from -1.796875 to 1.796875
- norm1_gain: bfloat16 [768], P('dp'), may hold values from 0.5 to 1.5
- norm1_bias: bfloat16 [768], P('dp'), may hold values from -1.796875 to 1.796875
- up_weight: bfloat16 [768, 3072], P('dp', 'mp'), may hold values from -0.21875 to 0.21875
- up_bias: bfloat16 [48, 64], P('mp', 'dp'), may hold values from -1.796875 to 1.796875
- down_weight: bfloat16 [3072, 768], P('mp', 'dp'), may hold values from -0.15625 to 0.15625
- down_bias: bfloat16 [768], P('dp'), may hold values from -1.796875 to 1.796875
- norm2_gain: bfloat16 [768], P('dp'), may hold values from 0.5 to 1.5
- norm2_bias: bfloat16 [768], P('dp'), may hold values from -1.796875 to 1.796875
- student_weight: bfloat16 [768, 128], P('dp'), may hold values from -0.21875 to 0.21875
- student_bias: bfloat16 [128], P('dp'), may hold values from -3 to 3
- pool_query: bfloat16 [128], P('dp'), may hold values from -9 to 9
- pooler_weight: bfloat16 [128, 128], P('dp'), may hold values from -0.5 to 0.5
- pooler_bias: bfloat16 [128], P('dp'), may hold values from -1.796875 to 1.796875
- class_weight: bfloat16 [128, 14], P('dp'), may hold values from -1 to 1
- class_bias: bfloat16 [14], replicated, may hold values from -6 to 6
Outputs:
- hidden_out: bfloat16 [16, 1024, 768], P(None, 'dp')
- logits: float32 [16, 14], replicated
- input_grad: bfloat16 [16, 1024, 768], P(None, 'dp')
- qkv_weight_grad: float32 [3, 768, 768], P(None, 'dp', 'mp')
- qv_bias_grad: float32 [12, 128], P('mp', 'dp')
- out_weight_grad: float32 [768, 768], P('mp', 'dp')
- out_bias_grad: float32 [768], P('dp')
- norm1_gain_grad: float32 [768], P('dp')
- norm1_bias_grad: float32 [768], P('dp')
- up_weight_grad: float32 [768, 3072], P('dp', 'mp')
- up_bias_grad: float32 [48, 64], P('mp', 'dp')
- down_weight_grad: float32 [3072, 768], P('mp', 'dp')
- down_bias_grad: float32 [768], P('dp')
- norm2_gain_grad: float32 [768], P('dp')
- norm2_bias_grad: float32 [768], P('dp')
- student_weight_grad: float32 [768, 128], P('dp')
- student_bias_grad: float32 [128], P('dp')
- pool_query_grad: float32 [128], P('dp')
- pooler_weight_grad: float32 [128, 128], P('dp')
- pooler_bias_grad: float32 [128], P('dp')
- class_weight_grad: float32 [128, 14], P('dp')
- class_bias_grad: float32 [14], replicated
- rms_stats: float32 [4], replicated
The draws below stay inside these ranges and needn't reach their ends.
Inputs may be any that keep to these rules, and one draw needn't show every extreme that they name: `lengths`: every sequence has at least one live position, and some sequence fills its whole slot of 1024 positions.
All inputs are finite; a program needn't handle non-finite values.
Results may differ from the reference program's by a relative error of at most 0.03.
Values may be sent and summed in bfloat16 or wider, within the bound.
No kernel may reach another device: no remote copies, remote signals or barrier semaphores. Data moves between devices by JAX's collectives and lax.ppermute only.
A program may use at most 192 MiB of HBM per device.

```python
import math
import jax
import jax.numpy as jnp
import numpy as np
from jax import lax

H = 12
HS = 64
D = 768
FF = 3072
CW = 128
PH = 2
CLASSES = 14
SLOT = 1024
SEQS = 16
N_MP = 4


def set_ends(values, rng, least, largest):
    shape = values.shape
    place = [jax.random.randint(jax.random.fold_in(rng, axis), (), 0, shape[axis]) for axis in range(len(shape))]
    values = values.at[tuple(place)].set(least)
    longest = shape.index(max(shape))
    place[longest] = (place[longest] + 1) % shape[longest]
    return values.at[tuple(place)].set(largest)


def levels(rng, dims, pieces, low, largest):
    def one(position, parts):
        draws = jax.random.uniform(jax.random.fold_in(jax.random.fold_in(rng, 6), position), (parts,), jnp.float32, low / len(pieces), largest / len(pieces))
        return jnp.repeat(jnp.exp(draws), dims[position] // parts).reshape((-1,) + (1,) * (len(dims) - position - 1))

    factor_of = one(*pieces[0])
    for cut in pieces[1:]:
        factor_of = factor_of * one(*cut)
    return factor_of


def length_profile(count, total, reach, slope):
    weights = [(1 << 20) // math.isqrt(standing ** slope) + 1 for standing in range(2, count + 1)]
    spare, given = total - reach - (count - 1), [1] * (count - 1)
    while spare > 0:
        candidates = [i for i in range(count - 1) if given[i] < reach]
        whole, remaining = sum([weights[i] for i in candidates]), spare
        for i in candidates:
            more = min(reach - given[i], max(1, remaining * weights[i] // whole), spare)
            given[i] = given[i] + more
            spare = spare - more
    return np.array([reach] + given)


def ragged(stream_key, number_of, total, reach, lean):
    if number_of == 2:
        one = jax.random.randint(stream_key, (), max(1, total - reach), min(reach, total - 1) + 1)
        return jnp.stack([one, total - one])
    sizes = jnp.asarray(length_profile(number_of, total, reach, lean), jnp.int32)
    couples = (number_of - 1) // 2
    donor, receiver = sizes[1:1 + 2 * couples:2], sizes[2:2 + 2 * couples:2]
    room = jnp.minimum(donor - 1, reach - receiver)
    passed = jax.random.randint(jax.random.fold_in(stream_key, 1), (couples,), 0, 1 << 20) % (room + 1)
    sizes = sizes.at[1:1 + 2 * couples:2].set(donor - passed).at[2:2 + 2 * couples:2].set(receiver + passed)
    return sizes[jax.random.permutation(jax.random.fold_in(stream_key, 2), number_of)]


def bell_draw(rng, shape, width, limit, pieces=(), kind=jnp.bfloat16):
    factor_of = levels(rng, shape, pieces, -0.22, 0.18) if pieces else 1.0
    array = jax.random.normal(rng, shape, jnp.float32) * width * factor_of
    return jnp.minimum(jnp.maximum(array, -limit), limit).astype(kind)


def setup_inputs(seed: int = 0) -> dict:
    splits = jax.random.split(jax.random.key(seed), 24)
    hidden_in = bell_draw(splits[0], (SEQS, SLOT, D), 2.0, 12.0, ((1, 8),))
    cotangent = bell_draw(splits[1], (SEQS, SLOT, D), 1.0, 6.0, ((1, 8),))
    lengths = ragged(splits[2], SEQS, SEQS * SLOT * 3 // 5, SLOT, 2).astype(jnp.int32)
    labels = set_ends(jax.random.randint(splits[3], (SEQS,), 0, CLASSES), jax.random.fold_in(splits[3], 1), 0, CLASSES - 1).astype(jnp.int32)
    qkv_weight = bell_draw(splits[4], (3, D, D), (2 * D) ** -0.5, 0.15625, ((1, 8), (2, 4)))
    qv_bias = bell_draw(splits[5], (H, 2 * HS), 0.3, 1.796875, ((0, 4), (1, 8)))
    out_weight = bell_draw(splits[6], (D, D), (D // 32) ** -0.5, 1.25, ((0, 4), (1, 8)))
    out_bias = bell_draw(splits[7], (D,), 0.3, 1.796875, ((0, 8),))
    norm1_gain = jnp.clip(1.0 + 0.1 * jax.random.normal(splits[8], (D,), jnp.float32), 0.5, 1.5).astype(jnp.bfloat16)
    norm1_bias = bell_draw(splits[9], (D,), 0.3, 1.796875, ((0, 8),))
    up_weight = bell_draw(splits[10], (D, FF), D ** -0.5, 0.21875, ((0, 8), (1, 4)))
    up_bias = bell_draw(splits[11], (FF // 64, 64), 0.3, 1.796875, ((0, 4), (1, 8)))
    down_weight = bell_draw(splits[12], (FF, D), (FF // 2) ** -0.5, 0.15625, ((0, 4), (1, 8)))
    down_bias = bell_draw(splits[13], (D,), 0.3, 1.796875, ((0, 8),))
    norm2_gain = jnp.clip(1.0 + 0.1 * jax.random.normal(splits[14], (D,), jnp.float32), 0.5, 1.5).astype(jnp.bfloat16)
    norm2_bias = bell_draw(splits[15], (D,), 0.3, 1.796875, ((0, 8),))
    student_weight = bell_draw(splits[16], (D, CW), D ** -0.5, 0.21875, ((0, 8),))
    student_bias = bell_draw(splits[17], (CW,), 0.5, 3.0, ((0, 8),))
    pool_query = bell_draw(splits[18], (CW,), 1.5, 9.0, ((0, 8),))
    pooler_weight = bell_draw(splits[19], (CW, CW), CW ** -0.5, 0.5, ((0, 8),))
    pooler_bias = bell_draw(splits[20], (CW,), 0.3, 1.796875, ((0, 8),))
    class_weight = bell_draw(splits[21], (CW, CLASSES), (CW // 4) ** -0.5, 1.0, ((0, 8),))
    class_bias = bell_draw(splits[22], (CLASSES,), 1.0, 6.0)
    return dict(hidden_in=hidden_in, cotangent=cotangent, lengths=lengths, labels=labels, qkv_weight=qkv_weight, qv_bias=qv_bias, out_weight=out_weight, out_bias=out_bias, norm1_gain=norm1_gain, norm1_bias=norm1_bias, up_weight=up_weight, up_bias=up_bias, down_weight=down_weight, down_bias=down_bias, norm2_gain=norm2_gain, norm2_bias=norm2_bias, student_weight=student_weight, student_bias=student_bias, pool_query=pool_query, pooler_weight=pooler_weight, pooler_bias=pooler_bias, class_weight=class_weight, class_bias=class_bias)


@jax.custom_vjp
def low(v):
    return lax.optimization_barrier(v.astype(jnp.bfloat16)).astype(jnp.float32)

@jax.custom_vjp
def low_back(v):
    return v

def low_keep(v):
    return (low(v), None)

def low_pass(kept, grad):
    return (grad,)

def back_keep(v):
    return (v, None)

def back_low(kept, grad):
    return (low(grad),)
low.defvjp(low_keep, low_pass)
low_back.defvjp(back_keep, back_low)
EPSILON = 1e-06
NEGATIVE = -1e+30
HIGHEST = lax.Precision.HIGHEST

def layer_norm(values, gain, shift):
    center = values - lax.optimization_barrier(jnp.mean(values, -1, keepdims=True))
    spread = lax.optimization_barrier(jnp.mean(center * center, -1, keepdims=True))
    return center * lax.rsqrt(spread + EPSILON) * gain + shift

def one_sequence(params, tokens, seq_length, seq_label):
    qkv_weight, qv_bias, out_weight, out_bias, norm1_gain, norm1_bias, up_weight, up_bias, down_weight, down_bias, norm2_gain, norm2_bias, student_weight, student_bias, pool_query, pooler_weight, pooler_bias, class_weight, class_bias = params
    live_keys = jnp.arange(SLOT) < seq_length
    projected = jnp.einsum('td,cde->cte', tokens, qkv_weight, precision=HIGHEST)
    query_bias = qv_bias[:, :HS].reshape(D)
    value_bias = qv_bias[:, HS:].reshape(D)
    queries = low_back(low(projected[0] + query_bias)).reshape(SLOT, H, HS)
    key_rows = low_back(low(projected[1])).reshape(SLOT, H, HS)
    value_rows = low_back(low(projected[2] + value_bias)).reshape(SLOT, H, HS)
    raw_scores = low_back(jnp.einsum('qhe,khe->hqk', queries, key_rows, precision=HIGHEST))
    scores = jnp.where(live_keys[None, None, :], raw_scores * HS ** (-0.5), NEGATIVE)
    weights_att = jax.nn.softmax(scores, axis=-1)
    context = jnp.einsum('hqk,khe->qhe', low(weights_att), value_rows, precision=HIGHEST).reshape(SLOT, D)
    context = low_back(low(context))
    partial_attn = jnp.einsum('tgf,gfd->gtd', context.reshape(SLOT, N_MP, D // N_MP), out_weight.reshape(N_MP, D // N_MP, D), precision=HIGHEST)
    attention = low_back(lax.optimization_barrier(jnp.sum(low(partial_attn), axis=0))) + out_bias
    first = layer_norm(tokens + attention, norm1_gain, norm1_bias)
    before = low_back(jnp.dot(low(first), up_weight, precision=HIGHEST) + up_bias.reshape(FF))
    active = low(jax.nn.gelu(before, approximate=False))
    partial_ffn = jnp.einsum('tgf,gfd->gtd', active.reshape(SLOT, N_MP, FF // N_MP), down_weight.reshape(N_MP, FF // N_MP, D), precision=HIGHEST)
    feed = low_back(lax.optimization_barrier(jnp.sum(low(partial_ffn), axis=0))) + down_bias
    second = layer_norm(first + feed, norm2_gain, norm2_bias)
    student = low_back(jnp.dot(low(second), student_weight, precision=HIGHEST) + student_bias)
    pool_heads = student.reshape(SLOT, PH, CW // PH)
    pool_logit = jnp.einsum('the,he->th', pool_heads, pool_query.reshape(PH, CW // PH), precision=HIGHEST) * (CW // PH) ** (-0.5)
    pool_logit = jnp.where(live_keys[:, None], pool_logit, NEGATIVE)
    pool_weights = jax.nn.softmax(pool_logit, axis=0)
    pooled = jnp.einsum('th,the->he', pool_weights, pool_heads, precision=HIGHEST).reshape(CW)
    hidden_cls = jnp.tanh(jnp.dot(pooled, pooler_weight, precision=HIGHEST) + pooler_bias)
    logit_row = jnp.dot(hidden_cls, class_weight, precision=HIGHEST) + class_bias
    onehot = (jnp.arange(CLASSES) == seq_label).astype(logit_row.dtype)
    loss = jax.nn.logsumexp(logit_row) - jnp.sum(onehot * logit_row)
    live_float = live_keys.astype(tokens.dtype)
    sums = jnp.stack([jnp.sum(live_float * lax.optimization_barrier(jnp.sum(stream * stream, -1))) for stream in (tokens, attention, first, feed)])
    return (second, logit_row, loss, sums)

def forward(params, tokens_all, lengths, labels):
    checked = jax.checkpoint(one_sequence)

    def step(carry, item):
        tokens, seq_length, seq_label = item
        second, logit_row, loss, sums = checked(params, tokens, seq_length, seq_label)
        return ((carry[0] + loss, carry[1] + sums), (second, logit_row))
    start = (jnp.zeros((), tokens_all.dtype), jnp.zeros((4,), tokens_all.dtype))
    (loss, sums), (hidden, logit_all) = lax.scan(step, start, (tokens_all, lengths, labels))
    return (hidden, loss, logit_all, sums)

def reference(hidden_in, cotangent, lengths, labels, qkv_weight, qv_bias, out_weight, out_bias, norm1_gain, norm1_bias, up_weight, up_bias, down_weight, down_bias, norm2_gain, norm2_bias, student_weight, student_bias, pool_query, pooler_weight, pooler_bias, class_weight, class_bias):
    params = tuple((weight.astype(jnp.float32) for weight in (qkv_weight, qv_bias, out_weight, out_bias, norm1_gain, norm1_bias, up_weight, up_bias, down_weight, down_bias, norm2_gain, norm2_bias, student_weight, student_bias, pool_query, pooler_weight, pooler_bias, class_weight, class_bias)))
    tokens_all = hidden_in.astype(jnp.float32)

    def objective(params_in, tokens_in):
        return forward(params_in, tokens_in, lengths, labels)
    outputs, pull = jax.vjp(objective, params, tokens_all)
    hidden, loss, logit_all, sums = outputs
    grads, token_grad = pull((cotangent.astype(jnp.float32), jnp.ones_like(loss), jnp.zeros_like(logit_all), jnp.zeros_like(sums)))
    rms_stats = jnp.sqrt(sums / (jnp.sum(lengths).astype(sums.dtype) * D))
    return (hidden.astype(jnp.bfloat16), logit_all, token_grad.astype(jnp.bfloat16), grads[0], grads[1], grads[2], grads[3], grads[4], grads[5], grads[6], grads[7], grads[8], grads[9], grads[10], grads[11], grads[12], grads[13], grads[14], grads[15], grads[16], grads[17], grads[18], rms_stats)
```

```python
import functools

import jax
import jax.numpy as jnp
import numpy as np
from jax import lax
from jax.experimental import pallas as pl
from jax.experimental.pallas import tpu as pltpu
from jax.sharding import PartitionSpec as P

D = 768
HS = 64
CW = 128
PH = 2
CLASSES = 14
EPSILON = 1e-06
NEGATIVE = -1e30
LOG2E = 1.4426950408889634
HIGHEST = lax.Precision.HIGHEST
BF = jnp.bfloat16
F32 = jnp.float32
AXES = ("dp", "mp")
QB = 256


def dot(a, b, ca, cb):
    return lax.dot_general(a, b, (((ca,), (cb,)), ((), ())), preferred_element_type=F32)


def hop(x, dbit, mbit):
    nd, nm = lax.axis_size("dp"), lax.axis_size("mp")
    pairs = [(d * nm + m, (d ^ dbit) * nm + (m ^ mbit)) for d in range(nd) for m in range(nm)]
    return lax.ppermute(x, AXES, pairs)


def bit_groups(nd):
    bits = []
    b = nd // 2
    while b > 1:
        bits.append(b)
        b //= 2
    groups = [bits[i : i + 2] for i in range(0, len(bits), 2)]
    out = []
    for g in groups:
        out.append([0, g[0]] if len(g) == 1 else [0, g[1], g[0], g[0] + g[1]])
    return out


def gather_chips(x):
    nd = lax.axis_size("dp")
    cur = x[None]
    for masks in bit_groups(nd):
        parts = [cur] + [hop(cur, k, 0) for k in masks[1:]]
        cur = jnp.stack(parts, 1).reshape(-1, *x.shape)
    near, far = (hop(cur, 1, 0), hop(cur, 0, 2))
    far2 = hop(cur, 1, 2)
    return (
        jnp.stack([cur, near], 1).reshape(nd, *x.shape),
        jnp.stack([far, far2], 1).reshape(nd, *x.shape),
    )


def scatter_chips(mine, other):
    nd = lax.axis_size("dp")
    tail = mine.shape[1:]
    a = mine.reshape(nd // 2, 2, *tail)
    b = other.reshape(nd // 2, 2, *tail)
    cur = (
        a[:, 0].astype(F32)
        + hop(a[:, 1], 1, 0).astype(F32)
        + hop(b[:, 0], 0, 2).astype(F32)
        + hop(b[:, 1], 1, 2).astype(F32)
    )
    for masks in reversed(bit_groups(nd)):
        low = cur.astype(BF).reshape(-1, len(masks), *tail)
        full = cur.reshape(-1, len(masks), *tail)
        cur = full[:, 0]
        for i, k in enumerate(masks[1:], 1):
            cur = cur + hop(low[:, i], k, 0).astype(F32)
    return cur[0]


def relative(x, me):
    return jnp.take(x, jnp.arange(x.shape[0], dtype=jnp.int32) ^ me, axis=0)


def split3(x):
    a = x.astype(BF)
    r = x - a.astype(F32)
    b = r.astype(BF)
    return a, b, (r - b.astype(F32)).astype(BF)


def swap64(x):
    return jnp.concatenate([x[:, 64:], x[:, :64]], axis=1)


def doubled(kp, head):
    lane = lax.broadcasted_iota(jnp.int32, kp.shape, 1)
    kr = swap64(kp)
    return jnp.where(lane < 64, kp, kr) if head == 0 else jnp.where(lane < 64, kr, kp)


def attn_fwd_kernel(q_ref, k_ref, v_ref, aux_ref, ctx_ref, lse_ref, o_ref):
    n = q_ref.shape[0]
    qt = jnp.transpose(q_ref[...].astype(F32)) * (HS**-0.5 * LOG2E)
    hi = qt.astype(BF)
    lo = (qt - hi.astype(F32)).astype(BF)
    vt = jnp.transpose(v_ref[...].astype(F32)).astype(BF)
    kp = k_ref[...]
    row = lax.broadcasted_iota(jnp.int32, (128, QB), 0)
    auxq = jnp.where(row == 0, 1.0, 0.0).astype(BF)
    for h in range(2):
        lhs = jnp.concatenate([doubled(kp, h), aux_ref[...]], axis=1)
        r = slice(64 * h, 64 * h + 64)
        vaug = jnp.concatenate([vt[r], jnp.ones((16, n), BF)], axis=0)
        for b in range(n // QB):
            s = slice(b * QB, b * QB + QB)
            rhs = jnp.concatenate([hi[r, s], lo[r, s], auxq], axis=0)
            sc = dot(lhs, rhs, 1, 0)
            m = jnp.max(sc, axis=0, keepdims=True)
            p = jnp.exp2(sc - m).astype(BF)
            o = dot(vaug, p, 1, 0)
            total = o[64:65]
            o_ref[r, s] = o[:64] / total
            lse_ref[0, h : h + 1, s] = m + jnp.log2(total)
    ctx_ref[...] = jnp.transpose(o_ref[...]).astype(BF)


def attn_fwd(proj, aux):
    n, w = proj.shape
    pairs = w // 3 // 128
    return pl.pallas_call(
        attn_fwd_kernel,
        grid=(pairs,),
        in_specs=[
            pl.BlockSpec((n, 128), lambda p: (0, p)),
            pl.BlockSpec((n, 128), lambda p: (0, p + pairs)),
            pl.BlockSpec((n, 128), lambda p: (0, p + 2 * pairs)),
            pl.BlockSpec((n, 128), lambda p: (0, 0)),
        ],
        out_specs=[
            pl.BlockSpec((n, 128), lambda p: (0, p)),
            pl.BlockSpec((1, 2, n), lambda p: (p, 0, 0)),
        ],
        out_shape=[
            jax.ShapeDtypeStruct((n, w // 3), BF),
            jax.ShapeDtypeStruct((pairs, 2, n), F32),
        ],
        scratch_shapes=[pltpu.VMEM((128, n), F32)],
        name="attn_fwd",
    )(proj, proj, proj, aux)


def attn_bwd_kernel(q_ref, k_ref, v_ref, aux_ref, ctx_ref, do_ref, lse_ref, dq_ref, dk_ref, dv_ref, dqt_ref):
    n = q_ref.shape[0]
    scale = HS**-0.5
    qp, kp, vp, dop = q_ref[...], k_ref[...], v_ref[...], do_ref[...]
    qt = jnp.transpose(qp.astype(F32)) * (scale * LOG2E)
    hi = qt.astype(BF)
    lo = (qt - hi.astype(F32)).astype(BF)
    kt = jnp.transpose(kp.astype(F32)).astype(BF)
    dot_f = jnp.transpose(dop.astype(F32))
    dot_b = dot_f.astype(BF)
    ctxt = jnp.transpose(ctx_ref[...].astype(F32))
    prod = dot_f * ctxt
    lane = lax.broadcasted_iota(jnp.int32, (n, 128), 1)
    row = lax.broadcasted_iota(jnp.int32, (128, QB), 0)
    lhs_v = jnp.concatenate([vp, aux_ref[...]], axis=1)
    dk = jnp.zeros((n, 128), F32)
    dv = jnp.zeros((n, 128), F32)
    for h in range(2):
        lhs = jnp.concatenate([doubled(kp, h), aux_ref[...]], axis=1)
        r = slice(64 * h, 64 * h + 64)
        mine = (lane < 64) if h == 0 else (lane >= 64)
        qm = jnp.where(mine, qp, jnp.zeros_like(qp))
        dom = jnp.where(mine, dop, jnp.zeros_like(dop))
        dsum = jnp.sum(prod[r], axis=0, keepdims=True)
        l1, l2, l3 = split3(-lse_ref[0, h : h + 1, :])
        d1, d2, d3 = split3(-dsum)
        for b in range(n // QB):
            s = slice(b * QB, b * QB + QB)

            def pieces(first, x1, x2, x3):
                z = jnp.where(row == 1, x1[:, s].astype(F32), jnp.where(row == 0, first, 0.0))
                z = jnp.where(row == 2, x2[:, s].astype(F32), z)
                return jnp.where(row == 3, x3[:, s].astype(F32), z).astype(BF)

            rhs = jnp.concatenate([hi[r, s], lo[r, s], pieces(1.0, l1, l2, l3)], axis=0)
            p = jnp.exp2(dot(lhs, rhs, 1, 0))
            zero = jnp.zeros((64, QB), BF)
            g = dot_b[r, s]
            half = [g, zero] if h == 0 else [zero, g]
            rhs_v = jnp.concatenate(half + [pieces(0.0, d1, d2, d3)], axis=0)
            ds = (p * dot(lhs_v, rhs_v, 1, 0)).astype(BF)
            dv = dv + dot(p.astype(BF), dom[s], 1, 0)
            dk = dk + dot(ds, qm[s], 1, 0)
            dqt_ref[r, s] = dot(kt[r], ds, 1, 0)
    dq_ref[...] = jnp.transpose(dqt_ref[...] * scale).astype(BF)
    dk_ref[...] = (dk * scale).astype(BF)
    dv_ref[...] = dv.astype(BF)


def attn_bwd(proj, aux, ctx, dctx, lse):
    n, w = proj.shape
    pairs = w // 3 // 128
    one = pl.BlockSpec((n, 128), lambda p: (0, p))
    return pl.pallas_call(
        attn_bwd_kernel,
        grid=(pairs,),
        in_specs=[
            one,
            pl.BlockSpec((n, 128), lambda p: (0, p + pairs)),
            pl.BlockSpec((n, 128), lambda p: (0, p + 2 * pairs)),
            pl.BlockSpec((n, 128), lambda p: (0, 0)),
            one,
            one,
            pl.BlockSpec((1, 2, n), lambda p: (p, 0, 0)),
        ],
        out_specs=[one, one, one],
        out_shape=[jax.ShapeDtypeStruct((n, w // 3), BF)] * 3,
        scratch_shapes=[pltpu.VMEM((128, n), F32)],
        name="attn_bwd",
    )(proj, proj, proj, aux, ctx, dctx, lse)


def norm_forward(values, gain, shift):
    center = values - jnp.mean(values, -1, keepdims=True)
    spread = jnp.mean(center * center, -1, keepdims=True)
    row_scale = lax.rsqrt(spread + EPSILON)
    normed = center * row_scale
    return (normed * gain + shift, normed, row_scale)


def norm_backward(upstream, normed, row_scale, gain):
    scaled = upstream * gain
    inner = (
        scaled
        - jnp.mean(scaled, -1, keepdims=True)
        - normed * jnp.mean(scaled * normed, -1, keepdims=True)
    )
    return (inner * row_scale, jnp.sum(upstream * normed, axis=0), jnp.sum(upstream, axis=0))


def pad_rows(flat, rows):
    size = -flat.shape[-1] % (rows * 128)
    flat = jnp.pad(flat, [(0, 0)] * (flat.ndim - 1) + [(0, size)])
    return flat.reshape(*flat.shape[:-1], -1, 128)


def take_parts(flat, shapes):
    out, at = [], 0
    for shape in shapes:
        size = int(np.prod(shape))
        out.append(flat[:, at : at + size].reshape(flat.shape[0], *shape))
        at += size
    return out


def body(
    hidden_in,
    cotangent,
    lengths,
    labels,
    qkv_weight,
    qv_bias,
    out_weight,
    out_bias,
    norm1_gain,
    norm1_bias,
    up_weight,
    up_bias,
    down_weight,
    down_bias,
    norm2_gain,
    norm2_bias,
    student_weight,
    student_bias,
    pool_query,
    pooler_weight,
    pooler_bias,
    class_weight,
    class_bias,
):
    nd = lax.axis_size("dp")
    me = lax.axis_index("dp")
    m = lax.axis_index("mp")
    c, y = m % 2, m // 2
    total, pd, _ = hidden_in.shape
    assert total == 2 * nd and lax.axis_size("mp") == 4
    hp = pd // 2
    half = nd * hp
    rows = D // nd
    hw = qkv_weight.shape[2]
    fw = up_weight.shape[1]
    seq = 2 * me + y
    length = lengths[seq]
    label = labels[seq]

    def deal(x):
        x = x.reshape(nd, 2, 2, hp, D)
        x = lax.dynamic_slice(x, (0, y, c, 0, 0), (nd, 1, 1, hp, D)).reshape(nd, hp, D)
        return lax.all_to_all(x, "dp", 0, 0, tiled=True).reshape(half, D)

    tokens = deal(hidden_in)

    q_near, q_far = gather_chips(jnp.transpose(qkv_weight, (1, 0, 2)).reshape(rows, 3 * hw))
    local_small = jnp.concatenate(
        [
            student_weight.reshape(-1),
            pooler_weight.reshape(-1),
            class_weight.reshape(-1),
            out_bias,
            norm1_gain,
            norm1_bias,
            down_bias,
            norm2_gain,
            norm2_bias,
            student_bias,
            pool_query,
            pooler_bias,
            qv_bias.reshape(-1),
            up_bias.reshape(-1),
        ]
    )
    small = pad_rows(local_small, 8)
    small = lax.all_to_all(jnp.broadcast_to(small[None], (nd, *small.shape)), "dp", 0, 0, tiled=True)
    small = small.reshape(nd, -1)
    nh = qv_bias.shape[0]
    nr = up_bias.shape[0]
    cr = CW // nd
    parts = take_parts(
        small,
        [(rows, CW), (cr, CW), (cr, CLASSES), (6, rows), (3, cr), (nh, 2 * HS // nd), (nr, HS // nd)],
    )
    student_full = parts[0].reshape(D, CW)
    pooler_full = parts[1].reshape(CW, CW).astype(F32)
    class_full = parts[2].reshape(CW, CLASSES).astype(F32)
    wide = jnp.transpose(parts[3], (1, 0, 2)).reshape(6, D).astype(F32)
    narrow = jnp.transpose(parts[4], (1, 0, 2)).reshape(3, CW).astype(F32)
    qv_mine = jnp.transpose(parts[5], (1, 0, 2)).reshape(nh, 2 * HS)
    ub_mine = jnp.transpose(parts[6], (1, 0, 2)).reshape(nr * HS)
    bias_mine = jnp.concatenate([qv_mine.reshape(-1), ub_mine])
    bias_far = hop(bias_mine, 0, 2)
    bias_two = jnp.stack([bias_mine, bias_far])
    bias_sib = hop(bias_two, 0, 1)
    qv_two = bias_two[:, : nh * 2 * HS].reshape(2, nh, 2 * HS).astype(F32)
    up_bias_full = jnp.concatenate([bias_two, bias_sib])[:, nh * 2 * HS :].reshape(-1).astype(F32)
    out_bias_f, gain_one, shift_one, down_bias_f, gain_two, shift_two = [wide[i : i + 1] for i in range(6)]

    f_pack = jnp.concatenate([out_weight.T, up_weight, down_weight.T], axis=1)
    f_near, f_far = gather_chips(f_pack)
    f_two = jnp.stack([relative(f_near, me), relative(f_far, me)])
    f_sib = hop(f_two, 0, 1)
    f_all = jnp.concatenate([f_two, f_sib]).reshape(4, D, hw + 2 * fw)
    out_t = jnp.concatenate([f_all[i, :, :hw] for i in range(4)], axis=1)
    up_full = jnp.concatenate([f_all[i, :, hw : hw + fw] for i in range(4)], axis=1)
    down_t = jnp.concatenate([f_all[i, :, hw + fw :] for i in range(4)], axis=1)
    cot = deal(cotangent)

    q_all = jnp.stack([relative(q_near, me), relative(q_far, me)]).reshape(2, D, 3, hw)
    w_qkv = jnp.transpose(q_all, (1, 2, 0, 3)).reshape(D, 6 * hw)
    zero = jnp.zeros((2, nh * HS), F32)
    proj_bias = jnp.stack([qv_two[:, :, :HS].reshape(2, -1), zero, qv_two[:, :, HS:].reshape(2, -1)]).reshape(1, 6 * hw)

    both = jnp.concatenate([tokens, hop(tokens, 0, 1)], axis=0)
    proj = (dot(both, w_qkv, 1, 0) + proj_bias).astype(BF)
    index = jnp.arange(half, dtype=jnp.int32)
    position = (index // hp) * pd + index % hp
    position = jnp.concatenate([position + c * hp, position + (1 - c) * hp])
    live = position < length
    col = jnp.arange(128, dtype=jnp.int32)[None, :]
    aux = jnp.where(
        col == 0, jnp.where(live, 0.0, NEGATIVE)[:, None], jnp.where(col <= 3, 1.0, 0.0)
    ).astype(BF)
    ctx, lse = attn_fwd(proj, aux)
    ctx_all = jnp.concatenate([ctx[:half], hop(ctx[half:], 0, 1)], axis=1)

    live_own = live[:half]
    live_float = live_own.astype(F32)[:, None]
    token_float = tokens.astype(F32)
    attention = dot(ctx_all, out_t, 1, 1) + out_bias_f
    first, normed_one, scale_one = norm_forward(token_float + attention, gain_one, shift_one)
    first_low = first.astype(BF)
    before = dot(first_low, up_full, 1, 0) + up_bias_full
    phi_c = 0.5 * (1.0 + lax.erf(before * (0.5**0.5)))
    slope = (phi_c + before * (jnp.exp(-0.5 * before * before) * (2 * np.pi) ** -0.5)).astype(BF)
    active = (before * phi_c).astype(BF)
    feed = dot(active, down_t, 1, 1) + down_bias_f
    second, normed_two, scale_two = norm_forward(first + feed, gain_two, shift_two)
    second_low = second.astype(BF)

    def undeal(x):
        a = lax.all_to_all(x.reshape(nd, hp, D), "dp", 0, 0, tiled=True)
        b = hop(a, 0, 2)
        pair = jnp.where(y == 0, jnp.stack([a, b], 1), jnp.stack([b, a], 1))
        sib = hop(pair, 0, 1)
        quad = jnp.where(c == 0, jnp.stack([pair, sib], 2), jnp.stack([sib, pair], 2))
        return quad.reshape(total, pd, D)

    hidden_out = undeal(second_low)

    student_bias_f, query_f, pooler_bias_f = narrow[0:1], narrow[1:2], narrow[2:3]
    student = dot(second_low, student_full, 1, 0) + student_bias_f
    pw = CW // PH
    heads = student.reshape(half, PH, pw)
    scale = pw**-0.5
    pool_logit = jnp.sum(heads * query_f.reshape(1, PH, pw), -1) * scale
    pool_logit = jnp.where(live_own[:, None], pool_logit, NEGATIVE)
    top = jnp.max(pool_logit, 0)
    weight = jnp.where(live_own[:, None], jnp.exp(pool_logit - top), 0.0)
    amount = jnp.sum(weight, 0)
    mass = jnp.sum(weight[:, :, None] * heads, 0).reshape(CW)
    sums = jnp.stack(
        [jnp.sum(live_float * v * v) for v in (token_float, attention, first, feed)]
    )
    mine = jnp.concatenate([top, amount, sums, mass])
    mine = jnp.pad(mine, (0, 256 - mine.shape[0])).reshape(2, 128)
    sib = hop(mine, 0, 1).reshape(-1)
    top2, amount2, sums2, mass2 = sib[0:2], sib[2:4], sib[4:8], sib[8 : 8 + CW]
    best = jnp.maximum(top, top2)
    fa, fb = jnp.exp(top - best), jnp.exp(top2 - best)
    whole = amount * fa + amount2 * fb
    pooled = (mass * jnp.repeat(fa, pw) + mass2 * jnp.repeat(fb, pw)) / jnp.repeat(whole, pw)
    pool_weight = weight * (fa / whole)
    pooled = pooled[None, :]
    z = jnp.tanh(jnp.dot(pooled, pooler_full, precision=HIGHEST) + pooler_bias_f)
    logit = jnp.dot(z, class_full, precision=HIGHEST) + class_bias.astype(F32)[None, :]
    onehot = (jnp.arange(CLASSES) == label).astype(F32)[None, :]
    dlogit = jax.nn.softmax(logit, axis=-1) - onehot
    once = jnp.where(c == 0, 1.0, 0.0)
    grad_class = jnp.dot(z.T, dlogit, precision=HIGHEST) * once
    dz = jnp.dot(dlogit, class_full.T, precision=HIGHEST)
    dzp = dz * (1.0 - z * z)
    grad_pooler = jnp.dot(pooled.T, dzp, precision=HIGHEST) * once
    grad_pooler_bias = dzp[0] * once
    dpooled = jnp.dot(dzp, pooler_full.T, precision=HIGHEST)
    dpooled_h = dpooled.reshape(1, PH, pw)
    dw = jnp.sum(heads * dpooled_h, -1)
    dq_pool = scale * pool_weight * (dw - jnp.sum((pooled * dpooled).reshape(PH, pw), -1)[None, :])
    grad_query = jnp.sum(dq_pool[:, :, None] * heads, 0).reshape(CW)
    dstudent = pool_weight[:, :, None] * dpooled_h + dq_pool[:, :, None] * query_f.reshape(1, PH, pw)
    dstudent = dstudent.reshape(half, CW).astype(BF)
    grad_student_bias = jnp.sum(dstudent.astype(F32), 0)
    grad_student = dot(second_low, dstudent, 0, 0)

    dsecond = dot(dstudent, student_full, 1, 1) + cot.astype(F32)
    dr2, grad_gain_two, grad_shift_two = norm_backward(dsecond, normed_two, scale_two, gain_two)
    grad_down_bias = jnp.sum(dr2, 0)
    dffn = dr2.astype(BF)
    grad_down_t = dot(dffn, active, 0, 0).astype(BF)
    dact = dot(dffn, down_t, 1, 0)
    dpre = (dact * slope.astype(F32)).astype(BF)
    grad_up_bias = jnp.sum(dpre.astype(F32), 0)
    grad_up = dot(first_low, dpre, 0, 0).astype(BF)
    dfirst = dot(dpre, up_full, 1, 1) + dr2
    dr1, grad_gain_one, grad_shift_one = norm_backward(dfirst, normed_one, scale_one, gain_one)
    grad_out_bias = jnp.sum(dr1, 0)
    dattn = dr1.astype(BF)
    grad_out_t = dot(dattn, ctx_all, 0, 0).astype(BF)
    dctx = dot(dattn, out_t, 1, 0).astype(BF)
    w2 = 2 * hw
    dctx_own = jnp.concatenate([dctx[:, :w2], hop(dctx[:, w2:], 0, 1)], axis=0)

    def quarter(i):
        return jnp.concatenate(
            [
                grad_out_t[:, i * hw : (i + 1) * hw],
                grad_up[:, i * fw : (i + 1) * fw],
                grad_down_t[:, i * fw : (i + 1) * fw],
            ],
            axis=1,
        )

    keep = [quarter(0), quarter(1)]
    got = hop(jnp.stack([quarter(2), quarter(3)]), 0, 1)
    f_grads = [
        relative((k.astype(F32) + got[i].astype(F32)).astype(BF).reshape(nd, rows, -1), me)
        for i, k in enumerate(keep)
    ]
    f_sum = scatter_chips(*f_grads)

    dq, dk, dv = attn_bwd(proj, aux, ctx, dctx_own, lse)
    dproj = jnp.concatenate([dq, dk, dv], axis=1)
    grad_qv = jnp.stack([jnp.sum(dq.astype(F32), 0), jnp.sum(dv.astype(F32), 0)])
    part = dot(dproj, w_qkv, 1, 1)
    dtokens = part[:half] + dr1 + hop(part[half:].astype(BF), 0, 1).astype(F32)
    input_grad = undeal(dtokens.astype(BF))
    grad_qkv = dot(both, dproj, 0, 0).astype(BF).reshape(nd, rows, 3, 2, hw)
    grad_qkv = relative(grad_qkv, me)
    q_sum = scatter_chips(
        grad_qkv[:, :, :, 0].reshape(nd, rows, 3 * hw), grad_qkv[:, :, :, 1].reshape(nd, rows, 3 * hw)
    )

    eye = (jnp.arange(4)[:, None] == jnp.stack([m, m ^ 2])[None, :]).astype(F32)
    qv_pair = jnp.transpose(grad_qv.reshape(2, 2, nh, HS), (1, 2, 0, 3)).reshape(2, nh * 2 * HS)
    grad_qv_full = jnp.dot(eye, qv_pair, precision=HIGHEST).reshape(4 * nh, nd, 2 * HS // nd)
    eye4 = (jnp.arange(4)[:, None] == jnp.stack([m, m ^ 2, m ^ 1, m ^ 3])[None, :]).astype(F32)
    grad_ub_full = jnp.dot(eye4, grad_up_bias.reshape(4, fw), precision=HIGHEST).reshape(4 * nr, nd, HS // nd)
    wide_g = jnp.stack([grad_out_bias, grad_gain_one, grad_shift_one, grad_down_bias, grad_gain_two, grad_shift_two])
    narrow_g = jnp.stack([grad_student_bias, grad_query, grad_pooler_bias])
    small_g = jnp.concatenate(
        [
            grad_student.reshape(nd, -1),
            grad_pooler.reshape(nd, -1),
            grad_class.reshape(nd, -1),
            jnp.transpose(wide_g.reshape(6, nd, rows), (1, 0, 2)).reshape(nd, -1),
            jnp.transpose(narrow_g.reshape(3, nd, cr), (1, 0, 2)).reshape(nd, -1),
            jnp.transpose(grad_qv_full, (1, 0, 2)).reshape(nd, -1),
            jnp.transpose(grad_ub_full, (1, 0, 2)).reshape(nd, -1),
        ],
        axis=1,
    )
    small_g = pad_rows(small_g, 8)
    small_g = small_g + hop(small_g.astype(BF), 0, 1).astype(F32)
    small_g = small_g + hop(small_g.astype(BF), 0, 2).astype(F32)
    small_g = lax.all_to_all(small_g.astype(BF), "dp", 0, 0, tiled=True).astype(F32).sum(0)
    g_student, g_pooler, g_class, g_wide, g_narrow, g_qv, g_ub = [
        a[0]
        for a in take_parts(
            small_g.reshape(1, -1),
            [
                (rows, CW),
                (cr, CW),
                (cr, CLASSES),
                (6, rows),
                (3, cr),
                (4, nh, 2 * HS // nd),
                (4, nr, HS // nd),
            ],
        )
    ]
    report = jnp.concatenate([logit[0], dlogit[0], sums + sums2])
    report = jnp.pad(report, (0, 128 - report.shape[0])).reshape(1, 128)
    far = hop(report, 0, 2)
    two = jnp.where(y == 0, jnp.concatenate([report, far]), jnp.concatenate([far, report]))
    two = jnp.pad(two, ((0, 6), (0, 0)))
    table = lax.all_to_all(jnp.broadcast_to(two[None], (nd, 8, 128)), "dp", 0, 0, tiled=True)
    table = table[:, :2].reshape(total, 128)
    logit_all = table[:, :CLASSES]
    class_bias_grad = jnp.sum(table[:, CLASSES : 2 * CLASSES], 0)
    squares = jnp.sum(table[:, 2 * CLASSES : 2 * CLASSES + 4], 0)
    rms = jnp.sqrt(squares / (jnp.sum(lengths).astype(F32) * D))
    return (
        hidden_out,
        logit_all,
        input_grad,
        jnp.transpose(q_sum.reshape(rows, 3, hw), (1, 0, 2)),
        g_qv[m],
        f_sum[:, :hw].T,
        g_wide[0],
        g_wide[1],
        g_wide[2],
        f_sum[:, hw : hw + fw],
        g_ub[m],
        f_sum[:, hw + fw :].T,
        g_wide[3],
        g_wide[4],
        g_wide[5],
        g_student,
        g_narrow[0],
        g_narrow[1],
        g_pooler,
        g_narrow[2],
        g_class,
        class_bias_grad,
        rms,
    )


def solution(mesh):
    rows = P(None, "dp", None)
    vec = P("dp")
    return jax.shard_map(
        body,
        mesh=mesh,
        in_specs=(
            rows,
            rows,
            P(),
            P(),
            P(None, "dp", "mp"),
            P("mp", "dp"),
            P("mp", "dp"),
            vec,
            vec,
            vec,
            P("dp", "mp"),
            P("mp", "dp"),
            P("mp", "dp"),
            vec,
            vec,
            vec,
            P("dp", None),
            vec,
            vec,
            P("dp", None),
            vec,
            P("dp", None),
            P(),
        ),
        out_specs=(
            rows,
            P(),
            rows,
            P(None, "dp", "mp"),
            P("mp", "dp"),
            P("mp", "dp"),
            vec,
            vec,
            vec,
            P("dp", "mp"),
            P("mp", "dp"),
            P("mp", "dp"),
            vec,
            vec,
            vec,
            P("dp", None),
            vec,
            vec,
            P("dp", None),
            vec,
            P("dp", None),
            P(),
            P(),
        ),
        check_vma=False,
    )
```

```python
import functools

import jax
import jax.numpy as jnp
import numpy as np
from jax import lax
from jax.experimental import pallas as pl
from jax.experimental.pallas import tpu as pltpu
from jax.sharding import PartitionSpec as P

D = 768
HS = 64
CW = 128
PH = 2
CLASSES = 14
EPSILON = 1e-06
NEGATIVE = -1e30
LOG2E = 1.4426950408889634
HIGHEST = lax.Precision.HIGHEST
BF = jnp.bfloat16
F32 = jnp.float32
AXES = ("dp", "mp")
QB = 256
RB = 128
SLOW = 1
ROOM = 16


def dot(a, b, ca, cb):
    return lax.dot_general(a, b, (((ca,), (cb,)), ((), ())), preferred_element_type=F32)


def hop(x, dbit, mbit):
    nd, nm = lax.axis_size("dp"), lax.axis_size("mp")
    pairs = [(d * nm + m, (d ^ dbit) * nm + (m ^ mbit)) for d in range(nd) for m in range(nm)]
    return lax.ppermute(x, AXES, pairs)


def after(x, *others):
    return lax.optimization_barrier((x, *others))[0]


def bit_groups(nd):
    bits = []
    b = nd // 2
    while b > 1:
        bits.append(b)
        b //= 2
    groups = [bits[i : i + 2] for i in range(0, len(bits), 2)]
    out = []
    for g in groups:
        out.append([0, g[0]] if len(g) == 1 else [0, g[1], g[0], g[0] + g[1]])
    return out


def gather_chips(x):
    nd = lax.axis_size("dp")
    cur = x[None]
    for masks in bit_groups(nd):
        parts = [cur] + [hop(cur, k, 0) for k in masks[1:]]
        cur = jnp.stack(parts, 1).reshape(-1, *x.shape)
    near, far = (hop(cur, 1, 0), hop(cur, 0, 2))
    far2 = hop(cur, 1, 2)
    return (
        jnp.stack([cur, near], 1).reshape(nd, *x.shape),
        jnp.stack([far, far2], 1).reshape(nd, *x.shape),
    )


def scatter_chips(mine, other):
    nd = lax.axis_size("dp")
    tail = mine.shape[1:]
    a = mine.reshape(nd // 2, 2, *tail)
    b = other.reshape(nd // 2, 2, *tail)
    cur = (
        a[:, 0].astype(F32)
        + hop(a[:, 1], 1, 0).astype(F32)
        + hop(b[:, 0], 0, 2).astype(F32)
        + hop(b[:, 1], 1, 2).astype(F32)
    )
    for masks in reversed(bit_groups(nd)):
        low = cur.astype(BF).reshape(-1, len(masks), *tail)
        full = cur.reshape(-1, len(masks), *tail)
        cur = full[:, 0]
        for i, k in enumerate(masks[1:], 1):
            cur = cur + hop(low[:, i], k, 0).astype(F32)
    return cur[0]


def relative(x, me):
    return jnp.take(x, jnp.arange(x.shape[0], dtype=jnp.int32) ^ me, axis=0)


def split3(x):
    a = x.astype(BF)
    r = x - a.astype(F32)
    b = r.astype(BF)
    return a, b, (r - b.astype(F32)).astype(BF)


def swap64(x):
    return jnp.concatenate([x[:, 64:], x[:, :64]], axis=1)


def doubled(kp, head):
    lane = lax.broadcasted_iota(jnp.int32, kp.shape, 1)
    kr = swap64(kp)
    return jnp.where(lane < 64, kp, kr) if head == 0 else jnp.where(lane < 64, kr, kp)


ANY = pl.BlockSpec(memory_space=pl.ANY)
SMEM = pl.BlockSpec(memory_space=pltpu.SMEM)


def room(mib):
    return pltpu.CompilerParams(vmem_limit_bytes=mib << 20)


def call(kernel, outs, args, specs=None, scratch=(), name=None, flops=0, mib=ROOM):
    specs = [pl.BlockSpec(memory_space=pltpu.VMEM) if s is None else s for s in (specs or [None] * len(args))]
    size = sum(a.size * a.dtype.itemsize for a in args) + sum(
        int(np.prod(o.shape)) * np.dtype(o.dtype).itemsize for o in outs
    )
    return pl.pallas_call(
        kernel,
        in_specs=specs,
        out_specs=[pl.BlockSpec(memory_space=pltpu.VMEM)] * len(outs),
        out_shape=outs,
        scratch_shapes=list(scratch),
        cost_estimate=cost(size, flops),
        compiler_params=room(mib),
        name=name,
    )(*args)


def cost(size, flops=0):
    return pl.CostEstimate(flops=int(flops) // SLOW, bytes_accessed=int(size) // SLOW, transcendentals=0)


def sds(shape, dtype=F32):
    return jax.ShapeDtypeStruct(shape, dtype)


def by_rows(kernel, outs, sums, args, consts, info=None, name=None):
    n = args[0].shape[0]

    def cut(a):
        return pl.BlockSpec((RB, a.shape[1]), lambda i: (i, 0))

    def whole(a):
        return pl.BlockSpec(a.shape, lambda i: (0,) * len(a.shape))

    head = [] if info is None else [info]
    size = sum(a.size * a.dtype.itemsize for a in [*args, *consts])
    return pl.pallas_call(
        kernel,
        grid=(n // RB,),
        in_specs=[SMEM] * len(head) + [cut(a) for a in args] + [whole(a) for a in consts],
        out_specs=[cut(o) for o in outs] + [whole(o) for o in sums],
        out_shape=[*outs, *sums],
        cost_estimate=cost(size),
        compiler_params=room(ROOM),
        name=name,
    )(*head, *args, *consts)


def start_sums(*refs):
    @pl.when(pl.program_id(0) == 0)
    def _():
        for r in refs:
            r[...] = jnp.zeros(r.shape, F32)


def start(copies):
    for cp in copies:
        cp.start()
    return copies


def load_pair(info, arrays, w_ref, sems):
    if len(arrays) == 1:
        return start([pltpu.make_async_copy(arrays[0].at[0], w_ref, sems.at[0])])
    nz = arrays[0].shape[1]
    rows = D // (2 * nz)
    copies = []
    for x, a in enumerate(arrays):
        for z in range(nz):
            at = pl.multiple_of((info[0] ^ (2 * z + x)) * rows, 16)
            copies.append(
                pltpu.make_async_copy(a.at[0, z, pl.ds(0, rows), :], w_ref.at[pl.ds(at, rows), :], sems.at[len(copies)])
            )
    return start(copies)


def load_rows(info, arrays, b_ref, sems):
    nz = arrays[0].shape[1]
    rows = D // (2 * nz)
    copies = []
    for x, a in enumerate(arrays):
        for z in range(nz):
            copies.append(
                pltpu.make_async_copy(
                    a.at[0, z, pl.ds(rows, 8), :], b_ref.at[info[0] ^ (2 * z + x)], sems.at[len(copies)]
                )
            )
    return start(copies)


def load_weight(info, arrays, w_ref, sems):
    if len(arrays) == 2:
        return start([pltpu.make_async_copy(a.at[0], w_ref.at[i], sems.at[i]) for i, a in enumerate(arrays)])
    nz = arrays[0].shape[1]
    rows = D // (2 * nz)
    copies = []
    for i, a in enumerate(arrays):
        for z in range(nz):
            at = pl.multiple_of((info[0] ^ (2 * z + i % 2)) * rows, 16)
            copies.append(
                pltpu.make_async_copy(
                    a.at[0, z, pl.ds(0, rows), :], w_ref.at[i // 2, pl.ds(at, rows), :], sems.at[len(copies)]
                )
            )
    return start(copies)


def wait(copies):
    for cp in copies:
        cp.wait()


def weight_scratch(arrays):
    count = len(arrays) if len(arrays) == 2 else 4 * arrays[0].shape[1]
    return [pltpu.VMEM((2, D, arrays[0].shape[-1]), BF), pltpu.SemaphoreType.DMA((count,))]


def gather_lines(local):
    k, rows, n = local.shape
    cur = local[:, None]
    for masks in bit_groups(lax.axis_size("dp")):
        parts = [cur] + [hop(cur, b, 0) for b in masks[1:]]
        cur = jnp.stack(parts, 2).reshape(k, -1, rows, n)
    return cur, parts[1:]


def gather_planes(cur, fast):
    near, far, far2 = hop(cur, 1, 0), hop(cur, 0, 2), hop(cur, 1, 2)
    if fast:
        return cur, near, far, far2
    me = lax.axis_index("dp")
    k, half, rows, n = cur.shape

    def ordered(a, b):
        both = jnp.stack([a, b], 2).reshape(k, 2 * half, rows, n)
        return jnp.moveaxis(relative(jnp.moveaxis(both, 1, 0), me), 0, 1).reshape(k, 2 * half * rows, n)

    return ordered(cur, near), ordered(far, far2)


def spread(info, g_ref, k, outs):
    nz = outs[0].shape[1]
    rows = D // (2 * nz)
    for z in range(nz):
        for x in range(2):
            at = pl.multiple_of((info[0] ^ (2 * z + x)) * rows, 8)
            outs[x][k, z, :rows] = g_ref[pl.ds(at, rows), :].astype(BF)


def grad_outs(k, ys, nd, rows, fast, more=0):
    return [sds((k, nd // 2, rows + more, D), BF)] * (2 * ys) if fast else [sds((k, D, D), BF)] * ys


def store_grad(info, k, y, g, g_ref, outs):
    if len(outs[0].shape) == 4:
        g_ref[...] = g
        spread(info, g_ref, k, outs[2 * y : 2 * y + 2])
    else:
        outs[y][k] = g.astype(BF)


def sum_first_kernel(count, *refs):
    parts, (keep_ref, *send_refs) = refs[:count], refs[count:]
    for k in range(parts[0].shape[0]):
        for z in range(parts[0].shape[1]):
            total = parts[0][k, z].astype(F32)
            for r in parts[1:]:
                total = total + r[k, z].astype(F32)
            if z == 0:
                keep_ref[k] = total
            else:
                send_refs[z - 1][k] = total.astype(BF)


def sum_planes(parts):
    if len(parts) == 2:
        return list(parts)
    keep, x, y, xy = parts
    return [keep, hop(x, 1, 0), hop(y, 0, 2), hop(xy, 1, 2)]


def sum_lines(parts):
    nd = lax.axis_size("dp")
    if len(parts) == 2:
        me = lax.axis_index("dp")
        k = parts[0].shape[0]
        near, far = (
            relative(jnp.moveaxis(p.reshape(k, nd, D // nd, D), 0, 1), me) for p in parts
        )
        return scatter_chips(near, far)
    return finish_lines(sum_blocks(parts))


def sum_blocks(parts):
    if len(parts) == 2:
        return parts
    k, nz, rows, n = parts[0].shape
    return call(
        functools.partial(sum_first_kernel, len(parts)),
        [sds((k, rows, n))] + [sds((k, rows, n), BF)] * (nz - 1),
        list(parts),
        name="grad_sum",
    )


def finish_lines(sums):
    own, *send = sums
    for z, piece in enumerate(send, 1):
        own = own + hop(piece, 2 * z, 0).astype(F32)
    return own


def bias_rows(b, first, count, low, high):
    return jnp.concatenate([b[first + i : first + i + 1, low:high] for i in range(count)], axis=1)


def block(ref, i):
    return ref[:, 128 * i : 128 * i + 128]


def attn_fwd_kernel(nh, info, own_ref, sib_ref, bias_ref, aux_ref, *rest):
    *arrays, proj_ref, w_ref, ctx_ref, lse_ref, w_sems, o_ref, b_ref, b_sems = rest
    copies = load_pair(info, arrays, w_ref, w_sems)
    hw = nh * HS
    if len(arrays) == 2:
        wait(load_rows(info, arrays, b_ref, b_sems))
        nd = b_ref.shape[0]
        w = 2 * HS // nd

        def bias_part(first):
            return [b_ref[a, 0:1, h * w : h * w + w] for h in range(nh) for a in range(first, first + nd // 2)]

        q_part, v_part = (
            jnp.concatenate(bias_part(a), axis=1).astype(F32) for a in (0, nd // 2)
        )
    else:
        bias = bias_ref[...].astype(F32)
        q_part = bias_rows(bias, 0, nh, 0, HS)
        v_part = bias_rows(bias, 0, nh, HS, 2 * HS)
    row_bias = jnp.concatenate([q_part, jnp.zeros((1, hw), F32), v_part, jnp.zeros((1, HS), F32)], axis=1)
    wait(copies)
    half = own_ref.shape[0]
    n = 2 * half
    for i, ref in enumerate((own_ref, sib_ref)):
        for j in range(2):
            r = slice(j * half // 2, (j + 1) * half // 2)
            out = dot(ref[r], w_ref[:, : 10 * HS], 1, 0) + row_bias
            proj_ref[i * half + r.start : i * half + r.stop] = out.astype(BF)
    qt = [jnp.transpose(block(proj_ref, i).astype(F32)) * (HS**-0.5 * LOG2E) for i in (0, 1)]
    hi = [q.astype(BF) for q in qt]
    lo = [(q - h.astype(F32)).astype(BF) for q, h in zip(qt, hi)]
    vt = [jnp.transpose(block(proj_ref, i).astype(F32)).astype(BF) for i in (3, 4)]
    row = lax.broadcasted_iota(jnp.int32, (128, QB), 0)
    auxq = jnp.where(row == 0, 1.0, 0.0).astype(BF)
    o_ref[0:HS] = jnp.zeros((HS, n), F32)
    lse_ref[...] = jnp.zeros(lse_ref.shape, F32)
    for h in range(nh):
        kb, kh = ((1, 1), (2, 0), (2, 1))[h]
        lhs = jnp.concatenate([doubled(block(proj_ref, kb), kh), aux_ref[...]], axis=1)
        i, r = h // 2, slice(64 * (h % 2), 64 * (h % 2) + 64)
        vaug = jnp.concatenate([vt[i][r], jnp.ones((16, n), BF)], axis=0)
        to = slice(64 * h + 64, 64 * h + 128)
        for b in range(n // QB):
            s = slice(b * QB, b * QB + QB)
            rhs = jnp.concatenate([hi[i][r, s], lo[i][r, s], auxq], axis=0)
            sc = dot(lhs, rhs, 1, 0)
            m = jnp.max(sc, axis=0, keepdims=True)
            p = jnp.exp2(sc - m).astype(BF)
            o = dot(vaug, p, 1, 0)
            total = o[64:65]
            o_ref[to, s] = o[:64] / total
            lse_ref[h : h + 1, s] = m + jnp.log2(total)
    for j in range(2):
        ctx_ref[:, 128 * j : 128 * j + 128] = jnp.transpose(o_ref[128 * j : 128 * j + 128]).astype(BF)


def attn_fwd(nh, info, own, sib, bias, aux, arrays):
    n = 2 * own.shape[0]
    count = len(arrays) * arrays[0].shape[1] if len(arrays) == 2 else 1
    return call(
        functools.partial(attn_fwd_kernel, nh),
        [sds((n, 10 * HS), BF), sds((D, D), BF), sds((n, 4 * HS), BF), sds((8, n))],
        [info, own, sib, bias, aux, *arrays],
        [SMEM] + [None] * 4 + [ANY] * len(arrays),
        [
            pltpu.SemaphoreType.DMA((count,)),
            pltpu.VMEM((4 * HS, n), F32),
            pltpu.VMEM((count, 8, D), BF),
            pltpu.SemaphoreType.DMA((count,)),
        ],
        "attn_fwd",
        flops=11_000_000_000,
    )


def out_kernel(first, c0_ref, c1_ref, w0_ref, w1_ref, out_ref):
    rows, cols = slice(first, first + out_ref.shape[0]), slice(8 * HS, 12 * HS)
    part = dot(c0_ref[rows], w0_ref[:, cols], 1, 1) + dot(c1_ref[rows], w1_ref[:, cols], 1, 1)
    out_ref[...] = part.astype(out_ref.dtype)


def norm(values, gain, shift):
    center = values - jnp.mean(values, -1, keepdims=True)
    spread_ = jnp.mean(center * center, -1, keepdims=True)
    scale = lax.rsqrt(spread_ + EPSILON)
    normed = center * scale
    return normed * gain + shift, normed, scale


def live_rows(aux_ref):
    return jnp.where(aux_ref[:, 0:1].astype(F32) > -1.0, 1.0, 0.0)


def square(live, v):
    return jnp.sum(jnp.sum(v * v, -1, keepdims=True) * live, axis=0, keepdims=True)


def ln1_kernel(part_ref, got_ref, tok_ref, aux_ref, wide_ref, first_ref, low_ref, n_ref, s_ref, sq_ref):
    start_sums(sq_ref)
    tok = tok_ref[...].astype(F32)
    att = part_ref[...] + got_ref[...].astype(F32) + wide_ref[0:1]
    first, normed, scale = norm(tok + att, wide_ref[1:2], wide_ref[2:3])
    first_ref[...] = first
    low_ref[...] = first.astype(BF)
    n_ref[...] = normed
    s_ref[...] = scale
    live = live_rows(aux_ref)
    lane = lax.broadcasted_iota(jnp.int32, (1, 128), 1)
    out = jnp.zeros((1, 128), F32)
    for i, v in enumerate((tok, att, first)):
        out = jnp.where(lane == i, square(live, v), out)
    sq_ref[...] += out


def hidden_bias(b_ref, nr):
    nd = b_ref.shape[0]
    w = HS // nd
    first = jnp.concatenate([b_ref[a, 0:1, :128] for a in range(nd)], axis=0)
    i = lax.broadcasted_iota(jnp.int32, (128, nr * HS), 0)
    f = lax.broadcasted_iota(jnp.int32, (128, nr * HS), 1)
    place = jnp.where(i == (f // HS) * w + f % w, 1.0, 0.0).astype(BF)
    spread_ = dot(first, place, 1, 0)
    a = lax.broadcasted_iota(jnp.int32, (nd, nr * HS), 0)
    f = lax.broadcasted_iota(jnp.int32, (nd, nr * HS), 1)
    return jnp.sum(jnp.where((f % HS) // w == a, spread_, 0.0), axis=0, keepdims=True)


def ffn_up_kernel(nh, nr, info, x_ref, b0_ref, b1_ref, *rest):
    *up, act_ref, slope_ref, up_ref, sems, r0_ref, r1_ref, r_sems = rest
    copies = load_weight(info, up, up_ref, sems)
    fw = nr * HS
    x = x_ref[...]
    if len(up) == 4:
        for i, r_ref in enumerate((r0_ref, r1_ref)):
            wait(load_rows(info, up[2 * i : 2 * i + 2], r_ref, r_sems))
        biases = [hidden_bias(r_ref, nr) for r_ref in (r0_ref, r1_ref)]
    else:
        biases = [bias_rows(b_ref[...].astype(F32), nh, nr, 0, HS) for b_ref in (b0_ref, b1_ref)]
    wait(copies)
    for y in range(2):
        for j in range(fw // 256):
            s = slice(j * 256, (j + 1) * 256)
            t = slice(y * fw + j * 256, y * fw + (j + 1) * 256)
            pre = dot(x, up_ref[y, :, s], 1, 0) + biases[y][:, s]
            phi = 0.5 + 0.5 * lax.erf(pre * (0.5**0.5))
            act_ref[:, t] = (pre * phi).astype(BF)
            slope_ref[:, t] = (phi + pre * (jnp.exp(-0.5 * pre * pre) * (2 * np.pi) ** -0.5)).astype(BF)


def product_kernel(info, a_ref, *rest):
    *w, out_ref, w_ref, sems = rest
    wait(load_weight(info, w, w_ref, sems))
    fw = w_ref.shape[2]
    out_ref[...] = (dot(a_ref[:, :fw], w_ref[0], 1, 1) + dot(a_ref[:, fw:], w_ref[1], 1, 1)).astype(out_ref.dtype)


def head_ones():
    a = lax.broadcasted_iota(jnp.int32, (CW, CW), 0) // (CW // PH)
    b = lax.broadcasted_iota(jnp.int32, (CW, CW), 1) // (CW // PH)
    return jnp.where(a == b, 1.0, 0.0)


def fdot(a, b, ca=1, cb=0):
    return lax.dot_general(a, b, (((ca,), (cb,)), ((), ())), precision=HIGHEST, preferred_element_type=F32)


def ln2_kernel(
    part_ref, got_ref, first_ref, aux_ref, wide_ref, narrow_ref, sw_ref, low_ref, n_ref, s_ref, st_ref, lg_ref, stat_ref
):
    feed = part_ref[...] + got_ref[...].astype(F32) + wide_ref[3:4]
    second, normed, scale = norm(first_ref[...] + feed, wide_ref[4:5], wide_ref[5:6])
    low = second.astype(BF)
    low_ref[...] = low
    n_ref[...] = normed
    s_ref[...] = scale
    student = dot(low, sw_ref[...], 1, 0) + narrow_ref[0:1]
    st_ref[...] = student
    live = live_rows(aux_ref)
    logit = fdot(student * narrow_ref[1:2], head_ones()) * (CW // PH) ** -0.5
    logit = jnp.where(live > 0.0, logit, NEGATIVE)
    lg_ref[...] = logit

    @pl.when(pl.program_id(0) == 0)
    def _():
        stat_ref[...] = jnp.zeros((8, 128), F32)
        stat_ref[0:1] = jnp.full((1, 128), NEGATIVE, F32)

    old = stat_ref[0:1]
    top = jnp.maximum(old, jnp.max(logit, axis=0, keepdims=True))
    shrink = jnp.exp(old - top)
    weight = jnp.where(live > 0.0, jnp.exp(logit - top), 0.0)
    stat_ref[0:1] = top
    stat_ref[1:2] = stat_ref[1:2] * shrink + jnp.sum(weight, axis=0, keepdims=True)
    stat_ref[2:3] = stat_ref[2:3] * shrink + jnp.sum(weight * student, axis=0, keepdims=True)
    stat_ref[3:4] += jnp.broadcast_to(square(live, feed), (1, 128))


def norm_back(up, normed, scale, gain):
    scaled = up * gain
    inner = scaled - jnp.mean(scaled, -1, keepdims=True) - normed * jnp.mean(scaled * normed, -1, keepdims=True)
    return inner * scale


def colsum(x):
    return jnp.sum(x, axis=0, keepdims=True)


def head_kernel(
    info,
    st_ref,
    lg_ref,
    low_ref,
    cot_ref,
    n_ref,
    s_ref,
    stat_ref,
    sib_ref,
    sq_ref,
    pooler_ref,
    class_ref,
    cb_ref,
    narrow_ref,
    sw_ref,
    wide_ref,
    dr2_ref,
    dffn_ref,
    gst_ref,
    gpool_ref,
    gclass_ref,
    rep_ref,
    vec_ref,
    nvec_ref,
    keep_ref,
):
    scale = (CW // PH) ** -0.5
    once = jnp.where(info[1] == 0, 1.0, 0.0)

    @pl.when(pl.program_id(0) == 0)
    def _():
        top, top2 = stat_ref[0:1], sib_ref[0:1]
        best = jnp.maximum(top, top2)
        fa, fb = jnp.exp(top - best), jnp.exp(top2 - best)
        whole = stat_ref[1:2] * fa + sib_ref[1:2] * fb
        pooled = (stat_ref[2:3] * fa + sib_ref[2:3] * fb) / whole
        pooled = jnp.broadcast_to(pooled, (8, CW))
        z = jnp.tanh(fdot(pooled, pooler_ref[...]) + narrow_ref[2:3])
        lane = lax.broadcasted_iota(jnp.int32, (8, 128), 1)
        row = lax.broadcasted_iota(jnp.int32, (8, 128), 0)
        logit = fdot(z, class_ref[...]) + cb_ref[...]
        masked = jnp.where(lane < CLASSES, logit, NEGATIVE)
        e = jnp.exp(masked - jnp.max(masked, axis=1, keepdims=True))
        dlogit = e / jnp.sum(e, axis=1, keepdims=True) - jnp.where(lane == info[3], 1.0, 0.0)
        only = jnp.where(row == 0, once, 0.0)
        gclass_ref[...] = fdot(z * only, dlogit, 0, 0)
        dz = fdot(dlogit, class_ref[...], 1, 1)
        dzp = dz * (1.0 - z * z)
        gpool_ref[...] = fdot(pooled * only, dzp, 0, 0)
        dpooled = fdot(dzp, pooler_ref[...], 1, 1)
        sq = jnp.where(lane[0:1] == 3, stat_ref[3:4] + sib_ref[3:4] * 0.0, sq_ref[...])
        sq = jnp.where(info[1] == 0, pltpu.roll(sq, 2 * CLASSES, 1), pltpu.roll(sq, 2 * CLASSES + 4, 1))
        rep = jnp.where(lane < CLASSES, logit, pltpu.roll(jnp.where(lane < CLASSES, dlogit, 0.0), CLASSES, 1)) * once
        rep_ref[...] = jnp.where(lane < 2 * CLASSES, rep, sq)
        nvec_ref[...] = jnp.zeros((8, CW), F32)
        nvec_ref[2:3] = dzp[0:1] * once
        vec_ref[...] = jnp.zeros((8, D), F32)
        gst_ref[...] = jnp.zeros((D, CW), F32)
        keep_ref[0:1] = best
        keep_ref[1:2] = whole
        keep_ref[2:3] = dpooled[0:1]
        keep_ref[3:4] = fdot(pooled * dpooled, head_ones())[0:1]

    student = st_ref[...]
    dp = keep_ref[2:3]
    logit = lg_ref[...]
    weight = jnp.where(logit > 0.5 * NEGATIVE, jnp.exp(logit - keep_ref[0:1]), 0.0) / keep_ref[1:2]
    dq = scale * weight * (fdot(student * dp, head_ones()) - keep_ref[3:4])
    dstudent = (weight * dp + dq * narrow_ref[1:2]).astype(BF)
    nvec_ref[0:1] += colsum(dstudent.astype(F32))
    nvec_ref[1:2] += colsum(dq * student)
    gst_ref[...] += dot(low_ref[...], dstudent, 0, 0)
    dsecond = dot(dstudent, sw_ref[...], 1, 1) + cot_ref[...].astype(F32)
    normed = n_ref[...]
    dr2 = norm_back(dsecond, normed, s_ref[...], wide_ref[4:5])
    dr2_ref[...] = dr2
    dffn_ref[...] = dr2.astype(BF)
    vec_ref[0:1] += colsum(dr2)
    vec_ref[1:2] += colsum(dsecond * normed)
    vec_ref[2:3] += colsum(dsecond)


def ffn_back_kernel(info, g_ref, slope_ref, *rest):
    *down, dpre_ref, ub_ref, w_ref, sems = rest
    copies = load_weight(info, down, w_ref, sems)
    fw = w_ref.shape[2]
    g = g_ref[...]
    ub_ref[...] = jnp.zeros(ub_ref.shape, F32)
    wait(copies)
    for y in range(2):
        for j in range(fw // 256):
            s = slice(j * 256, (j + 1) * 256)
            t = slice(y * fw + j * 256, y * fw + (j + 1) * 256)
            dpre = (dot(g, w_ref[y, :, s], 1, 0) * slope_ref[:, t].astype(F32)).astype(BF)
            dpre_ref[:, t] = dpre
            ub_ref[0:1, t] = colsum(dpre.astype(F32))


def ffn_grad_kernel(info, first, first2, dpre, dpre2, dffn, dffn2, act, act2, *rest):
    *outs, g_ref = rest
    fw = dpre.shape[1] // 2
    for k, (a0, a1, b0, b1) in enumerate(((first, first2, dpre, dpre2), (dffn, dffn2, act, act2))):
        for y in range(2):
            s = slice(y * fw, (y + 1) * fw)
            g = dot(a0[...], b0[:, s], 0, 0) + dot(a1[...], b1[:, s], 0, 0)
            store_grad(info, k, y, g, g_ref, outs)


def ln1_back_kernel(part_ref, got_ref, dr2_ref, n_ref, s_ref, wide_ref, dr1_ref, low_ref, vec_ref):
    start_sums(vec_ref)
    up = part_ref[...] + got_ref[...].astype(F32) + dr2_ref[...]
    normed = n_ref[...]
    dr1 = norm_back(up, normed, s_ref[...], wide_ref[1:2])
    dr1_ref[...] = dr1
    low_ref[...] = dr1.astype(BF)
    vec_ref[0:1] += colsum(dr1)
    vec_ref[1:2] += colsum(up * normed)
    vec_ref[2:3] += colsum(up)


def attn_bwd_kernel(nh, proj_ref, w_ref, aux_ref, ctx_ref, da_ref, db_ref, lse_ref, out_ref, sum_ref, do_ref, dqt_ref):
    n = proj_ref.shape[0]
    half = n // 2
    scale = HS**-0.5
    cols = slice(8 * HS, 12 * HS)
    for i, ref in enumerate((da_ref, db_ref)):
        do_ref[i * half : (i + 1) * half] = dot(ref[...], w_ref[:, cols], 1, 0).astype(BF)
    qb = [block(proj_ref, i) for i in (0, 1)]
    qt = [jnp.transpose(q.astype(F32)) * (scale * LOG2E) for q in qb]
    hi = [q.astype(BF) for q in qt]
    lo = [(q - h.astype(F32)).astype(BF) for q, h in zip(qt, hi)]
    kt = [jnp.transpose(block(proj_ref, i).astype(F32)).astype(BF) for i in (1, 2)]
    dob = [block(do_ref, i) for i in (0, 1)]
    dot_f = [jnp.transpose(d.astype(F32)) for d in dob]
    dot_b = [d.astype(BF) for d in dot_f]
    prod = [d * jnp.transpose(block(ctx_ref, i).astype(F32)) for i, d in enumerate(dot_f)]
    lane = lax.broadcasted_iota(jnp.int32, (n, 128), 1)
    row = lax.broadcasted_iota(jnp.int32, (128, QB), 0)
    zero = jnp.zeros((64, QB), BF)
    empty = jnp.zeros((n, 128), BF)
    dqt_ref[...] = jnp.zeros(dqt_ref.shape, F32)
    dk, dv = [], []
    for h in range(nh):
        kb, kh = ((1, 1), (2, 0), (2, 1))[h]
        i, ih = h // 2, h % 2
        vi, vh = ((3, 0), (3, 1), (4, 0))[h]
        oi, oh = ((0, 1), (1, 0), (1, 1))[h]
        lhs = jnp.concatenate([doubled(block(proj_ref, kb), kh), aux_ref[...]], axis=1)
        lhs_v = jnp.concatenate([block(proj_ref, vi), aux_ref[...]], axis=1)
        r = slice(64 * ih, 64 * ih + 64)
        ro = slice(64 * oh, 64 * oh + 64)
        rk = slice(64 * kh, 64 * kh + 64)
        qm = jnp.where((lane < 64) == (ih == 0), qb[i], empty)
        dom = jnp.where((lane < 64) == (oh == 0), dob[oi], empty)
        dsum = jnp.sum(prod[oi][ro], axis=0, keepdims=True)
        l1, l2, l3 = split3(-lse_ref[h : h + 1, :])
        d1, d2, d3 = split3(-dsum)
        dkh = jnp.zeros((n, 128), F32)
        dvh = jnp.zeros((n, 128), F32)
        for b in range(n // QB):
            s = slice(b * QB, b * QB + QB)

            def pieces(first, x1, x2, x3):
                z = jnp.where(row == 1, x1[:, s].astype(F32), jnp.where(row == 0, first, 0.0))
                z = jnp.where(row == 2, x2[:, s].astype(F32), z)
                return jnp.where(row == 3, x3[:, s].astype(F32), z).astype(BF)

            rhs = jnp.concatenate([hi[i][r, s], lo[i][r, s], pieces(1.0, l1, l2, l3)], axis=0)
            p = jnp.exp2(dot(lhs, rhs, 1, 0))
            g = dot_b[oi][ro, s]
            part = [g, zero] if vh == 0 else [zero, g]
            rhs_v = jnp.concatenate(part + [pieces(0.0, d1, d2, d3)], axis=0)
            ds = (p * dot(lhs_v, rhs_v, 1, 0)).astype(BF)
            dvh = dvh + dot(p.astype(BF), dom[s], 1, 0)
            dkh = dkh + dot(ds, qm[s], 1, 0)
            dqt_ref[64 * h : 64 * h + 64, s] = dot(kt[kb - 1][rk], ds, 1, 0)
        dk.append(dkh * scale)
        dv.append(dvh)

    def put(i, x):
        out_ref[:, 128 * i : 128 * i + 128] = x.astype(BF)
        sum_ref[:, 128 * i : 128 * i + 128] = jnp.broadcast_to(colsum(x.astype(BF).astype(F32)), (8, 128))

    left = lane < 64
    put(0, jnp.transpose(dqt_ref[0:128] * scale))
    put(1, jnp.where(left, jnp.transpose(dqt_ref[128:256] * scale), swap64(dk[0])))
    put(2, jnp.where(left, swap64(dk[1]), swap64(dk[2])))
    put(3, jnp.where(left, swap64(dv[0]), swap64(dv[1])))
    put(4, jnp.where(left, swap64(dv[2]), 0.0))


def attn_bwd(nh, proj, w, aux, ctx, da, db, lse):
    n = proj.shape[0]
    return call(
        functools.partial(attn_bwd_kernel, nh),
        [sds((n, 10 * HS), BF), sds((8, 10 * HS))],
        [proj, w, aux, ctx, da, db, lse],
        None,
        [pltpu.VMEM((n, 4 * HS), BF), pltpu.VMEM((4 * HS, n), F32)],
        "attn_bwd",
        flops=11_000_000_000,
    )


def token_grad_kernel(g0_ref, g1_ref, w0_ref, w1_ref, dr1_ref, send_ref, own_ref):
    n = g0_ref.shape[0]
    half = n // 2
    cols = slice(0, 10 * HS)
    for out_ref, s in ((send_ref, slice(half, n)), (own_ref, slice(0, half))):
        part = dot(g0_ref[s], w0_ref[:, cols], 1, 1) + dot(g1_ref[s], w1_ref[:, cols], 1, 1)
        if out_ref is own_ref:
            part = part + dr1_ref[...]
        out_ref[...] = part.astype(out_ref.dtype)


def qkv_grad_kernel(nh, info, x0, x1, g_in, da, db, ctx_ref, sum_ref, *rest):
    *outs, g_ref, t_ref = rest
    half = x0.shape[0]
    g = dot(x0[...], g_in[:half], 0, 0) + dot(x1[...], g_in[half:], 0, 0)
    o = dot(da[...], ctx_ref[:half], 0, 0) + dot(db[...], ctx_ref[half:], 0, 0)
    g = jnp.concatenate([g[:, : 8 * HS], g[:, 8 * HS :] + o[:, : 2 * HS], o[:, 2 * HS :]], axis=1)
    store_grad(info, 0, 0, g, g_ref, outs)
    if len(outs) == 2:
        nz = outs[0].shape[1]
        rows = D // (2 * nz)
        piece = HS // nz
        zero = jnp.zeros((1, 128 - nh * piece), F32)
        for a in range(2 * nz):
            base = (a % nz) * piece + (a // nz) * 2 * nh * HS
            cuts = [sum_ref[0:1, base + h * HS : base + h * HS + piece] for h in range(nh)]
            t_ref[a : a + 1] = jnp.concatenate([*cuts, zero], axis=1)
        for z in range(nz):
            for x in range(2):
                outs[x][0, z, rows:] = jnp.zeros((outs[x].shape[2] - rows, D), BF)
                row = t_ref[pl.ds(info[0] ^ (2 * z + x), 1), :]
                outs[x][0, z, rows : rows + 8, :128] = jnp.broadcast_to(row, (8, 128)).astype(BF)


def place_kernel(info, a_ref, b_ref, c_ref, d_ref, out_ref):
    c, y = info[1], info[2]
    out_ref[0, y, c] = a_ref[0]
    out_ref[0, 1 - y, c] = b_ref[0]
    out_ref[0, y, 1 - c] = c_ref[0]
    out_ref[0, 1 - y, 1 - c] = d_ref[0]


def lanes(x):
    x = x.reshape(1, -1) if x.ndim == 1 else x
    return jnp.pad(x, ((0, 0), (0, 128 - x.shape[1])))


def unpack_kernel(sizes, in_ref, sw_ref, pooler_ref, class_ref, wide_ref, narrow_ref, bias_ref):
    rows, cr, nh, nr = sizes
    nd = in_ref.shape[0]
    blocks = [in_ref[d].astype(F32) for d in range(nd)]
    at = rows + 2 * cr

    def joined(first, count, width):
        return jnp.concatenate([b[first : first + count, :width] for b in blocks], axis=1)

    sw_ref[...] = jnp.concatenate([b[:rows] for b in blocks], axis=0).astype(BF)
    pooler_ref[...] = jnp.concatenate([b[rows : rows + cr] for b in blocks], axis=0)
    class_ref[...] = jnp.concatenate([b[rows + cr : at] for b in blocks], axis=0)
    wide_ref[...] = jnp.zeros(wide_ref.shape, F32)
    wide_ref[0:6] = joined(at, 6, rows)
    narrow_ref[...] = jnp.zeros(narrow_ref.shape, F32)
    narrow_ref[0:3] = joined(at + 6, 3, cr)
    bias_ref[...] = jnp.zeros(bias_ref.shape, F32)
    bias_ref[0:nh, :] = joined(at + 9, nh, 2 * HS // nd)
    bias_ref[nh : nh + nr, :HS] = joined(at + 9 + nh, nr, HS // nd)


def pack_grads_kernel(sizes, info, gst, gpool, gclass, v1, v2, nv, ub0, ub1, rep, out_ref):
    rows, cr, nh, nr = sizes
    nd = out_ref.shape[0]
    fw = nr * HS
    me = info[2] * 2 + info[1]
    ub = ub0[0:1] + ub1[0:1]
    pair = [
        jnp.concatenate([ub[:, y * fw + r * HS : y * fw + (r + 1) * HS] for r in range(nr)], axis=0) for y in range(2)
    ]
    quads = jnp.concatenate(
        [jnp.where(me == q, pair[0], jnp.where((me ^ 2) == q, pair[1], 0.0)) for q in range(4)], axis=0
    )
    wide = jnp.concatenate([v1[0:1], v1[1:2], v1[2:3], v2[0:1], v2[1:2], v2[2:3]], axis=0)

    def wider(x):
        return jnp.concatenate([x, jnp.zeros((x.shape[0], 128 - x.shape[1]), F32)], axis=1)

    total = 2 * nd
    row = lax.broadcasted_iota(jnp.int32, (total, 128), 0)
    high = rep[0:1].astype(BF).astype(F32)
    mine = row == 2 * info[0] + info[2]
    table = [jnp.where(mine, high, 0.0), jnp.where(mine, rep[0:1] - high, 0.0)]
    hs = HS // nd
    for d in range(nd):
        parts = [
            gst[d * rows : (d + 1) * rows],
            gpool[d * cr : (d + 1) * cr],
            gclass[d * cr : (d + 1) * cr],
            wider(wide[:, d * rows : (d + 1) * rows]),
            wider(nv[0:3, d * cr : (d + 1) * cr]),
            wider(quads[:, d * hs : (d + 1) * hs]),
            *table,
        ]
        parts = jnp.concatenate(parts, axis=0)
        out_ref[d, : parts.shape[0]] = parts
        if parts.shape[0] < out_ref.shape[1]:
            out_ref[d, parts.shape[0] :] = jnp.zeros((out_ref.shape[1] - parts.shape[0], 128), F32)


def body(
    hidden_in,
    cotangent,
    lengths,
    labels,
    qkv_weight,
    qv_bias,
    out_weight,
    out_bias,
    norm1_gain,
    norm1_bias,
    up_weight,
    up_bias,
    down_weight,
    down_bias,
    norm2_gain,
    norm2_bias,
    student_weight,
    student_bias,
    pool_query,
    pooler_weight,
    pooler_bias,
    class_weight,
    class_bias,
):
    nd = lax.axis_size("dp")
    me = lax.axis_index("dp")
    m = lax.axis_index("mp")
    c, y = m % 2, m // 2
    total, pd, _ = hidden_in.shape
    assert total == 2 * nd and lax.axis_size("mp") == 4
    hp = pd // 2
    half = nd * hp
    rows, cr = D // nd, CW // nd
    nh, nr = qv_bias.shape[0], up_bias.shape[0]
    hw, fw = nh * HS, nr * HS
    fast = rows % 16 == 0 and len(bit_groups(nd)) == 1
    sizes = (rows, cr, nh, nr)
    seq = 2 * me + y
    length = lengths[seq]
    info = jnp.stack([me, c, y, labels[seq]]).astype(jnp.int32)

    def deal(x):
        x = x.reshape(nd, 2, 2, hp, D)
        x = lax.dynamic_slice(x, (0, y, c, 0, 0), (nd, 1, 1, hp, D)).reshape(nd, hp, D)
        return lax.all_to_all(x, "dp", 0, 0, tiled=True).reshape(half, D)

    def undeal(x):
        return lax.all_to_all(x.reshape(nd, hp, D), "dp", 0, 0, tiled=True)

    def place(a, b):
        one = pl.BlockSpec((1, hp, D), lambda d: (d, 0, 0))
        out = pl.pallas_call(
            place_kernel,
            grid=(nd,),
            in_specs=[SMEM] + [one] * 4,
            out_specs=pl.BlockSpec((1, 2, 2, hp, D), lambda d: (d, 0, 0, 0, 0)),
            out_shape=sds((nd, 2, 2, hp, D), BF),
            cost_estimate=cost(6_000_000),
            compiler_params=room(8),
            name="place",
        )(info, a, b, hop(a, 0, 1), hop(b, 0, 1))
        return out.reshape(total, pd, D)

    qo = jnp.concatenate([jnp.transpose(qkv_weight, (1, 0, 2)).reshape(rows, 3 * hw), out_weight.T], axis=1)
    if fast:
        row = jnp.pad(qv_bias.reshape(1, -1), ((0, 7), (0, D - qv_bias.size)))
        qo = jnp.concatenate([qo, row], axis=0)
    qo_line, _ = gather_lines(qo[None])
    tokens = deal(after(hidden_in, qo_line))
    w_qo = gather_planes(qo_line, fast)
    w_qo = (w_qo[:2], w_qo[2:]) if fast else (w_qo[:1], w_qo[1:])
    up_pack = up_weight
    if fast:
        row = jnp.pad(up_bias.reshape(1, -1), ((0, 7), (0, D - up_bias.size)))
        up_pack = jnp.concatenate([up_weight, row], axis=0)
    up_line, up_got = gather_lines(after(up_pack, qo_line)[None])
    w_up = gather_planes(up_line, fast)
    down_line, down_got = gather_lines(after(down_weight.T, up_line)[None])
    small = jnp.concatenate(
        [student_weight, pooler_weight]
        + [
            lanes(v)
            for v in (
                class_weight,
                out_bias,
                norm1_gain,
                norm1_bias,
                down_bias,
                norm2_gain,
                norm2_bias,
                student_bias,
                pool_query,
                pooler_bias,
                qv_bias,
                up_bias,
            )
        ],
        axis=0,
    )
    small = jnp.pad(small, ((0, -small.shape[0] % 16), (0, 0)))
    class_b = lanes(class_bias.astype(F32))
    cot = deal(cotangent)

    index = jnp.arange(half, dtype=jnp.int32)
    position = (index // hp) * pd + index % hp
    position = jnp.concatenate([position + c * hp, position + (1 - c) * hp])
    col = jnp.arange(128, dtype=jnp.int32)[None, :]
    aux = jnp.where(
        col == 0, jnp.where(position < length, 0.0, NEGATIVE)[:, None], jnp.where(col <= 3, 1.0, 0.0)
    ).astype(BF)
    aux_own = aux[:half]

    sib = hop(after(tokens, w_qo, up_got), 0, 1)
    n = 2 * half
    biases = [aux, aux]
    if not fast:
        piece = jnp.broadcast_to(qv_bias[None], (nd, *qv_bias.shape))
        piece = lax.all_to_all(piece, "dp", 0, 0, tiled=True)
        piece = jnp.transpose(piece, (1, 0, 2)).reshape(nh, 2 * HS)
        piece = jnp.pad(piece, ((0, 16 - nh), (0, 0)))
        biases = [piece, hop(piece, 0, 2)]
    proj0, w0, ctx0, lse0 = attn_fwd(nh, info, tokens, sib, biases[0], aux, w_qo[0])
    small = lax.all_to_all(jnp.broadcast_to(after(small, ctx0)[None], (nd, *small.shape)), "dp", 0, 0, tiled=True)
    student_w, pooler_f, class_f, wide, narrow, bias_near = call(
        functools.partial(unpack_kernel, sizes),
        [sds((D, CW), BF), sds((CW, CW)), sds((CW, CW)), sds((8, D)), sds((8, CW)), sds((16, 128))],
        [small],
        name="unpack",
    )
    bias_near = bias_near.astype(BF)
    bias_far = bias_near if fast else hop(bias_near, 0, 2)
    proj1, w1, ctx1, lse1 = attn_fwd(nh, info, tokens, sib, biases[1], after(aux, down_got, ctx0), w_qo[1])
    w_down = gather_planes(after(down_line, ctx0), fast)

    if fast:
        ctx1 = after(ctx1, w_up, w_down[1:3], student_w)

    def out(first, kind):
        return call(
            functools.partial(out_kernel, first), [sds((half, D), kind)], [ctx0, ctx1, w0, w1], name="out"
        )[0]

    att_got = hop(out(half, BF), 0, 1)
    att_part = out(0, F32)
    first, first_low, n1, s1, sq1 = by_rows(
        ln1_kernel,
        [sds((half, D)), sds((half, D), BF), sds((half, D)), sds((half, 1))],
        [sds((1, 128))],
        [att_part, att_got, tokens, aux_own],
        [wide],
        name="ln1",
    )
    first_sib = hop(first_low, 0, 1)

    def ffn_up(x):
        return call(
            functools.partial(ffn_up_kernel, nh, nr),
            [sds((half, 2 * fw), BF), sds((half, 2 * fw), BF)],
            [info, x, bias_near, bias_far, *w_up],
            [SMEM] + [None] * 3 + [ANY] * len(w_up),
            weight_scratch(w_up)
            + [pltpu.VMEM((max(nd, 8), 8, D), BF)] * 2
            + [pltpu.SemaphoreType.DMA((nd,))],
            "ffn_up",
        )

    def product(a, w, kind):
        return call(
            product_kernel,
            [sds((half, D), kind)],
            [info, a, *w],
            [SMEM, None] + [ANY] * len(w),
            weight_scratch(w),
            "product",
        )[0]

    act, slope = ffn_up(first_low)
    act_sib, slope_sib = ffn_up(after(first_sib, act))
    ffn_got = hop(product(act_sib, w_down, BF), 0, 1)
    ffn_part = product(act, w_down, F32)
    second_low, n2, s2, student, pool_logit, stat = by_rows(
        ln2_kernel,
        [sds((half, D), BF), sds((half, D)), sds((half, 1)), sds((half, CW)), sds((half, CW))],
        [sds((8, 128))],
        [ffn_part, ffn_got, after(first, cot), aux_own],
        [wide, narrow, student_w],
        name="ln2",
    )
    hidden_a = undeal(second_low)
    hidden_b = hop(hidden_a, 0, 2)

    dr2, dffn, g_st, g_pool, g_class, report, vec2, nvec, _ = by_rows(
        head_kernel,
        [sds((half, D)), sds((half, D), BF)],
        [
            sds((D, CW)),
            sds((CW, CW)),
            sds((CW, CW)),
            sds((8, 128)),
            sds((8, D)),
            sds((8, CW)),
            sds((8, 128)),
        ],
        [student, pool_logit, second_low, cot, n2, s2],
        [stat, hop(stat, 0, 1), sq1, pooler_f, class_f, class_b, narrow, student_w, wide],
        info,
        "head",
    )
    dffn_sib = hop(dffn, 0, 1)

    def ffn_back(g, s):
        return call(
            ffn_back_kernel,
            [sds((half, 2 * fw), BF), sds((8, 2 * fw))],
            [info, g, s, *w_down],
            [SMEM, None, None] + [ANY] * len(w_down),
            weight_scratch(w_down),
            "ffn_back",
        )

    dpre, ub0 = ffn_back(dffn, slope)
    dpre_sib, ub1 = ffn_back(after(dffn_sib, dpre, hidden_a), slope_sib)
    dfirst_got = hop(product(dpre_sib, w_up, BF), 0, 1)
    dfirst_part = product(dpre, w_up, F32)
    f_grads = call(
        ffn_grad_kernel,
        grad_outs(2, 2, nd, rows, fast),
        [info, first_low, first_sib, dpre, dpre_sib, dffn, dffn_sib, act, act_sib],
        [SMEM] + [None] * 8,
        [pltpu.VMEM((D, D), F32)],
        "ffn_grad",
    )
    dr1, dattn, vec1 = by_rows(
        ln1_back_kernel,
        [sds((half, D)), sds((half, D), BF)],
        [sds((8, D))],
        [dfirst_part, dfirst_got, after(dr2, hidden_b), n1, s1],
        [wide],
        name="ln1_back",
    )
    dattn_sib = hop(dattn, 0, 1)
    dattn_sib = after(dattn_sib, f_grads, hidden_b)
    f_parts = sum_planes(f_grads)
    count = rows + 2 * cr + 9 + 4 * nr + 2 * total
    (small_g,) = call(
        functools.partial(pack_grads_kernel, sizes),
        [sds((nd, count + -count % 16, 128))],
        [info, g_st, g_pool, g_class, vec1, vec2, nvec, ub0, ub1, report],
        [SMEM] + [None] * 9,
        name="pack",
    )
    small_g = small_g + hop(small_g.astype(BF), 0, 1).astype(F32)
    small_y = small_g + hop(small_g.astype(BF), 0, 2).astype(F32)


    def qkv_grad(g, ctx, sums):
        return call(
            functools.partial(qkv_grad_kernel, nh),
            grad_outs(1, 1, nd, rows, fast, 8),
            [info, tokens, sib, g, dattn, dattn_sib, ctx, sums],
            [SMEM] + [None] * 7,
            [pltpu.VMEM((D, D), F32), pltpu.VMEM((max(8, nd), 128), F32)],
            "qkv_grad",
        )

    g1, g1_sum = attn_bwd(nh, proj1, w1, aux, ctx1, dattn, after(dattn_sib, small_y), lse1)
    far_grad = qkv_grad(g1, ctx1, g1_sum)
    if fast:
        far_got = hop(far_grad[1], 1, 0)
    g0, g0_sum = attn_bwd(
        nh, proj0, w0, aux, ctx0, dattn, after(dattn_sib, g1, far_grad), lse0
    )
    if fast:
        g0, f_parts[1], f_parts[2], far_got = lax.optimization_barrier((g0, f_parts[1], f_parts[2], far_got))
        far_part = (far_grad[0].astype(F32) + far_got.astype(F32)).astype(BF)
    tok_send, tok_own = call(
        token_grad_kernel, [sds((half, D), BF), sds((half, D))], [g0, g1, w0, w1, dr1], name="token_grad"
    )
    near_grad = qkv_grad(g0, ctx0, g0_sum)
    tok_sum = after((tok_own + hop(tok_send, 0, 1).astype(F32)).astype(BF), near_grad)
    input_a = undeal(tok_sum)
    f_sums = sum_blocks(f_parts)
    small_g = lax.all_to_all(after(small_y.astype(BF), input_a), "dp", 0, 0, tiled=True).astype(F32).sum(0)
    hidden_out = place(after(hidden_a, f_sums), hidden_b)
    input_grad = place(input_a, hop(after(input_a, hidden_out), 0, 2))
    f_sum = finish_lines(f_sums) if fast else sum_lines(f_parts)
    up_sum, down_sum = f_sum
    if fast:
        qo_own = (near_grad[0], hop(near_grad[1], 1, 0), hop(far_part, 0, 2))
        qo_own = (after(qo_own[0], f_sum), *qo_own[1:])
        qo_sum = finish_lines(sum_blocks(qo_own))[0]
    else:
        qo_sum = sum_lines([*near_grad, *far_grad])[0]

    width = 2 * HS // nd
    if fast:
        g_qv = qo_sum[rows, : nh * width].reshape(nh, width)
        qo_sum = qo_sum[:rows]
    else:
        g_qv = [
            jnp.concatenate([g[0, :hw].reshape(nh, HS), g[0, 2 * hw : 3 * hw].reshape(nh, HS)], axis=1)
            for g in (g0_sum, g1_sum)
        ]
        g_qv = g_qv[0] + hop(g_qv[1], 0, 2)
        bit = 1
        while bit < nd:
            g_qv = g_qv + hop(g_qv, bit, 0)
            bit *= 2
        g_qv = lax.dynamic_slice(g_qv, (0, width * me), (nh, width))

    at = rows + 2 * cr + 9 + 4 * nr
    table = small_g[at : at + total] + small_g[at + total : at + 2 * total]
    logit_all = table[:, :CLASSES]
    class_bias_grad = jnp.sum(table[:, CLASSES : 2 * CLASSES], 0)
    squares = jnp.sum(table[:, 2 * CLASSES : 2 * CLASSES + 8], 0).reshape(2, 4).sum(0)
    rms = jnp.sqrt(squares / (jnp.sum(lengths).astype(F32) * D))

    at = rows + 2 * cr
    g_wide = small_g[at : at + 6, :rows]
    g_narrow = small_g[at + 6 : at + 9, :cr]
    g_ub = lax.dynamic_slice(small_g, (at + 9 + nr * m, 0), (nr, HS // nd))
    return (
        hidden_out,
        logit_all,
        input_grad,
        jnp.transpose(qo_sum[:, : 3 * hw].reshape(rows, 3, hw), (1, 0, 2)),
        g_qv,
        qo_sum[:, 3 * hw :].T,
        g_wide[0],
        g_wide[1],
        g_wide[2],
        up_sum,
        g_ub,
        down_sum.T,
        g_wide[3],
        g_wide[4],
        g_wide[5],
        small_g[:rows],
        g_narrow[0],
        g_narrow[1],
        small_g[rows : rows + cr],
        g_narrow[2],
        small_g[rows + cr : at, :CLASSES],
        class_bias_grad,
        rms,
    )


def solution(mesh):
    rows = P(None, "dp", None)
    vec = P("dp")
    return jax.shard_map(
        body,
        mesh=mesh,
        in_specs=(
            rows,
            rows,
            P(),
            P(),
            P(None, "dp", "mp"),
            P("mp", "dp"),
            P("mp", "dp"),
            vec,
            vec,
            vec,
            P("dp", "mp"),
            P("mp", "dp"),
            P("mp", "dp"),
            vec,
            vec,
            vec,
            P("dp", None),
            vec,
            vec,
            P("dp", None),
            vec,
            P("dp", None),
            P(),
        ),
        out_specs=(
            rows,
            P(),
            rows,
            P(None, "dp", "mp"),
            P("mp", "dp"),
            P("mp", "dp"),
            vec,
            vec,
            vec,
            P("dp", "mp"),
            P("mp", "dp"),
            P("mp", "dp"),
            vec,
            vec,
            vec,
            P("dp", None),
            vec,
            vec,
            P("dp", None),
            vec,
            P("dp", None),
            P(),
            P(),
        ),
        check_vma=False,
    )
```

```python
import functools

import jax
import jax.numpy as jnp
import numpy as np
from jax import lax
from jax.experimental import pallas as pl
from jax.experimental.pallas import tpu as pltpu
from jax.sharding import PartitionSpec as P

D = 768
HS = 64
CW = 128
PH = 2
CLASSES = 14
EPSILON = 1e-06
NEGATIVE = -1e30
LOG2E = 1.4426950408889634
HIGHEST = lax.Precision.HIGHEST
BF = jnp.bfloat16
F32 = jnp.float32
AXES = ("dp", "mp")
QB = 256
RB = 128
SLOW = 1
ROOM = 16


def dot(a, b, ca, cb):
    return lax.dot_general(a, b, (((ca,), (cb,)), ((), ())), preferred_element_type=F32)


def hop(x, dbit, mbit):
    nd, nm = lax.axis_size("dp"), lax.axis_size("mp")
    pairs = [(d * nm + m, (d ^ dbit) * nm + (m ^ mbit)) for d in range(nd) for m in range(nm)]
    return lax.ppermute(x, AXES, pairs)


def after(x, *others):
    return lax.optimization_barrier((x, *others))[0]


def bit_groups(nd):
    bits = []
    b = nd // 2
    while b > 1:
        bits.append(b)
        b //= 2
    groups = [bits[i : i + 2] for i in range(0, len(bits), 2)]
    out = []
    for g in groups:
        out.append([0, g[0]] if len(g) == 1 else [0, g[1], g[0], g[0] + g[1]])
    return out


def gather_chips(x):
    nd = lax.axis_size("dp")
    cur = x[None]
    for masks in bit_groups(nd):
        parts = [cur] + [hop(cur, k, 0) for k in masks[1:]]
        cur = jnp.stack(parts, 1).reshape(-1, *x.shape)
    near, far = (hop(cur, 1, 0), hop(cur, 0, 2))
    far2 = hop(cur, 1, 2)
    return (
        jnp.stack([cur, near], 1).reshape(nd, *x.shape),
        jnp.stack([far, far2], 1).reshape(nd, *x.shape),
    )


def scatter_chips(mine, other):
    nd = lax.axis_size("dp")
    tail = mine.shape[1:]
    a = mine.reshape(nd // 2, 2, *tail)
    b = other.reshape(nd // 2, 2, *tail)
    cur = (
        a[:, 0].astype(F32)
        + hop(a[:, 1], 1, 0).astype(F32)
        + hop(b[:, 0], 0, 2).astype(F32)
        + hop(b[:, 1], 1, 2).astype(F32)
    )
    for masks in reversed(bit_groups(nd)):
        low = cur.astype(BF).reshape(-1, len(masks), *tail)
        full = cur.reshape(-1, len(masks), *tail)
        cur = full[:, 0]
        for i, k in enumerate(masks[1:], 1):
            cur = cur + hop(low[:, i], k, 0).astype(F32)
    return cur[0]


def relative(x, me):
    return jnp.take(x, jnp.arange(x.shape[0], dtype=jnp.int32) ^ me, axis=0)


def split3(x):
    a = x.astype(BF)
    r = x - a.astype(F32)
    b = r.astype(BF)
    return a, b, (r - b.astype(F32)).astype(BF)


def swap64(x):
    return jnp.concatenate([x[:, 64:], x[:, :64]], axis=1)


def doubled(kp, head):
    lane = lax.broadcasted_iota(jnp.int32, kp.shape, 1)
    kr = swap64(kp)
    return jnp.where(lane < 64, kp, kr) if head == 0 else jnp.where(lane < 64, kr, kp)


ANY = pl.BlockSpec(memory_space=pl.ANY)
SMEM = pl.BlockSpec(memory_space=pltpu.SMEM)


def room(mib):
    return pltpu.CompilerParams(vmem_limit_bytes=mib << 20)


def call(kernel, outs, args, specs=None, scratch=(), name=None, flops=0, mib=ROOM):
    specs = [pl.BlockSpec(memory_space=pltpu.VMEM) if s is None else s for s in (specs or [None] * len(args))]
    size = sum(a.size * a.dtype.itemsize for a in args) + sum(
        int(np.prod(o.shape)) * np.dtype(o.dtype).itemsize for o in outs
    )
    return pl.pallas_call(
        kernel,
        in_specs=specs,
        out_specs=[pl.BlockSpec(memory_space=pltpu.VMEM)] * len(outs),
        out_shape=outs,
        scratch_shapes=list(scratch),
        cost_estimate=cost(size, flops),
        compiler_params=room(mib),
        name=name,
    )(*args)


def cost(size, flops=0):
    return pl.CostEstimate(flops=int(flops) // SLOW, bytes_accessed=int(size) // SLOW, transcendentals=0)


def sds(shape, dtype=F32):
    return jax.ShapeDtypeStruct(shape, dtype)


def by_rows(kernel, outs, sums, args, consts, info=None, name=None):
    n = args[0].shape[0]

    def cut(a):
        return pl.BlockSpec((RB, a.shape[1]), lambda i: (i, 0))

    def whole(a):
        return pl.BlockSpec(a.shape, lambda i: (0,) * len(a.shape))

    head = [] if info is None else [info]
    size = sum(a.size * a.dtype.itemsize for a in [*args, *consts])
    return pl.pallas_call(
        kernel,
        grid=(n // RB,),
        in_specs=[SMEM] * len(head) + [cut(a) for a in args] + [whole(a) for a in consts],
        out_specs=[cut(o) for o in outs] + [whole(o) for o in sums],
        out_shape=[*outs, *sums],
        cost_estimate=cost(size),
        compiler_params=room(60),
        name=name,
    )(*head, *args, *consts)


def start_sums(*refs):
    @pl.when(pl.program_id(0) == 0)
    def _():
        for r in refs:
            r[...] = jnp.zeros(r.shape, F32)


def start(copies):
    for cp in copies:
        cp.start()
    return copies


def load_pair(info, arrays, w_ref, sems):
    if len(arrays) == 1:
        return start([pltpu.make_async_copy(arrays[0].at[0], w_ref, sems.at[0])])
    nz = arrays[0].shape[1]
    rows = D // (2 * nz)
    copies = []
    for x, a in enumerate(arrays):
        for z in range(nz):
            at = pl.multiple_of((info[0] ^ (2 * z + x)) * rows, 16)
            copies.append(
                pltpu.make_async_copy(a.at[0, z, pl.ds(0, rows), :], w_ref.at[pl.ds(at, rows), :], sems.at[len(copies)])
            )
    return start(copies)


def load_rows(info, arrays, k, b_ref, sems):
    nz = arrays[0].shape[1]
    rows = D // (2 * nz)
    copies = []
    for x, a in enumerate(arrays):
        for z in range(nz):
            copies.append(
                pltpu.make_async_copy(
                    a.at[k, z, pl.ds(rows, b_ref.shape[1]), :], b_ref.at[info[0] ^ (2 * z + x)], sems.at[len(copies)]
                )
            )
    return start(copies)


def load_weight(info, arrays, k, w_ref, sems):
    if len(arrays) == 2:
        return start([pltpu.make_async_copy(a.at[k], w_ref.at[i], sems.at[i]) for i, a in enumerate(arrays)])
    nz = arrays[0].shape[1]
    rows = D // (2 * nz)
    copies = []
    for i, a in enumerate(arrays):
        for z in range(nz):
            at = pl.multiple_of((info[0] ^ (2 * z + i % 2)) * rows, 16)
            copies.append(
                pltpu.make_async_copy(
                    a.at[k, z, pl.ds(0, rows), :], w_ref.at[i // 2, pl.ds(at, rows), :], sems.at[len(copies)]
                )
            )
    return start(copies)


def wait(copies):
    for cp in copies:
        cp.wait()


def weight_scratch(arrays):
    count = len(arrays) if len(arrays) == 2 else 4 * arrays[0].shape[1]
    return [pltpu.VMEM((2, D, arrays[0].shape[-1]), BF), pltpu.SemaphoreType.DMA((count,))]


def gather_lines(local):
    k, rows, n = local.shape
    cur = local[:, None]
    *groups, last = bit_groups(lax.axis_size("dp"))
    for masks in groups:
        parts = [cur] + [hop(cur, b, 0) for b in masks[1:]]
        cur = jnp.stack(parts, 2).reshape(k, -1, rows, n)
    return [cur] + [hop(cur, b, 0) for b in last[1:]]


def gather_doubling(local, *others):
    k, rows, n = local.shape
    cur, got = local[:, None], []
    bit = lax.axis_size("dp") // 2
    while bit > 1:
        got.append(hop(cur, bit, 0))
        cur = jnp.stack([cur, got[-1]], 2).reshape(k, -1, rows, n)
        bit //= 2
    return cur, got


def join_lines(parts):
    k, _, rows, n = parts[0].shape
    return jnp.stack(parts, 2).reshape(k, -1, rows, n)


def gather_planes(cur, fast):
    near, far, far2 = hop(cur, 1, 0), hop(cur, 0, 2), hop(cur, 1, 2)
    if fast:
        return cur, near, far, far2
    me = lax.axis_index("dp")
    k, half, rows, n = cur.shape

    def ordered(a, b):
        both = jnp.stack([a, b], 2).reshape(k, 2 * half, rows, n)
        return jnp.moveaxis(relative(jnp.moveaxis(both, 1, 0), me), 0, 1).reshape(k, 2 * half * rows, n)

    return ordered(cur, near), ordered(far, far2)


def spread(info, g_ref, k, outs):
    nz = outs[0].shape[1]
    rows = D // (2 * nz)
    for z in range(nz):
        for x in range(2):
            at = pl.multiple_of((info[0] ^ (2 * z + x)) * rows, 8)
            outs[x][k, z, :rows] = g_ref[pl.ds(at, rows), :].astype(BF)


def grad_outs(k, ys, nd, rows, fast, more=0):
    return [sds((k, nd // 2, rows + more, D), BF)] * (2 * ys) if fast else [sds((k, D, D), BF)] * ys


def store_grad(info, k, y, g, g_ref, outs):
    if len(outs[0].shape) == 4:
        g_ref[...] = g
        spread(info, g_ref, k, outs[2 * y : 2 * y + 2])
    else:
        outs[y][k] = g.astype(BF)


def sum_first_kernel(count, *refs):
    parts, (keep_ref, *send_refs) = refs[:count], refs[count:]
    for k in range(parts[0].shape[0]):
        for z in range(parts[0].shape[1]):
            total = parts[0][k, z].astype(F32)
            for r in parts[1:]:
                total = total + r[k, z].astype(F32)
            if z == 0:
                keep_ref[k] = total
            else:
                send_refs[z - 1][k] = total.astype(BF)


def sum_planes(parts):
    if len(parts) == 2:
        return list(parts)
    keep, x, y, xy = parts
    return [keep, hop(x, 1, 0), hop(y, 0, 2), hop(xy, 1, 2)]


def sum_lines(parts):
    nd = lax.axis_size("dp")
    if len(parts) == 2:
        me = lax.axis_index("dp")
        k = parts[0].shape[0]
        near, far = (
            relative(jnp.moveaxis(p.reshape(k, nd, D // nd, D), 0, 1), me) for p in parts
        )
        return scatter_chips(near, far)
    return finish_lines(sum_blocks(parts))


def sum_blocks(parts):
    if len(parts) == 2:
        return parts
    k, nz, rows, n = parts[0].shape
    return call(
        functools.partial(sum_first_kernel, len(parts)),
        [sds((k, rows, n))] + [sds((k, rows, n), BF)] * (nz - 1),
        list(parts),
        name="grad_sum",
    )


def finish_lines(sums):
    own, low, *high = sums
    if len(high) != 2:
        for z, piece in enumerate([low, *high], 1):
            own = own + hop(piece, 2 * z, 0).astype(F32)
        return own
    got = hop(jnp.stack([low, high[1]]), 2, 0)
    send = (high[0].astype(F32) + got[1].astype(F32)).astype(BF)
    return own + got[0].astype(F32) + hop(send, 4, 0).astype(F32)


def bias_rows(b, first, count, low, high):
    return jnp.concatenate([b[first + i : first + i + 1, low:high] for i in range(count)], axis=1)


def block(ref, i):
    return ref[:, 128 * i : 128 * i + 128]


def attn_fwd_kernel(nh, info, own_ref, sib_ref, bias_ref, aux_ref, *rest):
    *arrays, proj_ref, w_ref, ctx_ref, lse_ref, w_sems, o_ref, b_ref, b_sems = rest
    copies = load_pair(info, arrays, w_ref, w_sems)
    hw = nh * HS
    if len(arrays) == 2:
        wait(load_rows(info, arrays, 0, b_ref, b_sems))
        nd = b_ref.shape[0]
        w = 2 * HS // nd

        def bias_part(first):
            return [b_ref[a, h : h + 1, :w] for h in range(nh) for a in range(first, first + nd // 2)]

        q_part, v_part = (
            jnp.concatenate(bias_part(a), axis=1).astype(F32) for a in (0, nd // 2)
        )
    else:
        bias = bias_ref[...].astype(F32)
        q_part = bias_rows(bias, 0, nh, 0, HS)
        v_part = bias_rows(bias, 0, nh, HS, 2 * HS)
    row_bias = jnp.concatenate([q_part, jnp.zeros((1, hw), F32), v_part, jnp.zeros((1, HS), F32)], axis=1)
    wait(copies)
    half = own_ref.shape[0]
    n = 2 * half
    for i, ref in enumerate((own_ref, sib_ref)):
        for j in range(2):
            r = slice(j * half // 2, (j + 1) * half // 2)
            out = dot(ref[r], w_ref[:, : 10 * HS], 1, 0) + row_bias
            proj_ref[i * half + r.start : i * half + r.stop] = out.astype(BF)
    qt = [jnp.transpose(block(proj_ref, i).astype(F32)) * (HS**-0.5 * LOG2E) for i in (0, 1)]
    hi = [q.astype(BF) for q in qt]
    lo = [(q - h.astype(F32)).astype(BF) for q, h in zip(qt, hi)]
    vt = [jnp.transpose(block(proj_ref, i).astype(F32)).astype(BF) for i in (3, 4)]
    row = lax.broadcasted_iota(jnp.int32, (128, QB), 0)
    auxq = jnp.where(row == 0, 1.0, 0.0).astype(BF)
    o_ref[0:HS] = jnp.zeros((HS, n), F32)
    lse_ref[...] = jnp.zeros(lse_ref.shape, F32)
    for h in range(nh):
        kb, kh = ((1, 1), (2, 0), (2, 1))[h]
        lhs = jnp.concatenate([doubled(block(proj_ref, kb), kh), aux_ref[...]], axis=1)
        i, r = h // 2, slice(64 * (h % 2), 64 * (h % 2) + 64)
        vaug = jnp.concatenate([vt[i][r], jnp.ones((16, n), BF)], axis=0)
        to = slice(64 * h + 64, 64 * h + 128)
        for b in range(n // QB):
            s = slice(b * QB, b * QB + QB)
            rhs = jnp.concatenate([hi[i][r, s], lo[i][r, s], auxq], axis=0)
            sc = dot(lhs, rhs, 1, 0)
            m = jnp.max(sc, axis=0, keepdims=True)
            p = jnp.exp2(sc - m).astype(BF)
            o = dot(vaug, p, 1, 0)
            total = o[64:65]
            o_ref[to, s] = o[:64] / total
            lse_ref[h : h + 1, s] = m + jnp.log2(total)
    for j in range(2):
        ctx_ref[:, 128 * j : 128 * j + 128] = jnp.transpose(o_ref[128 * j : 128 * j + 128]).astype(BF)


def attn_fwd(nh, info, own, sib, bias, aux, arrays):
    n = 2 * own.shape[0]
    count = len(arrays) * arrays[0].shape[1] if len(arrays) == 2 else 1
    return call(
        functools.partial(attn_fwd_kernel, nh),
        [sds((n, 10 * HS), BF), sds((D, D), BF), sds((n, 4 * HS), BF), sds((8, n))],
        [info, own, sib, bias, aux, *arrays],
        [SMEM] + [None] * 4 + [ANY] * len(arrays),
        [
            pltpu.SemaphoreType.DMA((count,)),
            pltpu.VMEM((4 * HS, n), F32),
            pltpu.VMEM((count, 16, D), BF),
            pltpu.SemaphoreType.DMA((count,)),
        ],
        "attn_fwd",
        flops=11_000_000_000,
    )


def out_kernel(first, c0_ref, c1_ref, w0_ref, w1_ref, out_ref):
    rows, cols = slice(first, first + out_ref.shape[0]), slice(8 * HS, 12 * HS)
    part = dot(c0_ref[rows], w0_ref[:, cols], 1, 1) + dot(c1_ref[rows], w1_ref[:, cols], 1, 1)
    out_ref[...] = part.astype(out_ref.dtype)


def norm(values, gain, shift):
    center = values - jnp.mean(values, -1, keepdims=True)
    spread_ = jnp.mean(center * center, -1, keepdims=True)
    scale = lax.rsqrt(spread_ + EPSILON)
    normed = center * scale
    return normed * gain + shift, normed, scale


def live_rows(aux_ref):
    return jnp.where(aux_ref[:, 0:1].astype(F32) > -1.0, 1.0, 0.0)


def square(live, v):
    return jnp.sum(jnp.sum(v * v, -1, keepdims=True) * live, axis=0, keepdims=True)


def ln1_kernel(part_ref, got_ref, tok_ref, aux_ref, wide_ref, first_ref, low_ref, n_ref, s_ref, sq_ref):
    start_sums(sq_ref)
    tok = tok_ref[...].astype(F32)
    att = part_ref[...] + got_ref[...].astype(F32) + wide_ref[0:1]
    first, normed, scale = norm(tok + att, wide_ref[1:2], wide_ref[2:3])
    first_ref[...] = first
    low_ref[...] = first.astype(BF)
    n_ref[...] = normed
    s_ref[...] = scale
    live = live_rows(aux_ref)
    lane = lax.broadcasted_iota(jnp.int32, (1, 128), 1)
    out = jnp.zeros((1, 128), F32)
    for i, v in enumerate((tok, att, first)):
        out = jnp.where(lane == i, square(live, v), out)
    sq_ref[...] += out


def hidden_bias(b_ref, nr):
    nd = b_ref.shape[0]
    w = HS // nd
    first = jnp.concatenate([b_ref[a, 0:1, :128] for a in range(nd)], axis=0)
    i = lax.broadcasted_iota(jnp.int32, (128, nr * HS), 0)
    f = lax.broadcasted_iota(jnp.int32, (128, nr * HS), 1)
    place = jnp.where(i == (f // HS) * w + f % w, 1.0, 0.0).astype(BF)
    spread_ = dot(first, place, 1, 0)
    a = lax.broadcasted_iota(jnp.int32, (nd, nr * HS), 0)
    f = lax.broadcasted_iota(jnp.int32, (nd, nr * HS), 1)
    return jnp.sum(jnp.where((f % HS) // w == a, spread_, 0.0), axis=0, keepdims=True)


def ffn_up_kernel(nh, nr, info, x_ref, b0_ref, b1_ref, *rest):
    *up, act_ref, slope_ref, up_ref, sems, r0_ref, r1_ref, r_sems = rest
    copies = load_weight(info, up, 0, up_ref, sems)
    fw = nr * HS
    x = x_ref[...]
    if len(up) == 4:
        for i, r_ref in enumerate((r0_ref, r1_ref)):
            wait(load_rows(info, up[2 * i : 2 * i + 2], 0, r_ref, r_sems))
        biases = [hidden_bias(r_ref, nr) for r_ref in (r0_ref, r1_ref)]
    else:
        biases = [bias_rows(b_ref[...].astype(F32), nh, nr, 0, HS) for b_ref in (b0_ref, b1_ref)]
    wait(copies)
    for y in range(2):
        for j in range(fw // 256):
            s = slice(j * 256, (j + 1) * 256)
            t = slice(y * fw + j * 256, y * fw + (j + 1) * 256)
            pre = dot(x, up_ref[y, :, s], 1, 0) + biases[y][:, s]
            phi = 0.5 + 0.5 * lax.erf(pre * (0.5**0.5))
            act_ref[:, t] = (pre * phi).astype(BF)
            slope_ref[:, t] = (phi + pre * (jnp.exp(-0.5 * pre * pre) * (2 * np.pi) ** -0.5)).astype(BF)


def product_kernel(k, info, a_ref, *rest):
    *w, out_ref, w_ref, sems = rest
    wait(load_weight(info, w, k, w_ref, sems))
    fw = w_ref.shape[2]
    out_ref[...] = (dot(a_ref[:, :fw], w_ref[0], 1, 1) + dot(a_ref[:, fw:], w_ref[1], 1, 1)).astype(out_ref.dtype)


def head_ones():
    a = lax.broadcasted_iota(jnp.int32, (CW, CW), 0) // (CW // PH)
    b = lax.broadcasted_iota(jnp.int32, (CW, CW), 1) // (CW // PH)
    return jnp.where(a == b, 1.0, 0.0)


def fdot(a, b, ca=1, cb=0):
    return lax.dot_general(a, b, (((ca,), (cb,)), ((), ())), precision=HIGHEST, preferred_element_type=F32)


def ln2_kernel(
    part_ref, got_ref, first_ref, aux_ref, wide_ref, narrow_ref, sw_ref, low_ref, n_ref, s_ref, st_ref, lg_ref, stat_ref
):
    feed = part_ref[...] + got_ref[...].astype(F32) + wide_ref[3:4]
    second, normed, scale = norm(first_ref[...] + feed, wide_ref[4:5], wide_ref[5:6])
    low = second.astype(BF)
    low_ref[...] = low
    n_ref[...] = normed
    s_ref[...] = scale
    student = dot(low, sw_ref[...], 1, 0) + narrow_ref[0:1]
    st_ref[...] = student
    live = live_rows(aux_ref)
    logit = fdot(student * narrow_ref[1:2], head_ones()) * (CW // PH) ** -0.5
    logit = jnp.where(live > 0.0, logit, NEGATIVE)
    lg_ref[...] = logit

    @pl.when(pl.program_id(0) == 0)
    def _():
        stat_ref[...] = jnp.zeros((8, 128), F32)
        stat_ref[0:1] = jnp.full((1, 128), NEGATIVE, F32)

    old = stat_ref[0:1]
    top = jnp.maximum(old, jnp.max(logit, axis=0, keepdims=True))
    shrink = jnp.exp(old - top)
    weight = jnp.where(live > 0.0, jnp.exp(logit - top), 0.0)
    stat_ref[0:1] = top
    stat_ref[1:2] = stat_ref[1:2] * shrink + jnp.sum(weight, axis=0, keepdims=True)
    stat_ref[2:3] = stat_ref[2:3] * shrink + jnp.sum(weight * student, axis=0, keepdims=True)
    stat_ref[3:4] += jnp.broadcast_to(square(live, feed), (1, 128))


def norm_back(up, normed, scale, gain):
    scaled = up * gain
    inner = scaled - jnp.mean(scaled, -1, keepdims=True) - normed * jnp.mean(scaled * normed, -1, keepdims=True)
    return inner * scale


def colsum(x):
    return jnp.sum(x, axis=0, keepdims=True)


def head_kernel(
    info,
    st_ref,
    lg_ref,
    low_ref,
    cot_ref,
    n_ref,
    s_ref,
    stat_ref,
    sib_ref,
    sq_ref,
    pooler_ref,
    class_ref,
    cb_ref,
    narrow_ref,
    sw_ref,
    wide_ref,
    dr2_ref,
    dffn_ref,
    gst_ref,
    gpool_ref,
    gclass_ref,
    rep_ref,
    vec_ref,
    nvec_ref,
    keep_ref,
):
    scale = (CW // PH) ** -0.5
    once = jnp.where(info[1] == 0, 1.0, 0.0)

    @pl.when(pl.program_id(0) == 0)
    def _():
        top, top2 = stat_ref[0:1], sib_ref[0:1]
        best = jnp.maximum(top, top2)
        fa, fb = jnp.exp(top - best), jnp.exp(top2 - best)
        whole = stat_ref[1:2] * fa + sib_ref[1:2] * fb
        pooled = (stat_ref[2:3] * fa + sib_ref[2:3] * fb) / whole
        pooled = jnp.broadcast_to(pooled, (8, CW))
        z = jnp.tanh(fdot(pooled, pooler_ref[...]) + narrow_ref[2:3])
        lane = lax.broadcasted_iota(jnp.int32, (8, 128), 1)
        row = lax.broadcasted_iota(jnp.int32, (8, 128), 0)
        logit = fdot(z, class_ref[...]) + cb_ref[...]
        masked = jnp.where(lane < CLASSES, logit, NEGATIVE)
        e = jnp.exp(masked - jnp.max(masked, axis=1, keepdims=True))
        dlogit = e / jnp.sum(e, axis=1, keepdims=True) - jnp.where(lane == info[3], 1.0, 0.0)
        only = jnp.where(row == 0, once, 0.0)
        gclass_ref[...] = fdot(z * only, dlogit, 0, 0)
        dz = fdot(dlogit, class_ref[...], 1, 1)
        dzp = dz * (1.0 - z * z)
        gpool_ref[...] = fdot(pooled * only, dzp, 0, 0)
        dpooled = fdot(dzp, pooler_ref[...], 1, 1)
        sq = jnp.where(lane[0:1] == 3, stat_ref[3:4] + sib_ref[3:4] * 0.0, sq_ref[...])
        sq = jnp.where(info[1] == 0, pltpu.roll(sq, 2 * CLASSES, 1), pltpu.roll(sq, 2 * CLASSES + 4, 1))
        rep = jnp.where(lane < CLASSES, logit, pltpu.roll(jnp.where(lane < CLASSES, dlogit, 0.0), CLASSES, 1)) * once
        rep_ref[...] = jnp.where(lane < 2 * CLASSES, rep, sq)
        nvec_ref[...] = jnp.zeros((8, CW), F32)
        nvec_ref[2:3] = dzp[0:1] * once
        vec_ref[...] = jnp.zeros((8, D), F32)
        gst_ref[...] = jnp.zeros((D, CW), F32)
        keep_ref[0:1] = best
        keep_ref[1:2] = whole
        keep_ref[2:3] = dpooled[0:1]
        keep_ref[3:4] = fdot(pooled * dpooled, head_ones())[0:1]

    student = st_ref[...]
    dp = keep_ref[2:3]
    logit = lg_ref[...]
    weight = jnp.where(logit > 0.5 * NEGATIVE, jnp.exp(logit - keep_ref[0:1]), 0.0) / keep_ref[1:2]
    dq = scale * weight * (fdot(student * dp, head_ones()) - keep_ref[3:4])
    dstudent = (weight * dp + dq * narrow_ref[1:2]).astype(BF)
    nvec_ref[0:1] += colsum(dstudent.astype(F32))
    nvec_ref[1:2] += colsum(dq * student)
    gst_ref[...] += dot(low_ref[...], dstudent, 0, 0)
    dsecond = dot(dstudent, sw_ref[...], 1, 1) + cot_ref[...].astype(F32)
    normed = n_ref[...]
    dr2 = norm_back(dsecond, normed, s_ref[...], wide_ref[4:5])
    dr2_ref[...] = dr2
    dffn_ref[...] = dr2.astype(BF)
    vec_ref[0:1] += colsum(dr2)
    vec_ref[1:2] += colsum(dsecond * normed)
    vec_ref[2:3] += colsum(dsecond)


def ffn_back_kernel(info, g_ref, slope_ref, *rest):
    *down, dpre_ref, ub_ref, w_ref, sems = rest
    copies = load_weight(info, down, 1, w_ref, sems)
    fw = w_ref.shape[2]
    g = g_ref[...]
    ub_ref[...] = jnp.zeros(ub_ref.shape, F32)
    wait(copies)
    for y in range(2):
        for j in range(fw // 256):
            s = slice(j * 256, (j + 1) * 256)
            t = slice(y * fw + j * 256, y * fw + (j + 1) * 256)
            dpre = (dot(g, w_ref[y, :, s], 1, 0) * slope_ref[:, t].astype(F32)).astype(BF)
            dpre_ref[:, t] = dpre
            ub_ref[0:1, t] = colsum(dpre.astype(F32))


def ffn_grad_kernel(info, first, first2, dpre, dpre2, dffn, dffn2, act, act2, *rest):
    *outs, g_ref = rest
    fw = dpre.shape[1] // 2
    for k, (a0, a1, b0, b1) in enumerate(((first, first2, dpre, dpre2), (dffn, dffn2, act, act2))):
        for y in range(2):
            s = slice(y * fw, (y + 1) * fw)
            g = dot(a0[...], b0[:, s], 0, 0) + dot(a1[...], b1[:, s], 0, 0)
            if len(outs) == 2:
                outs[y][k] = g.astype(BF)
                continue
            g_ref[...] = g
            nz = outs[0].shape[1]
            rows = D // (2 * nz)
            for z in range(nz):
                for x in range(2):
                    at = pl.multiple_of((info[0] ^ (2 * z + x)) * rows, 8)
                    piece = g_ref[pl.ds(at, rows), :].astype(BF)
                    if k == 0:
                        outs[y][x, z] = piece
                    else:
                        outs[2 + x][y, z] = piece


def sum_half_kernel(a_ref, ga_ref, b_ref, gb_ref, keep_ref, sa_ref, sb_ref):
    for k, (r, g, send_ref) in enumerate(((a_ref, ga_ref, sa_ref), (b_ref, gb_ref, sb_ref))):
        for z in range(r.shape[1]):
            keep_ref[k, z] = (r[0, z].astype(F32) + g[0, z].astype(F32)).astype(BF)
            send_ref[z] = (r[1, z].astype(F32) + g[1, z].astype(F32)).astype(BF)


def sum_last_kernel(keep_ref, a_ref, b_ref, own_ref, *send_refs):
    for k, g in enumerate((a_ref, b_ref)):
        for z in range(keep_ref.shape[1]):
            total = keep_ref[k, z].astype(F32) + g[z].astype(F32)
            if z == 0:
                own_ref[k] = total
            else:
                send_refs[z - 1][k] = total.astype(BF)


def ln1_back_kernel(part_ref, got_ref, dr2_ref, n_ref, s_ref, wide_ref, dr1_ref, low_ref, vec_ref):
    start_sums(vec_ref)
    up = part_ref[...] + got_ref[...].astype(F32) + dr2_ref[...]
    normed = n_ref[...]
    dr1 = norm_back(up, normed, s_ref[...], wide_ref[1:2])
    dr1_ref[...] = dr1
    low_ref[...] = dr1.astype(BF)
    vec_ref[0:1] += colsum(dr1)
    vec_ref[1:2] += colsum(up * normed)
    vec_ref[2:3] += colsum(up)


def attn_bwd_kernel(nh, proj_ref, w_ref, aux_ref, ctx_ref, da_ref, db_ref, lse_ref, out_ref, sum_ref, do_ref, dqt_ref):
    n = proj_ref.shape[0]
    half = n // 2
    scale = HS**-0.5
    cols = slice(8 * HS, 12 * HS)
    for i, ref in enumerate((da_ref, db_ref)):
        do_ref[i * half : (i + 1) * half] = dot(ref[...], w_ref[:, cols], 1, 0).astype(BF)
    qb = [block(proj_ref, i) for i in (0, 1)]
    qt = [jnp.transpose(q.astype(F32)) * (scale * LOG2E) for q in qb]
    hi = [q.astype(BF) for q in qt]
    lo = [(q - h.astype(F32)).astype(BF) for q, h in zip(qt, hi)]
    kt = [jnp.transpose(block(proj_ref, i).astype(F32)).astype(BF) for i in (1, 2)]
    dob = [block(do_ref, i) for i in (0, 1)]
    dot_f = [jnp.transpose(d.astype(F32)) for d in dob]
    dot_b = [d.astype(BF) for d in dot_f]
    prod = [d * jnp.transpose(block(ctx_ref, i).astype(F32)) for i, d in enumerate(dot_f)]
    lane = lax.broadcasted_iota(jnp.int32, (n, 128), 1)
    row = lax.broadcasted_iota(jnp.int32, (128, QB), 0)
    zero = jnp.zeros((64, QB), BF)
    empty = jnp.zeros((n, 128), BF)
    dqt_ref[...] = jnp.zeros(dqt_ref.shape, F32)
    dk, dv = [], []
    for h in range(nh):
        kb, kh = ((1, 1), (2, 0), (2, 1))[h]
        i, ih = h // 2, h % 2
        vi, vh = ((3, 0), (3, 1), (4, 0))[h]
        oi, oh = ((0, 1), (1, 0), (1, 1))[h]
        lhs = jnp.concatenate([doubled(block(proj_ref, kb), kh), aux_ref[...]], axis=1)
        lhs_v = jnp.concatenate([block(proj_ref, vi), aux_ref[...]], axis=1)
        r = slice(64 * ih, 64 * ih + 64)
        ro = slice(64 * oh, 64 * oh + 64)
        rk = slice(64 * kh, 64 * kh + 64)
        qm = jnp.where((lane < 64) == (ih == 0), qb[i], empty)
        dom = jnp.where((lane < 64) == (oh == 0), dob[oi], empty)
        dsum = jnp.sum(prod[oi][ro], axis=0, keepdims=True)
        l1, l2, l3 = split3(-lse_ref[h : h + 1, :])
        d1, d2, d3 = split3(-dsum)
        dkh = jnp.zeros((n, 128), F32)
        dvh = jnp.zeros((n, 128), F32)
        for b in range(n // QB):
            s = slice(b * QB, b * QB + QB)

            def pieces(first, x1, x2, x3):
                z = jnp.where(row == 1, x1[:, s].astype(F32), jnp.where(row == 0, first, 0.0))
                z = jnp.where(row == 2, x2[:, s].astype(F32), z)
                return jnp.where(row == 3, x3[:, s].astype(F32), z).astype(BF)

            rhs = jnp.concatenate([hi[i][r, s], lo[i][r, s], pieces(1.0, l1, l2, l3)], axis=0)
            p = jnp.exp2(dot(lhs, rhs, 1, 0))
            g = dot_b[oi][ro, s]
            part = [g, zero] if vh == 0 else [zero, g]
            rhs_v = jnp.concatenate(part + [pieces(0.0, d1, d2, d3)], axis=0)
            ds = (p * dot(lhs_v, rhs_v, 1, 0)).astype(BF)
            dvh = dvh + dot(p.astype(BF), dom[s], 1, 0)
            dkh = dkh + dot(ds, qm[s], 1, 0)
            dqt_ref[64 * h : 64 * h + 64, s] = dot(kt[kb - 1][rk], ds, 1, 0)
        dk.append(dkh * scale)
        dv.append(dvh)

    def put(i, x):
        out_ref[:, 128 * i : 128 * i + 128] = x.astype(BF)
        sum_ref[:, 128 * i : 128 * i + 128] = jnp.broadcast_to(colsum(x.astype(BF).astype(F32)), (8, 128))

    left = lane < 64
    put(0, jnp.transpose(dqt_ref[0:128] * scale))
    put(1, jnp.where(left, jnp.transpose(dqt_ref[128:256] * scale), swap64(dk[0])))
    put(2, jnp.where(left, swap64(dk[1]), swap64(dk[2])))
    put(3, jnp.where(left, swap64(dv[0]), swap64(dv[1])))
    put(4, jnp.where(left, swap64(dv[2]), 0.0))


def attn_bwd(nh, proj, w, aux, ctx, da, db, lse):
    n = proj.shape[0]
    return call(
        functools.partial(attn_bwd_kernel, nh),
        [sds((n, 10 * HS), BF), sds((8, 10 * HS))],
        [proj, w, aux, ctx, da, db, lse],
        None,
        [pltpu.VMEM((n, 4 * HS), BF), pltpu.VMEM((4 * HS, n), F32)],
        "attn_bwd",
        flops=11_000_000_000,
    )


def token_grad_kernel(g0_ref, g1_ref, w0_ref, w1_ref, dr1_ref, send_ref, own_ref):
    n = g0_ref.shape[0]
    half = n // 2
    cols = slice(0, 10 * HS)
    for out_ref, s in ((send_ref, slice(half, n)), (own_ref, slice(0, half))):
        part = dot(g0_ref[s], w0_ref[:, cols], 1, 1) + dot(g1_ref[s], w1_ref[:, cols], 1, 1)
        if out_ref is own_ref:
            part = part + dr1_ref[...]
        out_ref[...] = part.astype(out_ref.dtype)


def qkv_grad_kernel(nh, info, x0, x1, g_in, da, db, ctx_ref, sum_ref, *rest):
    *outs, g_ref, t_ref = rest
    half = x0.shape[0]
    g = dot(x0[...], g_in[:half], 0, 0) + dot(x1[...], g_in[half:], 0, 0)
    o = dot(da[...], ctx_ref[:half], 0, 0) + dot(db[...], ctx_ref[half:], 0, 0)
    g = jnp.concatenate([g[:, : 8 * HS], g[:, 8 * HS :] + o[:, : 2 * HS], o[:, 2 * HS :]], axis=1)
    store_grad(info, 0, 0, g, g_ref, outs)
    if len(outs) == 2:
        nz = outs[0].shape[1]
        rows = D // (2 * nz)
        piece = HS // nz
        zero = jnp.zeros((1, 128 - nh * piece), F32)
        for a in range(2 * nz):
            base = (a % nz) * piece + (a // nz) * 2 * nh * HS
            cuts = [sum_ref[0:1, base + h * HS : base + h * HS + piece] for h in range(nh)]
            t_ref[a : a + 1] = jnp.concatenate([*cuts, zero], axis=1)
        for z in range(nz):
            for x in range(2):
                outs[x][0, z, rows:] = jnp.zeros((outs[x].shape[2] - rows, D), BF)
                row = t_ref[pl.ds(info[0] ^ (2 * z + x), 1), :]
                outs[x][0, z, rows : rows + 8, :128] = jnp.broadcast_to(row, (8, 128)).astype(BF)


def place_kernel(info, a_ref, b_ref, c_ref, d_ref, out_ref):
    c, y = info[1], info[2]
    out_ref[0, y, c] = a_ref[0]
    out_ref[0, 1 - y, c] = b_ref[0]
    out_ref[0, y, 1 - c] = c_ref[0]
    out_ref[0, 1 - y, 1 - c] = d_ref[0]


def lanes(x):
    x = x.reshape(1, -1) if x.ndim == 1 else x
    return jnp.pad(x, ((0, 0), (0, 128 - x.shape[1])))


def vectors_kernel(sizes, info, a0, a1, wide_ref, narrow_ref, b_ref, sems):
    rows, cr, nh, _ = sizes
    wait(load_rows(info, [a0, a1], 0, b_ref, sems))
    nd = b_ref.shape[0]
    for out_ref, row, count, width in ((wide_ref, nh, 6, rows), (narrow_ref, nh + 6, 3, cr)):
        out_ref[...] = jnp.zeros(out_ref.shape, F32)
        for i in range(count):
            cuts = [b_ref[a, row + i : row + i + 1, :width] for a in range(nd)]
            out_ref[i : i + 1] = jnp.concatenate(cuts, axis=1).astype(F32)


def matrices_kernel(info, a0, a1, sw_ref, pooler_ref, class_ref, b_ref, c_ref, sems):
    copies = load_rows(info, [a0, a1], 0, b_ref, sems.at[0])
    copies += load_rows(info, [a0, a1], 1, c_ref, sems.at[1])
    wait(copies)
    for a in range(b_ref.shape[0]):
        for i in range(2):
            at = slice(16 * a + 8 * i, 16 * a + 8 * i + 8)
            pooler_ref[at] = b_ref[a, 8:16, 128 * i : 128 * i + 128].astype(F32)
            class_ref[at] = b_ref[a, 8:16, 256 + 128 * i : 384 + 128 * i].astype(F32)
        for i in range(6):
            at = 96 * a + 16 * i
            sw_ref[at : at + 16] = c_ref[a, :, 128 * i : 128 * i + 128]


def unpack_kernel(sizes, in_ref, sw_ref, pooler_ref, class_ref, wide_ref, narrow_ref, bias_ref):
    rows, cr, nh, nr = sizes
    nd = in_ref.shape[0]
    blocks = [in_ref[d].astype(F32) for d in range(nd)]
    at = rows + 2 * cr

    def joined(first, count, width):
        return jnp.concatenate([b[first : first + count, :width] for b in blocks], axis=1)

    sw_ref[...] = jnp.concatenate([b[:rows] for b in blocks], axis=0).astype(BF)
    pooler_ref[...] = jnp.concatenate([b[rows : rows + cr] for b in blocks], axis=0)
    class_ref[...] = jnp.concatenate([b[rows + cr : at] for b in blocks], axis=0)
    wide_ref[...] = jnp.zeros(wide_ref.shape, F32)
    wide_ref[0:6] = joined(at, 6, rows)
    narrow_ref[...] = jnp.zeros(narrow_ref.shape, F32)
    narrow_ref[0:3] = joined(at + 6, 3, cr)
    bias_ref[...] = jnp.zeros(bias_ref.shape, F32)
    bias_ref[0:nh, :] = joined(at + 9, nh, 2 * HS // nd)
    bias_ref[nh : nh + nr, :HS] = joined(at + 9 + nh, nr, HS // nd)


def pack_grads_kernel(sizes, info, gst, gpool, gclass, v1, v2, nv, ub0, ub1, rep, out_ref):
    rows, cr, nh, nr = sizes
    nd = out_ref.shape[0]
    fw = nr * HS
    me = info[2] * 2 + info[1]
    ub = ub0[0:1] + ub1[0:1]
    pair = [
        jnp.concatenate([ub[:, y * fw + r * HS : y * fw + (r + 1) * HS] for r in range(nr)], axis=0) for y in range(2)
    ]
    quads = jnp.concatenate(
        [jnp.where(me == q, pair[0], jnp.where((me ^ 2) == q, pair[1], 0.0)) for q in range(4)], axis=0
    )
    wide = jnp.concatenate([v1[0:1], v1[1:2], v1[2:3], v2[0:1], v2[1:2], v2[2:3]], axis=0)

    def wider(x):
        return jnp.concatenate([x, jnp.zeros((x.shape[0], 128 - x.shape[1]), F32)], axis=1)

    total = 2 * nd
    row = lax.broadcasted_iota(jnp.int32, (total, 128), 0)
    high = rep[0:1].astype(BF).astype(F32)
    mine = row == 2 * info[0] + info[2]
    table = [jnp.where(mine, high, 0.0), jnp.where(mine, rep[0:1] - high, 0.0)]
    hs = HS // nd
    for d in range(nd):
        parts = [
            gst[d * rows : (d + 1) * rows],
            gpool[d * cr : (d + 1) * cr],
            gclass[d * cr : (d + 1) * cr],
            wider(wide[:, d * rows : (d + 1) * rows]),
            wider(nv[0:3, d * cr : (d + 1) * cr]),
            wider(quads[:, d * hs : (d + 1) * hs]),
            *table,
        ]
        parts = jnp.concatenate(parts, axis=0)
        out_ref[d, : parts.shape[0]] = parts
        if parts.shape[0] < out_ref.shape[1]:
            out_ref[d, parts.shape[0] :] = jnp.zeros((out_ref.shape[1] - parts.shape[0], 128), F32)


def body(
    hidden_in,
    cotangent,
    lengths,
    labels,
    qkv_weight,
    qv_bias,
    out_weight,
    out_bias,
    norm1_gain,
    norm1_bias,
    up_weight,
    up_bias,
    down_weight,
    down_bias,
    norm2_gain,
    norm2_bias,
    student_weight,
    student_bias,
    pool_query,
    pooler_weight,
    pooler_bias,
    class_weight,
    class_bias,
):
    nd = lax.axis_size("dp")
    me = lax.axis_index("dp")
    m = lax.axis_index("mp")
    c, y = m % 2, m // 2
    total, pd, _ = hidden_in.shape
    assert total == 2 * nd and lax.axis_size("mp") == 4
    hp = pd // 2
    half = nd * hp
    rows, cr = D // nd, CW // nd
    nh, nr = qv_bias.shape[0], up_bias.shape[0]
    hw, fw = nh * HS, nr * HS
    fast = nd == 8
    sizes = (rows, cr, nh, nr)
    seq = 2 * me + y
    length = lengths[seq]
    info = jnp.stack([me, c, y, labels[seq]]).astype(jnp.int32)

    def deal(x):
        x = x.reshape(nd, 2, 2, hp, D)
        x = lax.dynamic_slice(x, (0, y, c, 0, 0), (nd, 1, 1, hp, D)).reshape(nd, hp, D)
        return lax.all_to_all(x, "dp", 0, 0, tiled=True).reshape(half, D)

    def undeal(x):
        return lax.all_to_all(x.reshape(nd, hp, D), "dp", 0, 0, tiled=True)

    def place(a, b):
        one = pl.BlockSpec((1, hp, D), lambda d: (d, 0, 0))
        out = pl.pallas_call(
            place_kernel,
            grid=(nd,),
            in_specs=[SMEM] + [one] * 4,
            out_specs=pl.BlockSpec((1, 2, 2, hp, D), lambda d: (d, 0, 0, 0, 0)),
            out_shape=sds((nd, 2, 2, hp, D), BF),
            cost_estimate=cost(6_000_000),
            compiler_params=room(8),
            name="place",
        )(info, a, b, hop(a, 0, 1), hop(b, 0, 1))
        return out.reshape(total, pd, D)

    qo = jnp.concatenate([jnp.transpose(qkv_weight, (1, 0, 2)).reshape(rows, 3 * hw), out_weight.T], axis=1)
    if fast:
        vectors = [qv_bias]
        vectors += [v[None] for v in (out_bias, norm1_gain, norm1_bias, down_bias, norm2_gain, norm2_bias)]
        vectors += [v[None] for v in (student_bias, pool_query, pooler_bias)]
        vectors = [jnp.pad(v, ((0, 0), (0, 128 - v.shape[1]))) for v in vectors]
        vectors = jnp.concatenate([*vectors, jnp.zeros((7 - nh, 128), BF)], axis=0)
        qo = jnp.concatenate([qo, jnp.pad(vectors, ((0, 0), (0, D - 128)))], axis=0)
    qo_line = join_lines(gather_lines(qo[None]))
    tokens = deal(after(hidden_in, qo_line))
    w_qo = gather_planes(qo_line, fast)
    w_qo = (w_qo[:2], w_qo[2:]) if fast else (w_qo[:1], w_qo[1:])
    up_pack, down_pack = up_weight, down_weight.T
    if fast:
        row = jnp.pad(up_bias.reshape(1, -1), ((0, 7), (0, D - up_bias.size)))
        cls = lanes(class_weight)
        more = jnp.concatenate([pooler_weight[:8], pooler_weight[8:], cls[:8], cls[8:]], axis=1)
        more = jnp.pad(more, ((0, 0), (0, D - 512)))
        up_pack = jnp.concatenate([up_pack, row, more], axis=0)
        more = jnp.concatenate([student_weight[16 * i : 16 * i + 16] for i in range(6)], axis=1)
        down_pack = jnp.concatenate([down_pack, more], axis=0)
    f_line, f_got = gather_doubling(after(jnp.stack([up_pack, down_pack]), qo_line))
    class_b = lanes(class_bias.astype(F32))
    cot = deal(cotangent)

    index = jnp.arange(half, dtype=jnp.int32)
    position = (index // hp) * pd + index % hp
    position = jnp.concatenate([position + c * hp, position + (1 - c) * hp])
    col = jnp.arange(128, dtype=jnp.int32)[None, :]
    aux = jnp.where(
        col == 0, jnp.where(position < length, 0.0, NEGATIVE)[:, None], jnp.where(col <= 3, 1.0, 0.0)
    ).astype(BF)
    aux_own = aux[:half]

    sib = hop(after(tokens, w_qo, f_got[0]), 0, 1)
    n = 2 * half
    biases = [aux, aux]
    if not fast:
        piece = jnp.broadcast_to(qv_bias[None], (nd, *qv_bias.shape))
        piece = lax.all_to_all(piece, "dp", 0, 0, tiled=True)
        piece = jnp.transpose(piece, (1, 0, 2)).reshape(nh, 2 * HS)
        piece = jnp.pad(piece, ((0, 16 - nh), (0, 0)))
        biases = [piece, hop(piece, 0, 2)]
    proj0, w0, ctx0, lse0 = attn_fwd(nh, info, tokens, sib, biases[0], aux, w_qo[0])
    if fast:
        wide, narrow = call(
            functools.partial(vectors_kernel, sizes),
            [sds((8, D)), sds((8, CW))],
            [info, *w_qo[0]],
            [SMEM, ANY, ANY],
            [pltpu.VMEM((nd, 16, D), BF), pltpu.SemaphoreType.DMA((nd,))],
            "vectors",
        )
        bias_near = bias_far = aux
    else:
        small = jnp.concatenate(
            [student_weight, pooler_weight]
            + [
                lanes(v)
                for v in (
                    class_weight,
                    out_bias,
                    norm1_gain,
                    norm1_bias,
                    down_bias,
                    norm2_gain,
                    norm2_bias,
                    student_bias,
                    pool_query,
                    pooler_bias,
                    qv_bias,
                    up_bias,
                )
            ],
            axis=0,
        )
        small = jnp.pad(small, ((0, -small.shape[0] % 16), (0, 0)))
        small = lax.all_to_all(jnp.broadcast_to(small[None], (nd, *small.shape)), "dp", 0, 0, tiled=True)
        student_w, pooler_f, class_f, wide, narrow, bias_near = call(
            functools.partial(unpack_kernel, sizes),
            [sds((D, CW), BF), sds((CW, CW)), sds((CW, CW)), sds((8, D)), sds((8, CW)), sds((16, 128))],
            [small],
            name="unpack",
        )
        bias_near = bias_near.astype(BF)
        bias_far = hop(bias_near, 0, 2)
    proj1, w1, ctx1, lse1 = attn_fwd(nh, info, tokens, sib, biases[1], after(aux, ctx0), w_qo[1])
    w_ffn = gather_planes(f_line, fast)

    if fast:
            ctx1 = after(ctx1, wide)

    def out(first, kind):
        return call(
            functools.partial(out_kernel, first), [sds((half, D), kind)], [ctx0, ctx1, w0, w1], name="out"
        )[0]

    att_got = hop(out(half, BF), 0, 1)
    att_part = out(0, F32)
    first, first_low, n1, s1, sq1 = by_rows(
        ln1_kernel,
        [sds((half, D)), sds((half, D), BF), sds((half, D)), sds((half, 1))],
        [sds((1, 128))],
        [att_part, att_got, tokens, aux_own],
        [wide],
        name="ln1",
    )
    first_sib = hop(after(first_low, w_ffn), 0, 1)

    if fast:
        student_w, pooler_f, class_f = call(
            matrices_kernel,
            [sds((D, CW), BF), sds((CW, CW)), sds((CW, CW))],
            [info, *w_ffn[:2]],
            [SMEM, ANY, ANY],
            [pltpu.VMEM((nd, 16, D), BF)] * 2 + [pltpu.SemaphoreType.DMA((2, nd))],
            "matrices",
        )

    def ffn_up(x):
        return call(
            functools.partial(ffn_up_kernel, nh, nr),
            [sds((half, 2 * fw), BF), sds((half, 2 * fw), BF)],
            [info, x, bias_near, bias_far, *w_ffn],
            [SMEM] + [None] * 3 + [ANY] * len(w_ffn),
            weight_scratch(w_ffn)
            + [pltpu.VMEM((max(nd, 8), 8, D), BF)] * 2
            + [pltpu.SemaphoreType.DMA((nd,))],
            "ffn_up",
        )

    def product(a, k, kind):
        return call(
            functools.partial(product_kernel, k),
            [sds((half, D), kind)],
            [info, a, *w_ffn],
            [SMEM, None] + [ANY] * len(w_ffn),
            weight_scratch(w_ffn),
            "product",
        )[0]

    act, slope = ffn_up(first_low)
    act_sib, slope_sib = ffn_up(after(first_sib, act))
    ffn_got = hop(product(act_sib, 1, BF), 0, 1)
    ffn_part = product(act, 1, F32)
    second_low, n2, s2, student, pool_logit, stat = by_rows(
        ln2_kernel,
        [sds((half, D), BF), sds((half, D)), sds((half, 1)), sds((half, CW)), sds((half, CW))],
        [sds((8, 128))],
        [ffn_part, ffn_got, after(first, cot), aux_own],
        [wide, narrow, student_w],
        name="ln2",
    )
    hidden_a = undeal(second_low)
    hidden_b = hop(hidden_a, 0, 2)

    dr2, dffn, g_st, g_pool, g_class, report, vec2, nvec, _ = by_rows(
        head_kernel,
        [sds((half, D)), sds((half, D), BF)],
        [
            sds((D, CW)),
            sds((CW, CW)),
            sds((CW, CW)),
            sds((8, 128)),
            sds((8, D)),
            sds((8, CW)),
            sds((8, 128)),
        ],
        [student, pool_logit, second_low, cot, n2, s2],
        [stat, hop(stat, 0, 1), sq1, pooler_f, class_f, class_b, narrow, student_w, wide],
        info,
        "head",
    )
    dffn_sib = hop(dffn, 0, 1)

    def ffn_back(g, s):
        return call(
            ffn_back_kernel,
            [sds((half, 2 * fw), BF), sds((8, 2 * fw))],
            [info, g, s, *w_ffn],
            [SMEM, None, None] + [ANY] * len(w_ffn),
            weight_scratch(w_ffn),
            "ffn_back",
        )

    dpre, ub0 = ffn_back(dffn, slope)
    dpre_sib, ub1 = ffn_back(after(dffn_sib, dpre, hidden_a), slope_sib)
    dfirst_got = hop(product(dpre_sib, 0, BF), 0, 1)
    dfirst_part = product(dpre, 0, F32)
    f_grads = call(
        ffn_grad_kernel,
        grad_outs(2, 2, nd, rows, fast),
        [info, first_low, first_sib, dpre, dpre_sib, dffn, dffn_sib, act, act_sib],
        [SMEM] + [None] * 8,
        [pltpu.VMEM((D, D), F32)],
        "ffn_grad",
    )
    dr1, dattn, vec1 = by_rows(
        ln1_back_kernel,
        [sds((half, D)), sds((half, D), BF)],
        [sds((8, D))],
        [dfirst_part, dfirst_got, after(dr2, hidden_b), n1, s1],
        [wide],
        name="ln1_back",
    )
    dattn_sib = hop(dattn, 0, 1)
    dattn_sib = after(dattn_sib, f_grads, hidden_b)
    if fast:
        up_keep, up_send, down_keep, down_send = f_grads
        up_got, down_got = hop(up_send, 0, 2), hop(down_send, 1, 0)
    count = rows + 2 * cr + 9 + 4 * nr + 2 * total
    (small_g,) = call(
        functools.partial(pack_grads_kernel, sizes),
        [sds((nd, count + -count % 16, 128))],
        [info, g_st, g_pool, g_class, vec1, vec2, nvec, ub0, ub1, report],
        [SMEM] + [None] * 9,
        name="pack",
    )
    small_g = small_g + hop(small_g.astype(BF), 0, 1).astype(F32)
    small_y = small_g + hop(small_g.astype(BF), 0, 2).astype(F32)


    def qkv_grad(g, ctx, sums):
        return call(
            functools.partial(qkv_grad_kernel, nh),
            grad_outs(1, 1, nd, rows, fast, 8),
            [info, tokens, sib, g, dattn, dattn_sib, ctx, sums],
            [SMEM] + [None] * 7,
            [pltpu.VMEM((D, D), F32), pltpu.VMEM((max(8, nd), 128), F32)],
            "qkv_grad",
        )

    g1, g1_sum = attn_bwd(nh, proj1, w1, aux, ctx1, dattn, after(dattn_sib, small_y), lse1)
    far_grad = qkv_grad(g1, ctx1, g1_sum)
    if fast:
        far_got = hop(far_grad[1], 1, 0)
    g0, g0_sum = attn_bwd(
        nh, proj0, w0, aux, ctx0, dattn, after(dattn_sib, g1, far_grad), lse0
    )
    if fast:
        g0, up_got, down_got = lax.optimization_barrier((g0, up_got, down_got))
    tok_send, tok_own = call(
        token_grad_kernel, [sds((half, D), BF), sds((half, D))], [g0, g1, w0, w1, dr1], name="token_grad"
    )
    near_grad = qkv_grad(g0, ctx0, g0_sum)
    tok_sum = after((tok_own + hop(tok_send, 0, 1).astype(F32)).astype(BF), near_grad)
    input_a = undeal(tok_sum)
    if fast:
        block_ = (nd // 2, rows, D)
        f_keep, up_half, down_half = call(
            sum_half_kernel,
            [sds((2, *block_), BF), sds(block_, BF), sds(block_, BF)],
            [up_keep, up_got, down_keep, down_got],
            name="grad_half",
        )
        f_sums = call(
            sum_last_kernel,
            [sds((2, rows, D))] + [sds((2, rows, D), BF)] * (nd // 2 - 1),
            [f_keep, hop(up_half, 1, 0), hop(down_half, 0, 2)],
            name="grad_sum",
        )
        f_sum = finish_lines(f_sums)
        far_part = (far_grad[0].astype(F32) + far_got.astype(F32)).astype(BF)
        qo_own = (near_grad[0], hop(near_grad[1], 1, 0), hop(far_part, 0, 2))
    else:
        qo_own = ()
        f_sums = f_sum = sum_lines(f_grads)
    hidden_out = place(hidden_a, hidden_b)
    input_b = hop(after(input_a, hidden_out, f_sums, qo_own[1:]), 0, 2)
    small_g = lax.all_to_all(after(small_y.astype(BF), input_b), "dp", 0, 0, tiled=True).astype(F32).sum(0)
    input_grad = place(input_a, input_b)
    up_sum, down_sum = f_sum
    if fast:
        qo_sum = finish_lines(sum_blocks(qo_own))[0]
    else:
        qo_sum = sum_lines([*near_grad, *far_grad])[0]

    width = 2 * HS // nd
    if fast:
        g_qv = qo_sum[rows, : nh * width].reshape(nh, width)
        qo_sum = qo_sum[:rows]
    else:
        g_qv = [
            jnp.concatenate([g[0, :hw].reshape(nh, HS), g[0, 2 * hw : 3 * hw].reshape(nh, HS)], axis=1)
            for g in (g0_sum, g1_sum)
        ]
        g_qv = g_qv[0] + hop(g_qv[1], 0, 2)
        bit = 1
        while bit < nd:
            g_qv = g_qv + hop(g_qv, bit, 0)
            bit *= 2
        g_qv = lax.dynamic_slice(g_qv, (0, width * me), (nh, width))

    at = rows + 2 * cr + 9 + 4 * nr
    table = small_g[at : at + total] + small_g[at + total : at + 2 * total]
    logit_all = table[:, :CLASSES]
    class_bias_grad = jnp.sum(table[:, CLASSES : 2 * CLASSES], 0)
    squares = jnp.sum(table[:, 2 * CLASSES : 2 * CLASSES + 8], 0).reshape(2, 4).sum(0)
    rms = jnp.sqrt(squares / (jnp.sum(lengths).astype(F32) * D))

    at = rows + 2 * cr
    g_wide = small_g[at : at + 6, :rows]
    g_narrow = small_g[at + 6 : at + 9, :cr]
    g_ub = lax.dynamic_slice(small_g, (at + 9 + nr * m, 0), (nr, HS // nd))
    return (
        hidden_out,
        logit_all,
        input_grad,
        jnp.transpose(qo_sum[:, : 3 * hw].reshape(rows, 3, hw), (1, 0, 2)),
        g_qv,
        qo_sum[:, 3 * hw :].T,
        g_wide[0],
        g_wide[1],
        g_wide[2],
        up_sum,
        g_ub,
        down_sum.T,
        g_wide[3],
        g_wide[4],
        g_wide[5],
        small_g[:rows],
        g_narrow[0],
        g_narrow[1],
        small_g[rows : rows + cr],
        g_narrow[2],
        small_g[rows + cr : at, :CLASSES],
        class_bias_grad,
        rms,
    )


def solution(mesh):
    rows = P(None, "dp", None)
    vec = P("dp")
    return jax.shard_map(
        body,
        mesh=mesh,
        in_specs=(
            rows,
            rows,
            P(),
            P(),
            P(None, "dp", "mp"),
            P("mp", "dp"),
            P("mp", "dp"),
            vec,
            vec,
            vec,
            P("dp", "mp"),
            P("mp", "dp"),
            P("mp", "dp"),
            vec,
            vec,
            vec,
            P("dp", None),
            vec,
            vec,
            P("dp", None),
            vec,
            P("dp", None),
            P(),
        ),
        out_specs=(
            rows,
            P(),
            rows,
            P(None, "dp", "mp"),
            P("mp", "dp"),
            P("mp", "dp"),
            vec,
            vec,
            vec,
            P("dp", "mp"),
            P("mp", "dp"),
            P("mp", "dp"),
            vec,
            vec,
            vec,
            P("dp", None),
            vec,
            vec,
            P("dp", None),
            vec,
            P("dp", None),
            P(),
            P(),
        ),
        check_vma=False,
    )
```

```python
import functools

import jax
import jax.numpy as jnp
import numpy as np
from jax import lax
from jax.experimental import pallas as pl
from jax.experimental.pallas import tpu as pltpu
from jax.sharding import PartitionSpec as P

D = 768
HS = 64
CW = 128
PH = 2
CLASSES = 14
EPSILON = 1e-06
NEGATIVE = -1e30
LOG2E = 1.4426950408889634
HIGHEST = lax.Precision.HIGHEST
BF = jnp.bfloat16
F32 = jnp.float32
AXES = ("dp", "mp")
QB = 256
RB = 128
SLOW = 1
ROOM = 16


def dot(a, b, ca, cb):
    return lax.dot_general(a, b, (((ca,), (cb,)), ((), ())), preferred_element_type=F32)


def hop(x, dbit, mbit):
    nd, nm = lax.axis_size("dp"), lax.axis_size("mp")
    pairs = [(d * nm + m, (d ^ dbit) * nm + (m ^ mbit)) for d in range(nd) for m in range(nm)]
    return lax.ppermute(x, AXES, pairs)


def after(x, *others):
    return lax.optimization_barrier((x, *others))[0]


def bit_groups(nd):
    bits = []
    b = nd // 2
    while b > 1:
        bits.append(b)
        b //= 2
    groups = [bits[i : i + 2] for i in range(0, len(bits), 2)]
    out = []
    for g in groups:
        out.append([0, g[0]] if len(g) == 1 else [0, g[1], g[0], g[0] + g[1]])
    return out


def gather_chips(x):
    nd = lax.axis_size("dp")
    cur = x[None]
    for masks in bit_groups(nd):
        parts = [cur] + [hop(cur, k, 0) for k in masks[1:]]
        cur = jnp.stack(parts, 1).reshape(-1, *x.shape)
    near, far = (hop(cur, 1, 0), hop(cur, 0, 2))
    far2 = hop(cur, 1, 2)
    return (
        jnp.stack([cur, near], 1).reshape(nd, *x.shape),
        jnp.stack([far, far2], 1).reshape(nd, *x.shape),
    )


def scatter_chips(mine, other):
    nd = lax.axis_size("dp")
    tail = mine.shape[1:]
    a = mine.reshape(nd // 2, 2, *tail)
    b = other.reshape(nd // 2, 2, *tail)
    cur = (
        a[:, 0].astype(F32)
        + hop(a[:, 1], 1, 0).astype(F32)
        + hop(b[:, 0], 0, 2).astype(F32)
        + hop(b[:, 1], 1, 2).astype(F32)
    )
    for masks in reversed(bit_groups(nd)):
        low = cur.astype(BF).reshape(-1, len(masks), *tail)
        full = cur.reshape(-1, len(masks), *tail)
        cur = full[:, 0]
        for i, k in enumerate(masks[1:], 1):
            cur = cur + hop(low[:, i], k, 0).astype(F32)
    return cur[0]


def relative(x, me):
    return jnp.take(x, jnp.arange(x.shape[0], dtype=jnp.int32) ^ me, axis=0)


def split3(x):
    a = x.astype(BF)
    r = x - a.astype(F32)
    b = r.astype(BF)
    return a, b, (r - b.astype(F32)).astype(BF)


def swap64(x):
    return jnp.concatenate([x[:, 64:], x[:, :64]], axis=1)


def doubled(kp, head):
    lane = lax.broadcasted_iota(jnp.int32, kp.shape, 1)
    kr = swap64(kp)
    return jnp.where(lane < 64, kp, kr) if head == 0 else jnp.where(lane < 64, kr, kp)


ANY = pl.BlockSpec(memory_space=pl.ANY)
SMEM = pl.BlockSpec(memory_space=pltpu.SMEM)


def room(mib):
    return pltpu.CompilerParams(vmem_limit_bytes=mib << 20)


def call(kernel, outs, args, specs=None, scratch=(), name=None, flops=0, mib=ROOM):
    specs = [pl.BlockSpec(memory_space=pltpu.VMEM) if s is None else s for s in (specs or [None] * len(args))]
    size = sum(a.size * a.dtype.itemsize for a in args) + sum(
        int(np.prod(o.shape)) * np.dtype(o.dtype).itemsize for o in outs
    )
    return pl.pallas_call(
        kernel,
        in_specs=specs,
        out_specs=[pl.BlockSpec(memory_space=pltpu.VMEM)] * len(outs),
        out_shape=outs,
        scratch_shapes=list(scratch),
        cost_estimate=cost(size, flops),
        compiler_params=room(mib),
        name=name,
    )(*args)


def cost(size, flops=0):
    return pl.CostEstimate(flops=int(flops) // SLOW, bytes_accessed=int(size) // SLOW, transcendentals=0)


def sds(shape, dtype=F32):
    return jax.ShapeDtypeStruct(shape, dtype)


def by_rows(kernel, outs, sums, args, consts, info=None, name=None):
    n = args[0].shape[0]

    def cut(a):
        return pl.BlockSpec((RB, a.shape[1]), lambda i: (i, 0))

    def whole(a):
        return pl.BlockSpec(a.shape, lambda i: (0,) * len(a.shape))

    head = [] if info is None else [info]
    size = sum(a.size * a.dtype.itemsize for a in [*args, *consts])
    return pl.pallas_call(
        kernel,
        grid=(n // RB,),
        in_specs=[SMEM] * len(head) + [cut(a) for a in args] + [whole(a) for a in consts],
        out_specs=[cut(o) for o in outs] + [whole(o) for o in sums],
        out_shape=[*outs, *sums],
        cost_estimate=cost(size),
        compiler_params=room(60),
        name=name,
    )(*head, *args, *consts)


def start_sums(*refs):
    @pl.when(pl.program_id(0) == 0)
    def _():
        for r in refs:
            r[...] = jnp.zeros(r.shape, F32)


def start(copies):
    for cp in copies:
        cp.start()
    return copies


def load_pair(info, arrays, w_ref, sems):
    if len(arrays) == 1:
        return start([pltpu.make_async_copy(arrays[0].at[0], w_ref, sems.at[0])])
    nz = arrays[0].shape[1]
    rows = D // (2 * nz)
    copies = []
    for x, a in enumerate(arrays):
        for z in range(nz):
            at = pl.multiple_of((info[0] ^ (2 * z + x)) * rows, 16)
            copies.append(
                pltpu.make_async_copy(a.at[0, z, pl.ds(0, rows), :], w_ref.at[pl.ds(at, rows), :], sems.at[len(copies)])
            )
    return start(copies)


def load_rows(info, arrays, k, b_ref, sems):
    nz = arrays[0].shape[1]
    rows = D // (2 * nz)
    copies = []
    for x, a in enumerate(arrays):
        for z in range(nz):
            copies.append(
                pltpu.make_async_copy(
                    a.at[k, z, pl.ds(rows, b_ref.shape[1]), :], b_ref.at[info[0] ^ (2 * z + x)], sems.at[len(copies)]
                )
            )
    return start(copies)


def load_weight(info, arrays, k, w_ref, sems):
    if len(arrays) == 2:
        return start([pltpu.make_async_copy(a.at[k], w_ref.at[i], sems.at[i]) for i, a in enumerate(arrays)])
    nz = arrays[0].shape[1]
    rows = D // (2 * nz)
    copies = []
    for i, a in enumerate(arrays):
        for z in range(nz):
            at = pl.multiple_of((info[0] ^ (2 * z + i % 2)) * rows, 16)
            copies.append(
                pltpu.make_async_copy(
                    a.at[k, z, pl.ds(0, rows), :], w_ref.at[i // 2, pl.ds(at, rows), :], sems.at[len(copies)]
                )
            )
    return start(copies)


def wait(copies):
    for cp in copies:
        cp.wait()


def weight_scratch(arrays):
    count = len(arrays) if len(arrays) == 2 else 4 * arrays[0].shape[1]
    return [pltpu.VMEM((2, D, arrays[0].shape[-1]), BF), pltpu.SemaphoreType.DMA((count,))]


def gather_lines(local):
    k, rows, n = local.shape
    cur = local[:, None]
    *groups, last = bit_groups(lax.axis_size("dp"))
    for masks in groups:
        parts = [cur] + [hop(cur, b, 0) for b in masks[1:]]
        cur = jnp.stack(parts, 2).reshape(k, -1, rows, n)
    return [cur] + [hop(cur, b, 0) for b in last[1:]]


def gather_doubling(local, *others):
    k, rows, n = local.shape
    cur, got = local[:, None], []
    bit = lax.axis_size("dp") // 2
    while bit > 1:
        got.append(hop(cur, bit, 0))
        cur = jnp.stack([cur, got[-1]], 2).reshape(k, -1, rows, n)
        bit //= 2
    return cur, got


def join_lines(parts):
    k, _, rows, n = parts[0].shape
    return jnp.stack(parts, 2).reshape(k, -1, rows, n)


def gather_planes(cur, fast):
    near, far, far2 = hop(cur, 1, 0), hop(cur, 0, 2), hop(cur, 1, 2)
    if fast:
        return cur, near, far, far2
    me = lax.axis_index("dp")
    k, half, rows, n = cur.shape

    def ordered(a, b):
        both = jnp.stack([a, b], 2).reshape(k, 2 * half, rows, n)
        return jnp.moveaxis(relative(jnp.moveaxis(both, 1, 0), me), 0, 1).reshape(k, 2 * half * rows, n)

    return ordered(cur, near), ordered(far, far2)


def spread(info, g_ref, k, outs):
    nz = outs[0].shape[1]
    rows = D // (2 * nz)
    for z in range(nz):
        for x in range(2):
            at = pl.multiple_of((info[0] ^ (2 * z + x)) * rows, 8)
            outs[x][k, z, :rows] = g_ref[pl.ds(at, rows), :].astype(BF)


def grad_outs(k, ys, nd, rows, fast, more=0):
    return [sds((k, nd // 2, rows + more, D), BF)] * (2 * ys) if fast else [sds((k, D, D), BF)] * ys


def store_grad(info, k, y, g, g_ref, outs):
    if len(outs[0].shape) == 4:
        g_ref[...] = g
        spread(info, g_ref, k, outs[2 * y : 2 * y + 2])
    else:
        outs[y][k] = g.astype(BF)


def sum_first_kernel(count, *refs):
    parts, (keep_ref, *send_refs) = refs[:count], refs[count:]
    for k in range(parts[0].shape[0]):
        for z in range(parts[0].shape[1]):
            total = parts[0][k, z].astype(F32)
            for r in parts[1:]:
                total = total + r[k, z].astype(F32)
            if z == 0:
                keep_ref[k] = total
            else:
                send_refs[z - 1][k] = total.astype(BF)


def sum_planes(parts):
    if len(parts) == 2:
        return list(parts)
    keep, x, y, xy = parts
    return [keep, hop(x, 1, 0), hop(y, 0, 2), hop(xy, 1, 2)]


def sum_lines(parts):
    nd = lax.axis_size("dp")
    if len(parts) == 2:
        me = lax.axis_index("dp")
        k = parts[0].shape[0]
        near, far = (
            relative(jnp.moveaxis(p.reshape(k, nd, D // nd, D), 0, 1), me) for p in parts
        )
        return scatter_chips(near, far)
    return finish_lines(sum_blocks(parts))


def sum_blocks(parts):
    if len(parts) == 2:
        return parts
    k, nz, rows, n = parts[0].shape
    return call(
        functools.partial(sum_first_kernel, len(parts)),
        [sds((k, rows, n))] + [sds((k, rows, n), BF)] * (nz - 1),
        list(parts),
        name="grad_sum",
    )


def finish_lines(sums):
    own, low, *high = sums
    if len(high) != 2:
        for z, piece in enumerate([low, *high], 1):
            own = own + hop(piece, 2 * z, 0).astype(F32)
        return own
    got = hop(jnp.stack([low, high[1]]), 2, 0)
    send = (high[0].astype(F32) + got[1].astype(F32)).astype(BF)
    return own + got[0].astype(F32) + hop(send, 4, 0).astype(F32)


def bias_rows(b, first, count, low, high):
    return jnp.concatenate([b[first + i : first + i + 1, low:high] for i in range(count)], axis=1)


def block(ref, i):
    return ref[:, 128 * i : 128 * i + 128]


def attn_fwd_kernel(nh, info, own_ref, sib_ref, bias_ref, aux_ref, *rest):
    *arrays, proj_ref, w_ref, ctx_ref, lse_ref, w_sems, o_ref, b_ref, b_sems = rest
    copies = load_pair(info, arrays, w_ref, w_sems)
    hw = nh * HS
    if len(arrays) == 2:
        wait(load_rows(info, arrays, 0, b_ref, b_sems))
        nd = b_ref.shape[0]
        w = 2 * HS // nd

        def bias_part(first):
            return [b_ref[a, h : h + 1, :w] for h in range(nh) for a in range(first, first + nd // 2)]

        q_part, v_part = (
            jnp.concatenate(bias_part(a), axis=1).astype(F32) for a in (0, nd // 2)
        )
    else:
        bias = bias_ref[...].astype(F32)
        q_part = bias_rows(bias, 0, nh, 0, HS)
        v_part = bias_rows(bias, 0, nh, HS, 2 * HS)
    row_bias = jnp.concatenate([q_part, jnp.zeros((1, hw), F32), v_part, jnp.zeros((1, HS), F32)], axis=1)
    wait(copies)
    half = own_ref.shape[0]
    n = 2 * half
    for i, ref in enumerate((own_ref, sib_ref)):
        for j in range(2):
            r = slice(j * half // 2, (j + 1) * half // 2)
            out = dot(ref[r], w_ref[:, : 10 * HS], 1, 0) + row_bias
            proj_ref[i * half + r.start : i * half + r.stop] = out.astype(BF)
    qt = [jnp.transpose(block(proj_ref, i).astype(F32)) * (HS**-0.5 * LOG2E) for i in (0, 1)]
    hi = [q.astype(BF) for q in qt]
    lo = [(q - h.astype(F32)).astype(BF) for q, h in zip(qt, hi)]
    vt = [jnp.transpose(block(proj_ref, i).astype(F32)).astype(BF) for i in (3, 4)]
    row = lax.broadcasted_iota(jnp.int32, (128, QB), 0)
    auxq = jnp.where(row == 0, 1.0, 0.0).astype(BF)
    o_ref[0:HS] = jnp.zeros((HS, n), F32)
    lse_ref[...] = jnp.zeros(lse_ref.shape, F32)
    for h in range(nh):
        kb, kh = ((1, 1), (2, 0), (2, 1))[h]
        lhs = jnp.concatenate([doubled(block(proj_ref, kb), kh), aux_ref[...]], axis=1)
        i, r = h // 2, slice(64 * (h % 2), 64 * (h % 2) + 64)
        vaug = jnp.concatenate([vt[i][r], jnp.ones((16, n), BF)], axis=0)
        to = slice(64 * h + 64, 64 * h + 128)
        for b in range(n // QB):
            s = slice(b * QB, b * QB + QB)
            rhs = jnp.concatenate([hi[i][r, s], lo[i][r, s], auxq], axis=0)
            sc = dot(lhs, rhs, 1, 0)
            m = jnp.max(sc, axis=0, keepdims=True)
            p = jnp.exp2(sc - m).astype(BF)
            o = dot(vaug, p, 1, 0)
            total = o[64:65]
            o_ref[to, s] = o[:64] / total
            lse_ref[h : h + 1, s] = m + jnp.log2(total)
    for j in range(2):
        ctx_ref[:, 128 * j : 128 * j + 128] = jnp.transpose(o_ref[128 * j : 128 * j + 128]).astype(BF)


def attn_fwd(nh, info, own, sib, bias, aux, arrays):
    n = 2 * own.shape[0]
    count = len(arrays) * arrays[0].shape[1] if len(arrays) == 2 else 1
    return call(
        functools.partial(attn_fwd_kernel, nh),
        [sds((n, 10 * HS), BF), sds((D, D), BF), sds((n, 4 * HS), BF), sds((8, n))],
        [info, own, sib, bias, aux, *arrays],
        [SMEM] + [None] * 4 + [ANY] * len(arrays),
        [
            pltpu.SemaphoreType.DMA((count,)),
            pltpu.VMEM((4 * HS, n), F32),
            pltpu.VMEM((count, 16, D), BF),
            pltpu.SemaphoreType.DMA((count,)),
        ],
        "attn_fwd",
        flops=11_000_000_000,
    )


def out_kernel(first, c0_ref, c1_ref, w0_ref, w1_ref, out_ref):
    rows, cols = slice(first, first + out_ref.shape[0]), slice(8 * HS, 12 * HS)
    part = dot(c0_ref[rows], w0_ref[:, cols], 1, 1) + dot(c1_ref[rows], w1_ref[:, cols], 1, 1)
    out_ref[...] = part.astype(out_ref.dtype)


def norm(values, gain, shift):
    center = values - jnp.mean(values, -1, keepdims=True)
    spread_ = jnp.mean(center * center, -1, keepdims=True)
    scale = lax.rsqrt(spread_ + EPSILON)
    normed = center * scale
    return normed * gain + shift, normed, scale


def live_rows(aux_ref):
    return jnp.where(aux_ref[:, 0:1].astype(F32) > -1.0, 1.0, 0.0)


def square(live, v):
    return jnp.sum(jnp.sum(v * v, -1, keepdims=True) * live, axis=0, keepdims=True)


def ln1_kernel(part_ref, got_ref, tok_ref, aux_ref, wide_ref, first_ref, low_ref, n_ref, s_ref, sq_ref):
    start_sums(sq_ref)
    tok = tok_ref[...].astype(F32)
    att = part_ref[...] + got_ref[...].astype(F32) + wide_ref[0:1]
    first, normed, scale = norm(tok + att, wide_ref[1:2], wide_ref[2:3])
    first_ref[...] = first
    low_ref[...] = first.astype(BF)
    n_ref[...] = normed
    s_ref[...] = scale
    live = live_rows(aux_ref)
    lane = lax.broadcasted_iota(jnp.int32, (1, 128), 1)
    out = jnp.zeros((1, 128), F32)
    for i, v in enumerate((tok, att, first)):
        out = jnp.where(lane == i, square(live, v), out)
    sq_ref[...] += out


def hidden_bias(b_ref, nr):
    nd = b_ref.shape[0]
    w = HS // nd
    first = jnp.concatenate([b_ref[a, 0:1, :128] for a in range(nd)], axis=0)
    i = lax.broadcasted_iota(jnp.int32, (128, nr * HS), 0)
    f = lax.broadcasted_iota(jnp.int32, (128, nr * HS), 1)
    place = jnp.where(i == (f // HS) * w + f % w, 1.0, 0.0).astype(BF)
    spread_ = dot(first, place, 1, 0)
    a = lax.broadcasted_iota(jnp.int32, (nd, nr * HS), 0)
    f = lax.broadcasted_iota(jnp.int32, (nd, nr * HS), 1)
    return jnp.sum(jnp.where((f % HS) // w == a, spread_, 0.0), axis=0, keepdims=True)


def ffn_up_kernel(nh, nr, info, x_ref, b0_ref, b1_ref, *rest):
    *up, act_ref, slope_ref, up_ref, sems, r0_ref, r1_ref, r_sems = rest
    copies = load_weight(info, up, 0, up_ref, sems)
    fw = nr * HS
    x = x_ref[...]
    if len(up) == 4:
        for i, r_ref in enumerate((r0_ref, r1_ref)):
            wait(load_rows(info, up[2 * i : 2 * i + 2], 0, r_ref, r_sems))
        biases = [hidden_bias(r_ref, nr) for r_ref in (r0_ref, r1_ref)]
    else:
        biases = [bias_rows(b_ref[...].astype(F32), nh, nr, 0, HS) for b_ref in (b0_ref, b1_ref)]
    wait(copies)
    for y in range(2):
        for j in range(fw // 256):
            s = slice(j * 256, (j + 1) * 256)
            t = slice(y * fw + j * 256, y * fw + (j + 1) * 256)
            pre = dot(x, up_ref[y, :, s], 1, 0) + biases[y][:, s]
            phi = 0.5 + 0.5 * lax.erf(pre * (0.5**0.5))
            act_ref[:, t] = (pre * phi).astype(BF)
            slope_ref[:, t] = (phi + pre * (jnp.exp(-0.5 * pre * pre) * (2 * np.pi) ** -0.5)).astype(BF)


def product_kernel(k, info, a_ref, *rest):
    *w, out_ref, w_ref, sems = rest
    wait(load_weight(info, w, k, w_ref, sems))
    fw = w_ref.shape[2]
    out_ref[...] = (dot(a_ref[:, :fw], w_ref[0], 1, 1) + dot(a_ref[:, fw:], w_ref[1], 1, 1)).astype(out_ref.dtype)


def head_ones():
    a = lax.broadcasted_iota(jnp.int32, (CW, CW), 0) // (CW // PH)
    b = lax.broadcasted_iota(jnp.int32, (CW, CW), 1) // (CW // PH)
    return jnp.where(a == b, 1.0, 0.0)


def fdot(a, b, ca=1, cb=0):
    return lax.dot_general(a, b, (((ca,), (cb,)), ((), ())), precision=HIGHEST, preferred_element_type=F32)


def ln2_kernel(
    part_ref, got_ref, first_ref, aux_ref, wide_ref, narrow_ref, sw_ref, low_ref, n_ref, s_ref, st_ref, lg_ref, stat_ref
):
    feed = part_ref[...] + got_ref[...].astype(F32) + wide_ref[3:4]
    second, normed, scale = norm(first_ref[...] + feed, wide_ref[4:5], wide_ref[5:6])
    low = second.astype(BF)
    low_ref[...] = low
    n_ref[...] = normed
    s_ref[...] = scale
    student = dot(low, sw_ref[...], 1, 0) + narrow_ref[0:1]
    st_ref[...] = student
    live = live_rows(aux_ref)
    logit = fdot(student * narrow_ref[1:2], head_ones()) * (CW // PH) ** -0.5
    logit = jnp.where(live > 0.0, logit, NEGATIVE)
    lg_ref[...] = logit

    @pl.when(pl.program_id(0) == 0)
    def _():
        stat_ref[...] = jnp.zeros((8, 128), F32)
        stat_ref[0:1] = jnp.full((1, 128), NEGATIVE, F32)

    old = stat_ref[0:1]
    top = jnp.maximum(old, jnp.max(logit, axis=0, keepdims=True))
    shrink = jnp.exp(old - top)
    weight = jnp.where(live > 0.0, jnp.exp(logit - top), 0.0)
    stat_ref[0:1] = top
    stat_ref[1:2] = stat_ref[1:2] * shrink + jnp.sum(weight, axis=0, keepdims=True)
    stat_ref[2:3] = stat_ref[2:3] * shrink + jnp.sum(weight * student, axis=0, keepdims=True)
    stat_ref[3:4] += jnp.broadcast_to(square(live, feed), (1, 128))


def norm_back(up, normed, scale, gain):
    scaled = up * gain
    inner = scaled - jnp.mean(scaled, -1, keepdims=True) - normed * jnp.mean(scaled * normed, -1, keepdims=True)
    return inner * scale


def colsum(x):
    return jnp.sum(x, axis=0, keepdims=True)


def head_kernel(
    info,
    st_ref,
    lg_ref,
    low_ref,
    cot_ref,
    n_ref,
    s_ref,
    stat_ref,
    sib_ref,
    sq_ref,
    pooler_ref,
    class_ref,
    cb_ref,
    narrow_ref,
    sw_ref,
    wide_ref,
    dr2_ref,
    dffn_ref,
    gst_ref,
    gpool_ref,
    gclass_ref,
    rep_ref,
    vec_ref,
    nvec_ref,
    keep_ref,
):
    scale = (CW // PH) ** -0.5
    once = jnp.where(info[1] == 0, 1.0, 0.0)

    @pl.when(pl.program_id(0) == 0)
    def _():
        top, top2 = stat_ref[0:1], sib_ref[0:1]
        best = jnp.maximum(top, top2)
        fa, fb = jnp.exp(top - best), jnp.exp(top2 - best)
        whole = stat_ref[1:2] * fa + sib_ref[1:2] * fb
        pooled = (stat_ref[2:3] * fa + sib_ref[2:3] * fb) / whole
        pooled = jnp.broadcast_to(pooled, (8, CW))
        z = jnp.tanh(fdot(pooled, pooler_ref[...]) + narrow_ref[2:3])
        lane = lax.broadcasted_iota(jnp.int32, (8, 128), 1)
        row = lax.broadcasted_iota(jnp.int32, (8, 128), 0)
        logit = fdot(z, class_ref[...]) + cb_ref[...]
        masked = jnp.where(lane < CLASSES, logit, NEGATIVE)
        e = jnp.exp(masked - jnp.max(masked, axis=1, keepdims=True))
        dlogit = e / jnp.sum(e, axis=1, keepdims=True) - jnp.where(lane == info[3], 1.0, 0.0)
        only = jnp.where(row == 0, once, 0.0)
        gclass_ref[...] = fdot(z * only, dlogit, 0, 0)
        dz = fdot(dlogit, class_ref[...], 1, 1)
        dzp = dz * (1.0 - z * z)
        gpool_ref[...] = fdot(pooled * only, dzp, 0, 0)
        dpooled = fdot(dzp, pooler_ref[...], 1, 1)
        sq = jnp.where(lane[0:1] == 3, stat_ref[3:4] + sib_ref[3:4] * 0.0, sq_ref[...])
        sq = jnp.where(info[1] == 0, pltpu.roll(sq, 2 * CLASSES, 1), pltpu.roll(sq, 2 * CLASSES + 4, 1))
        rep = jnp.where(lane < CLASSES, logit, pltpu.roll(jnp.where(lane < CLASSES, dlogit, 0.0), CLASSES, 1)) * once
        rep_ref[...] = jnp.where(lane < 2 * CLASSES, rep, sq)
        nvec_ref[...] = jnp.zeros((8, CW), F32)
        nvec_ref[2:3] = dzp[0:1] * once
        vec_ref[...] = jnp.zeros((8, D), F32)
        gst_ref[...] = jnp.zeros((D, CW), F32)
        keep_ref[0:1] = best
        keep_ref[1:2] = whole
        keep_ref[2:3] = dpooled[0:1]
        keep_ref[3:4] = fdot(pooled * dpooled, head_ones())[0:1]

    student = st_ref[...]
    dp = keep_ref[2:3]
    logit = lg_ref[...]
    weight = jnp.where(logit > 0.5 * NEGATIVE, jnp.exp(logit - keep_ref[0:1]), 0.0) / keep_ref[1:2]
    dq = scale * weight * (fdot(student * dp, head_ones()) - keep_ref[3:4])
    dstudent = (weight * dp + dq * narrow_ref[1:2]).astype(BF)
    nvec_ref[0:1] += colsum(dstudent.astype(F32))
    nvec_ref[1:2] += colsum(dq * student)
    gst_ref[...] += dot(low_ref[...], dstudent, 0, 0)
    dsecond = dot(dstudent, sw_ref[...], 1, 1) + cot_ref[...].astype(F32)
    normed = n_ref[...]
    dr2 = norm_back(dsecond, normed, s_ref[...], wide_ref[4:5])
    dr2_ref[...] = dr2
    dffn_ref[...] = dr2.astype(BF)
    vec_ref[0:1] += colsum(dr2)
    vec_ref[1:2] += colsum(dsecond * normed)
    vec_ref[2:3] += colsum(dsecond)


def ffn_back_kernel(info, g_ref, slope_ref, *rest):
    *down, dpre_ref, ub_ref, w_ref, sems = rest
    copies = load_weight(info, down, 1, w_ref, sems)
    fw = w_ref.shape[2]
    g = g_ref[...]
    ub_ref[...] = jnp.zeros(ub_ref.shape, F32)
    wait(copies)
    for y in range(2):
        for j in range(fw // 256):
            s = slice(j * 256, (j + 1) * 256)
            t = slice(y * fw + j * 256, y * fw + (j + 1) * 256)
            dpre = (dot(g, w_ref[y, :, s], 1, 0) * slope_ref[:, t].astype(F32)).astype(BF)
            dpre_ref[:, t] = dpre
            ub_ref[0:1, t] = colsum(dpre.astype(F32))


def ffn_grad_kernel(info, first, first2, dpre, dpre2, dffn, dffn2, act, act2, *rest):
    *outs, g_ref = rest
    fw = dpre.shape[1] // 2
    for k, (a0, a1, b0, b1) in enumerate(((first, first2, dpre, dpre2), (dffn, dffn2, act, act2))):
        for y in range(2):
            s = slice(y * fw, (y + 1) * fw)
            g = dot(a0[...], b0[:, s], 0, 0) + dot(a1[...], b1[:, s], 0, 0)
            if len(outs) == 2:
                outs[y][k] = g.astype(BF)
                continue
            g_ref[...] = g
            nz = outs[0].shape[1]
            rows = D // (2 * nz)
            for z in range(nz):
                for x in range(2):
                    at = pl.multiple_of((info[0] ^ (2 * z + x)) * rows, 8)
                    piece = g_ref[pl.ds(at, rows), :].astype(BF)
                    if k == 0:
                        outs[y][x, z] = piece
                    else:
                        outs[2 + x][y, z] = piece


def sum_half_kernel(a_ref, ga_ref, b_ref, gb_ref, keep_ref, sa_ref, sb_ref):
    for k, (r, g, send_ref) in enumerate(((a_ref, ga_ref, sa_ref), (b_ref, gb_ref, sb_ref))):
        for z in range(r.shape[1]):
            keep_ref[k, z] = (r[0, z].astype(F32) + g[0, z].astype(F32)).astype(BF)
            send_ref[z] = (r[1, z].astype(F32) + g[1, z].astype(F32)).astype(BF)


def sum_last_kernel(keep_ref, a_ref, b_ref, own_ref, *send_refs):
    for k, g in enumerate((a_ref, b_ref)):
        for z in range(keep_ref.shape[1]):
            total = keep_ref[k, z].astype(F32) + g[z].astype(F32)
            if z == 0:
                own_ref[k] = total
            else:
                send_refs[z - 1][k] = total.astype(BF)


def ln1_back_kernel(part_ref, got_ref, dr2_ref, n_ref, s_ref, wide_ref, dr1_ref, low_ref, vec_ref):
    start_sums(vec_ref)
    up = part_ref[...] + got_ref[...].astype(F32) + dr2_ref[...]
    normed = n_ref[...]
    dr1 = norm_back(up, normed, s_ref[...], wide_ref[1:2])
    dr1_ref[...] = dr1
    low_ref[...] = dr1.astype(BF)
    vec_ref[0:1] += colsum(dr1)
    vec_ref[1:2] += colsum(up * normed)
    vec_ref[2:3] += colsum(up)


def attn_bwd_kernel(nh, proj_ref, w_ref, aux_ref, ctx_ref, da_ref, db_ref, lse_ref, out_ref, sum_ref, do_ref, dqt_ref):
    n = proj_ref.shape[0]
    half = n // 2
    scale = HS**-0.5
    cols = slice(8 * HS, 12 * HS)
    for i, ref in enumerate((da_ref, db_ref)):
        do_ref[i * half : (i + 1) * half] = dot(ref[...], w_ref[:, cols], 1, 0).astype(BF)
    qb = [block(proj_ref, i) for i in (0, 1)]
    qt = [jnp.transpose(q.astype(F32)) * (scale * LOG2E) for q in qb]
    hi = [q.astype(BF) for q in qt]
    lo = [(q - h.astype(F32)).astype(BF) for q, h in zip(qt, hi)]
    kt = [jnp.transpose(block(proj_ref, i).astype(F32)).astype(BF) for i in (1, 2)]
    dob = [block(do_ref, i) for i in (0, 1)]
    dot_f = [jnp.transpose(d.astype(F32)) for d in dob]
    dot_b = [d.astype(BF) for d in dot_f]
    prod = [d * jnp.transpose(block(ctx_ref, i).astype(F32)) for i, d in enumerate(dot_f)]
    lane = lax.broadcasted_iota(jnp.int32, (n, 128), 1)
    row = lax.broadcasted_iota(jnp.int32, (128, QB), 0)
    zero = jnp.zeros((64, QB), BF)
    empty = jnp.zeros((n, 128), BF)
    dqt_ref[...] = jnp.zeros(dqt_ref.shape, F32)
    dk, dv = [], []
    for h in range(nh):
        kb, kh = ((1, 1), (2, 0), (2, 1))[h]
        i, ih = h // 2, h % 2
        vi, vh = ((3, 0), (3, 1), (4, 0))[h]
        oi, oh = ((0, 1), (1, 0), (1, 1))[h]
        lhs = jnp.concatenate([doubled(block(proj_ref, kb), kh), aux_ref[...]], axis=1)
        lhs_v = jnp.concatenate([block(proj_ref, vi), aux_ref[...]], axis=1)
        r = slice(64 * ih, 64 * ih + 64)
        ro = slice(64 * oh, 64 * oh + 64)
        rk = slice(64 * kh, 64 * kh + 64)
        qm = jnp.where((lane < 64) == (ih == 0), qb[i], empty)
        dom = jnp.where((lane < 64) == (oh == 0), dob[oi], empty)
        dsum = jnp.sum(prod[oi][ro], axis=0, keepdims=True)
        l1, l2, l3 = split3(-lse_ref[h : h + 1, :])
        d1, d2, d3 = split3(-dsum)
        dkh = jnp.zeros((n, 128), F32)
        dvh = jnp.zeros((n, 128), F32)
        for b in range(n // QB):
            s = slice(b * QB, b * QB + QB)

            def pieces(first, x1, x2, x3):
                z = jnp.where(row == 1, x1[:, s].astype(F32), jnp.where(row == 0, first, 0.0))
                z = jnp.where(row == 2, x2[:, s].astype(F32), z)
                return jnp.where(row == 3, x3[:, s].astype(F32), z).astype(BF)

            rhs = jnp.concatenate([hi[i][r, s], lo[i][r, s], pieces(1.0, l1, l2, l3)], axis=0)
            p = jnp.exp2(dot(lhs, rhs, 1, 0))
            g = dot_b[oi][ro, s]
            part = [g, zero] if vh == 0 else [zero, g]
            rhs_v = jnp.concatenate(part + [pieces(0.0, d1, d2, d3)], axis=0)
            ds = (p * dot(lhs_v, rhs_v, 1, 0)).astype(BF)
            dvh = dvh + dot(p.astype(BF), dom[s], 1, 0)
            dkh = dkh + dot(ds, qm[s], 1, 0)
            dqt_ref[64 * h : 64 * h + 64, s] = dot(kt[kb - 1][rk], ds, 1, 0)
        dk.append(dkh * scale)
        dv.append(dvh)

    def put(i, x):
        out_ref[:, 128 * i : 128 * i + 128] = x.astype(BF)
        sum_ref[:, 128 * i : 128 * i + 128] = jnp.broadcast_to(colsum(x.astype(BF).astype(F32)), (8, 128))

    left = lane < 64
    put(0, jnp.transpose(dqt_ref[0:128] * scale))
    put(1, jnp.where(left, jnp.transpose(dqt_ref[128:256] * scale), swap64(dk[0])))
    put(2, jnp.where(left, swap64(dk[1]), swap64(dk[2])))
    put(3, jnp.where(left, swap64(dv[0]), swap64(dv[1])))
    put(4, jnp.where(left, swap64(dv[2]), 0.0))


def attn_bwd(nh, proj, w, aux, ctx, da, db, lse):
    n = proj.shape[0]
    return call(
        functools.partial(attn_bwd_kernel, nh),
        [sds((n, 10 * HS), BF), sds((8, 10 * HS))],
        [proj, w, aux, ctx, da, db, lse],
        None,
        [pltpu.VMEM((n, 4 * HS), BF), pltpu.VMEM((4 * HS, n), F32)],
        "attn_bwd",
        flops=11_000_000_000,
    )


def token_grad_kernel(g0_ref, g1_ref, w0_ref, w1_ref, dr1_ref, send_ref, own_ref):
    n = g0_ref.shape[0]
    half = n // 2
    cols = slice(0, 10 * HS)
    for out_ref, s in ((send_ref, slice(half, n)), (own_ref, slice(0, half))):
        part = dot(g0_ref[s], w0_ref[:, cols], 1, 1) + dot(g1_ref[s], w1_ref[:, cols], 1, 1)
        if out_ref is own_ref:
            part = part + dr1_ref[...]
        out_ref[...] = part.astype(out_ref.dtype)


def qkv_grad_kernel(nh, info, x0, x1, g_in, da, db, ctx_ref, sum_ref, *rest):
    *outs, g_ref, t_ref = rest
    half = x0.shape[0]
    g = dot(x0[...], g_in[:half], 0, 0) + dot(x1[...], g_in[half:], 0, 0)
    o = dot(da[...], ctx_ref[:half], 0, 0) + dot(db[...], ctx_ref[half:], 0, 0)
    g = jnp.concatenate([g[:, : 8 * HS], g[:, 8 * HS :] + o[:, : 2 * HS], o[:, 2 * HS :]], axis=1)
    store_grad(info, 0, 0, g, g_ref, outs)
    if len(outs) == 2:
        nz = outs[0].shape[1]
        rows = D // (2 * nz)
        piece = HS // nz
        zero = jnp.zeros((1, 128 - nh * piece), F32)
        for a in range(2 * nz):
            base = (a % nz) * piece + (a // nz) * 2 * nh * HS
            cuts = [sum_ref[0:1, base + h * HS : base + h * HS + piece] for h in range(nh)]
            t_ref[a : a + 1] = jnp.concatenate([*cuts, zero], axis=1)
        for z in range(nz):
            for x in range(2):
                outs[x][0, z, rows:] = jnp.zeros((outs[x].shape[2] - rows, D), BF)
                row = t_ref[pl.ds(info[0] ^ (2 * z + x), 1), :]
                outs[x][0, z, rows : rows + 8, :128] = jnp.broadcast_to(row, (8, 128)).astype(BF)


def place_kernel(info, a_ref, b_ref, c_ref, d_ref, out_ref):
    c, y = info[1], info[2]
    out_ref[0, y, c] = a_ref[0]
    out_ref[0, 1 - y, c] = b_ref[0]
    out_ref[0, y, 1 - c] = c_ref[0]
    out_ref[0, 1 - y, 1 - c] = d_ref[0]


def lanes(x):
    x = x.reshape(1, -1) if x.ndim == 1 else x
    return jnp.pad(x, ((0, 0), (0, 128 - x.shape[1])))


def vectors_kernel(sizes, info, a0, a1, wide_ref, narrow_ref, b_ref, sems):
    rows, cr, nh, _ = sizes
    wait(load_rows(info, [a0, a1], 0, b_ref, sems))
    nd = b_ref.shape[0]
    for out_ref, row, count, width in ((wide_ref, nh, 6, rows), (narrow_ref, nh + 6, 3, cr)):
        out_ref[...] = jnp.zeros(out_ref.shape, F32)
        for i in range(count):
            cuts = [b_ref[a, row + i : row + i + 1, :width] for a in range(nd)]
            out_ref[i : i + 1] = jnp.concatenate(cuts, axis=1).astype(F32)


def matrices_kernel(info, a0, a1, sw_ref, pooler_ref, class_ref, b_ref, c_ref, sems):
    copies = load_rows(info, [a0, a1], 0, b_ref, sems.at[0])
    copies += load_rows(info, [a0, a1], 1, c_ref, sems.at[1])
    wait(copies)
    for a in range(b_ref.shape[0]):
        for i in range(2):
            at = slice(16 * a + 8 * i, 16 * a + 8 * i + 8)
            pooler_ref[at] = b_ref[a, 8:16, 128 * i : 128 * i + 128].astype(F32)
            class_ref[at] = b_ref[a, 8:16, 256 + 128 * i : 384 + 128 * i].astype(F32)
        for i in range(6):
            at = 96 * a + 16 * i
            sw_ref[at : at + 16] = c_ref[a, :, 128 * i : 128 * i + 128]


def unpack_kernel(sizes, in_ref, sw_ref, pooler_ref, class_ref, wide_ref, narrow_ref, bias_ref):
    rows, cr, nh, nr = sizes
    nd = in_ref.shape[0]
    blocks = [in_ref[d].astype(F32) for d in range(nd)]
    at = rows + 2 * cr

    def joined(first, count, width):
        return jnp.concatenate([b[first : first + count, :width] for b in blocks], axis=1)

    sw_ref[...] = jnp.concatenate([b[:rows] for b in blocks], axis=0).astype(BF)
    pooler_ref[...] = jnp.concatenate([b[rows : rows + cr] for b in blocks], axis=0)
    class_ref[...] = jnp.concatenate([b[rows + cr : at] for b in blocks], axis=0)
    wide_ref[...] = jnp.zeros(wide_ref.shape, F32)
    wide_ref[0:6] = joined(at, 6, rows)
    narrow_ref[...] = jnp.zeros(narrow_ref.shape, F32)
    narrow_ref[0:3] = joined(at + 6, 3, cr)
    bias_ref[...] = jnp.zeros(bias_ref.shape, F32)
    bias_ref[0:nh, :] = joined(at + 9, nh, 2 * HS // nd)
    bias_ref[nh : nh + nr, :HS] = joined(at + 9 + nh, nr, HS // nd)


def pack_grads_kernel(sizes, info, gst, gpool, gclass, v1, v2, nv, ub0, ub1, rep, out_ref):
    rows, cr, nh, nr = sizes
    nd = out_ref.shape[0]
    fw = nr * HS
    me = info[2] * 2 + info[1]
    ub = ub0[0:1] + ub1[0:1]
    pair = [
        jnp.concatenate([ub[:, y * fw + r * HS : y * fw + (r + 1) * HS] for r in range(nr)], axis=0) for y in range(2)
    ]
    quads = jnp.concatenate(
        [jnp.where(me == q, pair[0], jnp.where((me ^ 2) == q, pair[1], 0.0)) for q in range(4)], axis=0
    )
    wide = jnp.concatenate([v1[0:1], v1[1:2], v1[2:3], v2[0:1], v2[1:2], v2[2:3]], axis=0)

    def wider(x):
        return jnp.concatenate([x, jnp.zeros((x.shape[0], 128 - x.shape[1]), F32)], axis=1)

    total = 2 * nd
    row = lax.broadcasted_iota(jnp.int32, (total, 128), 0)
    high = rep[0:1].astype(BF).astype(F32)
    mine = row == 2 * info[0] + info[2]
    table = [jnp.where(mine, high, 0.0), jnp.where(mine, rep[0:1] - high, 0.0)]
    hs = HS // nd
    for d in range(nd):
        parts = [
            gst[d * rows : (d + 1) * rows],
            gpool[d * cr : (d + 1) * cr],
            gclass[d * cr : (d + 1) * cr],
            wider(wide[:, d * rows : (d + 1) * rows]),
            wider(nv[0:3, d * cr : (d + 1) * cr]),
            wider(quads[:, d * hs : (d + 1) * hs]),
            *table,
        ]
        parts = jnp.concatenate(parts, axis=0)
        out_ref[d, : parts.shape[0]] = parts
        if parts.shape[0] < out_ref.shape[1]:
            out_ref[d, parts.shape[0] :] = jnp.zeros((out_ref.shape[1] - parts.shape[0], 128), F32)


def body(
    hidden_in,
    cotangent,
    lengths,
    labels,
    qkv_weight,
    qv_bias,
    out_weight,
    out_bias,
    norm1_gain,
    norm1_bias,
    up_weight,
    up_bias,
    down_weight,
    down_bias,
    norm2_gain,
    norm2_bias,
    student_weight,
    student_bias,
    pool_query,
    pooler_weight,
    pooler_bias,
    class_weight,
    class_bias,
):
    nd = lax.axis_size("dp")
    me = lax.axis_index("dp")
    m = lax.axis_index("mp")
    c, y = m % 2, m // 2
    total, pd, _ = hidden_in.shape
    assert total == 2 * nd and lax.axis_size("mp") == 4
    hp = pd // 2
    half = nd * hp
    rows, cr = D // nd, CW // nd
    nh, nr = qv_bias.shape[0], up_bias.shape[0]
    hw, fw = nh * HS, nr * HS
    fast = nd == 8
    sizes = (rows, cr, nh, nr)
    seq = 2 * me + y
    length = lengths[seq]
    info = jnp.stack([me, c, y, labels[seq]]).astype(jnp.int32)

    def deal(x):
        x = x.reshape(nd, 2, 2, hp, D)
        x = lax.dynamic_slice(x, (0, y, c, 0, 0), (nd, 1, 1, hp, D)).reshape(nd, hp, D)
        return lax.all_to_all(x, "dp", 0, 0, tiled=True).reshape(half, D)

    def undeal(x):
        return lax.all_to_all(x.reshape(nd, hp, D), "dp", 0, 0, tiled=True)

    def place(a, b):
        one = pl.BlockSpec((1, hp, D), lambda d: (d, 0, 0))
        out = pl.pallas_call(
            place_kernel,
            grid=(nd,),
            in_specs=[SMEM] + [one] * 4,
            out_specs=pl.BlockSpec((1, 2, 2, hp, D), lambda d: (d, 0, 0, 0, 0)),
            out_shape=sds((nd, 2, 2, hp, D), BF),
            cost_estimate=cost(6_000_000),
            compiler_params=room(8),
            name="place",
        )(info, a, b, hop(a, 0, 1), hop(b, 0, 1))
        return out.reshape(total, pd, D)

    qo = jnp.concatenate([jnp.transpose(qkv_weight, (1, 0, 2)).reshape(rows, 3 * hw), out_weight.T], axis=1)
    if fast:
        vectors = [qv_bias]
        vectors += [v[None] for v in (out_bias, norm1_gain, norm1_bias, down_bias, norm2_gain, norm2_bias)]
        vectors += [v[None] for v in (student_bias, pool_query, pooler_bias)]
        vectors = [jnp.pad(v, ((0, 0), (0, 128 - v.shape[1]))) for v in vectors]
        vectors = jnp.concatenate([*vectors, jnp.zeros((7 - nh, 128), BF)], axis=0)
        qo = jnp.concatenate([qo, jnp.pad(vectors, ((0, 0), (0, D - 128)))], axis=0)
    qo_got = gather_lines(qo[None])
    qo_line = join_lines(qo_got)
    tokens = deal(after(hidden_in, qo_got[1:]))
    w_qo = gather_planes(qo_line, fast)
    w_qo = (w_qo[:2], w_qo[2:]) if fast else (w_qo[:1], w_qo[1:])
    up_pack, down_pack = up_weight, down_weight.T
    if fast:
        row = jnp.pad(up_bias.reshape(1, -1), ((0, 7), (0, D - up_bias.size)))
        cls = lanes(class_weight)
        more = jnp.concatenate([pooler_weight[:8], pooler_weight[8:], cls[:8], cls[8:]], axis=1)
        more = jnp.pad(more, ((0, 0), (0, D - 512)))
        up_pack = jnp.concatenate([up_pack, row, more], axis=0)
        more = jnp.concatenate([student_weight[16 * i : 16 * i + 16] for i in range(6)], axis=1)
        down_pack = jnp.concatenate([down_pack, more], axis=0)
    f_line, f_got = gather_doubling(after(jnp.stack([up_pack, down_pack]), qo_got[1:]))
    class_b = lanes(class_bias.astype(F32))
    cot = deal(after(cotangent, f_got))

    index = jnp.arange(half, dtype=jnp.int32)
    position = (index // hp) * pd + index % hp
    position = jnp.concatenate([position + c * hp, position + (1 - c) * hp])
    col = jnp.arange(128, dtype=jnp.int32)[None, :]
    aux = jnp.where(
        col == 0, jnp.where(position < length, 0.0, NEGATIVE)[:, None], jnp.where(col <= 3, 1.0, 0.0)
    ).astype(BF)
    aux_own = aux[:half]

    sib = hop(after(tokens, w_qo, f_got[0]), 0, 1)
    n = 2 * half
    biases = [aux, aux]
    if not fast:
        piece = jnp.broadcast_to(qv_bias[None], (nd, *qv_bias.shape))
        piece = lax.all_to_all(piece, "dp", 0, 0, tiled=True)
        piece = jnp.transpose(piece, (1, 0, 2)).reshape(nh, 2 * HS)
        piece = jnp.pad(piece, ((0, 16 - nh), (0, 0)))
        biases = [piece, hop(piece, 0, 2)]
    proj0, w0, ctx0, lse0 = attn_fwd(nh, info, tokens, sib, biases[0], aux, w_qo[0])
    if fast:
        wide, narrow = call(
            functools.partial(vectors_kernel, sizes),
            [sds((8, D)), sds((8, CW))],
            [info, *w_qo[0]],
            [SMEM, ANY, ANY],
            [pltpu.VMEM((nd, 16, D), BF), pltpu.SemaphoreType.DMA((nd,))],
            "vectors",
        )
        bias_near = bias_far = aux
    else:
        small = jnp.concatenate(
            [student_weight, pooler_weight]
            + [
                lanes(v)
                for v in (
                    class_weight,
                    out_bias,
                    norm1_gain,
                    norm1_bias,
                    down_bias,
                    norm2_gain,
                    norm2_bias,
                    student_bias,
                    pool_query,
                    pooler_bias,
                    qv_bias,
                    up_bias,
                )
            ],
            axis=0,
        )
        small = jnp.pad(small, ((0, -small.shape[0] % 16), (0, 0)))
        small = lax.all_to_all(jnp.broadcast_to(small[None], (nd, *small.shape)), "dp", 0, 0, tiled=True)
        student_w, pooler_f, class_f, wide, narrow, bias_near = call(
            functools.partial(unpack_kernel, sizes),
            [sds((D, CW), BF), sds((CW, CW)), sds((CW, CW)), sds((8, D)), sds((8, CW)), sds((16, 128))],
            [small],
            name="unpack",
        )
        bias_near = bias_near.astype(BF)
        bias_far = hop(bias_near, 0, 2)
    proj1, w1, ctx1, lse1 = attn_fwd(nh, info, tokens, sib, biases[1], after(aux, ctx0), w_qo[1])
    w_ffn = gather_planes(f_line, fast)

    if fast:
            ctx1 = after(ctx1, wide)

    def out(first, kind):
        return call(
            functools.partial(out_kernel, first), [sds((half, D), kind)], [ctx0, ctx1, w0, w1], name="out"
        )[0]

    att_got = hop(out(half, BF), 0, 1)
    att_part = out(0, F32)
    first, first_low, n1, s1, sq1 = by_rows(
        ln1_kernel,
        [sds((half, D)), sds((half, D), BF), sds((half, D)), sds((half, 1))],
        [sds((1, 128))],
        [att_part, att_got, tokens, aux_own],
        [wide],
        name="ln1",
    )
    first_sib = hop(after(first_low, w_ffn, cot), 0, 1)

    if fast:
        student_w, pooler_f, class_f = call(
            matrices_kernel,
            [sds((D, CW), BF), sds((CW, CW)), sds((CW, CW))],
            [info, *w_ffn[:2]],
            [SMEM, ANY, ANY],
            [pltpu.VMEM((nd, 16, D), BF)] * 2 + [pltpu.SemaphoreType.DMA((2, nd))],
            "matrices",
        )

    def ffn_up(x):
        return call(
            functools.partial(ffn_up_kernel, nh, nr),
            [sds((half, 2 * fw), BF), sds((half, 2 * fw), BF)],
            [info, x, bias_near, bias_far, *w_ffn],
            [SMEM] + [None] * 3 + [ANY] * len(w_ffn),
            weight_scratch(w_ffn)
            + [pltpu.VMEM((max(nd, 8), 8, D), BF)] * 2
            + [pltpu.SemaphoreType.DMA((nd,))],
            "ffn_up",
        )

    def product(a, k, kind):
        return call(
            functools.partial(product_kernel, k),
            [sds((half, D), kind)],
            [info, a, *w_ffn],
            [SMEM, None] + [ANY] * len(w_ffn),
            weight_scratch(w_ffn),
            "product",
        )[0]

    act, slope = ffn_up(first_low)
    act_sib, slope_sib = ffn_up(after(first_sib, act))
    ffn_got = hop(product(act_sib, 1, BF), 0, 1)
    ffn_part = product(act, 1, F32)
    second_low, n2, s2, student, pool_logit, stat = by_rows(
        ln2_kernel,
        [sds((half, D), BF), sds((half, D)), sds((half, 1)), sds((half, CW)), sds((half, CW))],
        [sds((8, 128))],
        [ffn_part, ffn_got, first, aux_own],
        [wide, narrow, student_w],
        name="ln2",
    )
    hidden_a = undeal(second_low)
    hidden_b = hop(hidden_a, 0, 2)

    dr2, dffn, g_st, g_pool, g_class, report, vec2, nvec, _ = by_rows(
        head_kernel,
        [sds((half, D)), sds((half, D), BF)],
        [
            sds((D, CW)),
            sds((CW, CW)),
            sds((CW, CW)),
            sds((8, 128)),
            sds((8, D)),
            sds((8, CW)),
            sds((8, 128)),
        ],
        [student, pool_logit, second_low, cot, n2, s2],
        [stat, hop(stat, 0, 1), sq1, pooler_f, class_f, class_b, narrow, student_w, wide],
        info,
        "head",
    )
    dffn_sib = hop(dffn, 0, 1)

    def ffn_back(g, s):
        return call(
            ffn_back_kernel,
            [sds((half, 2 * fw), BF), sds((8, 2 * fw))],
            [info, g, s, *w_ffn],
            [SMEM, None, None] + [ANY] * len(w_ffn),
            weight_scratch(w_ffn),
            "ffn_back",
        )

    dpre, ub0 = ffn_back(dffn, slope)
    dpre_sib, ub1 = ffn_back(after(dffn_sib, dpre, hidden_a), slope_sib)
    dfirst_got = hop(product(dpre_sib, 0, BF), 0, 1)
    dfirst_part = product(dpre, 0, F32)
    f_grads = call(
        ffn_grad_kernel,
        grad_outs(2, 2, nd, rows, fast),
        [info, first_low, first_sib, dpre, dpre_sib, dffn, dffn_sib, act, act_sib],
        [SMEM] + [None] * 8,
        [pltpu.VMEM((D, D), F32)],
        "ffn_grad",
    )
    dr1, dattn, vec1 = by_rows(
        ln1_back_kernel,
        [sds((half, D)), sds((half, D), BF)],
        [sds((8, D))],
        [dfirst_part, dfirst_got, after(dr2, hidden_b), n1, s1],
        [wide],
        name="ln1_back",
    )
    dattn_sib = hop(dattn, 0, 1)
    dattn_sib = after(dattn_sib, f_grads, hidden_b)
    if fast:
        up_keep, up_send, down_keep, down_send = f_grads
        up_got, down_got = hop(up_send, 0, 2), hop(down_send, 1, 0)
    count = rows + 2 * cr + 9 + 4 * nr + 2 * total
    (small_g,) = call(
        functools.partial(pack_grads_kernel, sizes),
        [sds((nd, count + -count % 16, 128))],
        [info, g_st, g_pool, g_class, vec1, vec2, nvec, ub0, ub1, report],
        [SMEM] + [None] * 9,
        name="pack",
    )
    small_g = small_g + hop(small_g.astype(BF), 0, 1).astype(F32)
    small_y = small_g + hop(small_g.astype(BF), 0, 2).astype(F32)


    def qkv_grad(g, ctx, sums):
        return call(
            functools.partial(qkv_grad_kernel, nh),
            grad_outs(1, 1, nd, rows, fast, 8),
            [info, tokens, sib, g, dattn, dattn_sib, ctx, sums],
            [SMEM] + [None] * 7,
            [pltpu.VMEM((D, D), F32), pltpu.VMEM((max(8, nd), 128), F32)],
            "qkv_grad",
        )

    g1, g1_sum = attn_bwd(nh, proj1, w1, aux, ctx1, dattn, after(dattn_sib, small_y), lse1)
    far_grad = qkv_grad(g1, ctx1, g1_sum)
    if fast:
        far_got = [hop(g, 0, 2) for g in far_grad]
    g0, g0_sum = attn_bwd(
        nh, proj0, w0, aux, ctx0, dattn, after(dattn_sib, g1, far_grad), lse0
    )
    if fast:
        g0, up_got, down_got = lax.optimization_barrier((g0, up_got, down_got))
    tok_send, tok_own = call(
        token_grad_kernel, [sds((half, D), BF), sds((half, D))], [g0, g1, w0, w1, dr1], name="token_grad"
    )
    near_grad = qkv_grad(g0, ctx0, g0_sum)
    tok_sum = after((tok_own + hop(tok_send, 0, 1).astype(F32)).astype(BF), near_grad)
    input_a = undeal(tok_sum)
    if fast:
        block_ = (nd // 2, rows, D)
        f_keep, up_half, down_half = call(
            sum_half_kernel,
            [sds((2, *block_), BF), sds(block_, BF), sds(block_, BF)],
            [up_keep, up_got, down_keep, down_got],
            name="grad_half",
        )
        f_sums = call(
            sum_last_kernel,
            [sds((2, rows, D))] + [sds((2, rows, D), BF)] * (nd // 2 - 1),
            [f_keep, hop(up_half, 1, 0), hop(down_half, 0, 2)],
            name="grad_sum",
        )
        f_sum = finish_lines(f_sums)
        near_part = (near_grad[1].astype(F32) + far_got[1].astype(F32)).astype(BF)
        qo_own = (near_grad[0], far_got[0], hop(near_part, 1, 0))
    else:
        qo_own = ()
        f_sums = f_sum = sum_lines(f_grads)
    hidden_out = place(hidden_a, hidden_b)
    input_b = hop(after(input_a, hidden_out, f_sums, qo_own[1:]), 0, 2)
    small_g = lax.all_to_all(after(small_y.astype(BF), input_b), "dp", 0, 0, tiled=True).astype(F32).sum(0)
    input_grad = place(input_a, input_b)
    up_sum, down_sum = f_sum
    if fast:
        qo_sum = finish_lines(sum_blocks(qo_own))[0]
    else:
        qo_sum = sum_lines([*near_grad, *far_grad])[0]

    width = 2 * HS // nd
    if fast:
        g_qv = qo_sum[rows, : nh * width].reshape(nh, width)
        qo_sum = qo_sum[:rows]
    else:
        g_qv = [
            jnp.concatenate([g[0, :hw].reshape(nh, HS), g[0, 2 * hw : 3 * hw].reshape(nh, HS)], axis=1)
            for g in (g0_sum, g1_sum)
        ]
        g_qv = g_qv[0] + hop(g_qv[1], 0, 2)
        bit = 1
        while bit < nd:
            g_qv = g_qv + hop(g_qv, bit, 0)
            bit *= 2
        g_qv = lax.dynamic_slice(g_qv, (0, width * me), (nh, width))

    at = rows + 2 * cr + 9 + 4 * nr
    table = small_g[at : at + total] + small_g[at + total : at + 2 * total]
    logit_all = table[:, :CLASSES]
    class_bias_grad = jnp.sum(table[:, CLASSES : 2 * CLASSES], 0)
    squares = jnp.sum(table[:, 2 * CLASSES : 2 * CLASSES + 8], 0).reshape(2, 4).sum(0)
    rms = jnp.sqrt(squares / (jnp.sum(lengths).astype(F32) * D))

    at = rows + 2 * cr
    g_wide = small_g[at : at + 6, :rows]
    g_narrow = small_g[at + 6 : at + 9, :cr]
    g_ub = lax.dynamic_slice(small_g, (at + 9 + nr * m, 0), (nr, HS // nd))
    return (
        hidden_out,
        logit_all,
        input_grad,
        jnp.transpose(qo_sum[:, : 3 * hw].reshape(rows, 3, hw), (1, 0, 2)),
        g_qv,
        qo_sum[:, 3 * hw :].T,
        g_wide[0],
        g_wide[1],
        g_wide[2],
        up_sum,
        g_ub,
        down_sum.T,
        g_wide[3],
        g_wide[4],
        g_wide[5],
        small_g[:rows],
        g_narrow[0],
        g_narrow[1],
        small_g[rows : rows + cr],
        g_narrow[2],
        small_g[rows + cr : at, :CLASSES],
        class_bias_grad,
        rms,
    )


def solution(mesh):
    rows = P(None, "dp", None)
    vec = P("dp")
    return jax.shard_map(
        body,
        mesh=mesh,
        in_specs=(
            rows,
            rows,
            P(),
            P(),
            P(None, "dp", "mp"),
            P("mp", "dp"),
            P("mp", "dp"),
            vec,
            vec,
            vec,
            P("dp", "mp"),
            P("mp", "dp"),
            P("mp", "dp"),
            vec,
            vec,
            vec,
            P("dp", None),
            vec,
            vec,
            P("dp", None),
            vec,
            P("dp", None),
            P(),
        ),
        out_specs=(
            rows,
            P(),
            rows,
            P(None, "dp", "mp"),
            P("mp", "dp"),
            P("mp", "dp"),
            vec,
            vec,
            vec,
            P("dp", "mp"),
            P("mp", "dp"),
            P("mp", "dp"),
            vec,
            vec,
            vec,
            P("dp", None),
            vec,
            vec,
            P("dp", None),
            vec,
            P("dp", None),
            P(),
            P(),
        ),
        check_vma=False,
    )
```

```python
import functools

import jax
import jax.numpy as jnp
import numpy as np
from jax import lax
from jax.experimental import pallas as pl
from jax.experimental.pallas import tpu as pltpu
from jax.sharding import PartitionSpec as P

D = 768
HS = 64
CW = 128
PH = 2
CLASSES = 14
EPSILON = 1e-06
NEGATIVE = -1e30
LOG2E = 1.4426950408889634
HIGHEST = lax.Precision.HIGHEST
BF = jnp.bfloat16
F32 = jnp.float32
AXES = ("dp", "mp")
QB = 256
RB = 128
SLOW = 1
ROOM = 16
ROOMS = {'product': 60, 'ffn_back': 60}


def dot(a, b, ca, cb):
    return lax.dot_general(a, b, (((ca,), (cb,)), ((), ())), preferred_element_type=F32)


def hop(x, dbit, mbit):
    nd, nm = lax.axis_size("dp"), lax.axis_size("mp")
    pairs = [(d * nm + m, (d ^ dbit) * nm + (m ^ mbit)) for d in range(nd) for m in range(nm)]
    return lax.ppermute(x, AXES, pairs)


def after(x, *others):
    return lax.optimization_barrier((x, *others))[0]


def bit_groups(nd):
    bits = []
    b = nd // 2
    while b > 1:
        bits.append(b)
        b //= 2
    groups = [bits[i : i + 2] for i in range(0, len(bits), 2)]
    out = []
    for g in groups:
        out.append([0, g[0]] if len(g) == 1 else [0, g[1], g[0], g[0] + g[1]])
    return out


def gather_chips(x):
    nd = lax.axis_size("dp")
    cur = x[None]
    for masks in bit_groups(nd):
        parts = [cur] + [hop(cur, k, 0) for k in masks[1:]]
        cur = jnp.stack(parts, 1).reshape(-1, *x.shape)
    near, far = (hop(cur, 1, 0), hop(cur, 0, 2))
    far2 = hop(cur, 1, 2)
    return (
        jnp.stack([cur, near], 1).reshape(nd, *x.shape),
        jnp.stack([far, far2], 1).reshape(nd, *x.shape),
    )


def scatter_chips(mine, other):
    nd = lax.axis_size("dp")
    tail = mine.shape[1:]
    a = mine.reshape(nd // 2, 2, *tail)
    b = other.reshape(nd // 2, 2, *tail)
    cur = (
        a[:, 0].astype(F32)
        + hop(a[:, 1], 1, 0).astype(F32)
        + hop(b[:, 0], 0, 2).astype(F32)
        + hop(b[:, 1], 1, 2).astype(F32)
    )
    for masks in reversed(bit_groups(nd)):
        low = cur.astype(BF).reshape(-1, len(masks), *tail)
        full = cur.reshape(-1, len(masks), *tail)
        cur = full[:, 0]
        for i, k in enumerate(masks[1:], 1):
            cur = cur + hop(low[:, i], k, 0).astype(F32)
    return cur[0]


def relative(x, me):
    return jnp.take(x, jnp.arange(x.shape[0], dtype=jnp.int32) ^ me, axis=0)


def split3(x):
    a = x.astype(BF)
    r = x - a.astype(F32)
    b = r.astype(BF)
    return a, b, (r - b.astype(F32)).astype(BF)


def swap64(x):
    return jnp.concatenate([x[:, 64:], x[:, :64]], axis=1)


def doubled(kp, head):
    lane = lax.broadcasted_iota(jnp.int32, kp.shape, 1)
    kr = swap64(kp)
    return jnp.where(lane < 64, kp, kr) if head == 0 else jnp.where(lane < 64, kr, kp)


ANY = pl.BlockSpec(memory_space=pl.ANY)
SMEM = pl.BlockSpec(memory_space=pltpu.SMEM)


def room(mib):
    return pltpu.CompilerParams(vmem_limit_bytes=mib << 20)


def call(kernel, outs, args, specs=None, scratch=(), name=None, flops=0, mib=ROOM):
    specs = [pl.BlockSpec(memory_space=pltpu.VMEM) if s is None else s for s in (specs or [None] * len(args))]
    size = sum(a.size * a.dtype.itemsize for a in args) + sum(
        int(np.prod(o.shape)) * np.dtype(o.dtype).itemsize for o in outs
    )
    return pl.pallas_call(
        kernel,
        in_specs=specs,
        out_specs=[pl.BlockSpec(memory_space=pltpu.VMEM)] * len(outs),
        out_shape=outs,
        scratch_shapes=list(scratch),
        cost_estimate=cost(size, flops),
        compiler_params=room(ROOMS.get(name, ROOM)),
        name=name,
    )(*args)


def cost(size, flops=0):
    return pl.CostEstimate(flops=int(flops) // SLOW, bytes_accessed=int(size) // SLOW, transcendentals=0)


def sds(shape, dtype=F32):
    return jax.ShapeDtypeStruct(shape, dtype)


def by_rows(kernel, outs, sums, args, consts, info=None, name=None):
    n = args[0].shape[0]

    def cut(a):
        return pl.BlockSpec((RB, a.shape[1]), lambda i: (i, 0))

    def whole(a):
        return pl.BlockSpec(a.shape, lambda i: (0,) * len(a.shape))

    head = [] if info is None else [info]
    size = sum(a.size * a.dtype.itemsize for a in [*args, *consts])
    return pl.pallas_call(
        kernel,
        grid=(n // RB,),
        in_specs=[SMEM] * len(head) + [cut(a) for a in args] + [whole(a) for a in consts],
        out_specs=[cut(o) for o in outs] + [whole(o) for o in sums],
        out_shape=[*outs, *sums],
        cost_estimate=cost(size),
        compiler_params=room(60),
        name=name,
    )(*head, *args, *consts)


def start_sums(*refs):
    @pl.when(pl.program_id(0) == 0)
    def _():
        for r in refs:
            r[...] = jnp.zeros(r.shape, F32)


def start(copies):
    for cp in copies:
        cp.start()
    return copies


def load_pair(info, arrays, w_ref, sems):
    if len(arrays) == 1:
        return start([pltpu.make_async_copy(arrays[0].at[0], w_ref, sems.at[0])])
    nz = arrays[0].shape[1]
    rows = D // (2 * nz)
    copies = []
    for x, a in enumerate(arrays):
        for z in range(nz):
            at = pl.multiple_of((info[0] ^ (2 * z + x)) * rows, 16)
            copies.append(
                pltpu.make_async_copy(a.at[0, z, pl.ds(0, rows), :], w_ref.at[pl.ds(at, rows), :], sems.at[len(copies)])
            )
    return start(copies)


def load_rows(info, arrays, k, b_ref, sems):
    nz = arrays[0].shape[1]
    rows = D // (2 * nz)
    copies = []
    for x, a in enumerate(arrays):
        for z in range(nz):
            copies.append(
                pltpu.make_async_copy(
                    a.at[k, z, pl.ds(rows, b_ref.shape[1]), :], b_ref.at[info[0] ^ (2 * z + x)], sems.at[len(copies)]
                )
            )
    return start(copies)


def load_weight(info, arrays, k, w_ref, sems):
    if len(arrays) == 2:
        return start([pltpu.make_async_copy(a.at[k], w_ref.at[i], sems.at[i]) for i, a in enumerate(arrays)])
    nz = arrays[0].shape[1]
    rows = D // (2 * nz)
    copies = []
    for i, a in enumerate(arrays):
        for z in range(nz):
            at = pl.multiple_of((info[0] ^ (2 * z + i % 2)) * rows, 16)
            copies.append(
                pltpu.make_async_copy(
                    a.at[k, z, pl.ds(0, rows), :], w_ref.at[i // 2, pl.ds(at, rows), :], sems.at[len(copies)]
                )
            )
    return start(copies)


def wait(copies):
    for cp in copies:
        cp.wait()


def weight_scratch(arrays):
    count = len(arrays) if len(arrays) == 2 else 4 * arrays[0].shape[1]
    return [pltpu.VMEM((2, D, arrays[0].shape[-1]), BF), pltpu.SemaphoreType.DMA((count,))]


def gather_lines(local):
    k, rows, n = local.shape
    cur = local[:, None]
    *groups, last = bit_groups(lax.axis_size("dp"))
    for masks in groups:
        parts = [cur] + [hop(cur, b, 0) for b in masks[1:]]
        cur = jnp.stack(parts, 2).reshape(k, -1, rows, n)
    return [cur] + [hop(cur, b, 0) for b in last[1:]]


def gather_doubling(local, *others):
    k, rows, n = local.shape
    cur, got = local[:, None], []
    bit = lax.axis_size("dp") // 2
    while bit > 1:
        got.append(hop(cur, bit, 0))
        cur = jnp.stack([cur, got[-1]], 2).reshape(k, -1, rows, n)
        bit //= 2
    return cur, got


def join_lines(parts):
    k, _, rows, n = parts[0].shape
    return jnp.stack(parts, 2).reshape(k, -1, rows, n)


def gather_planes(cur, fast):
    near, far, far2 = hop(cur, 1, 0), hop(cur, 0, 2), hop(cur, 1, 2)
    if fast:
        return cur, near, far, far2
    me = lax.axis_index("dp")
    k, half, rows, n = cur.shape

    def ordered(a, b):
        both = jnp.stack([a, b], 2).reshape(k, 2 * half, rows, n)
        return jnp.moveaxis(relative(jnp.moveaxis(both, 1, 0), me), 0, 1).reshape(k, 2 * half * rows, n)

    return ordered(cur, near), ordered(far, far2)


def spread(info, g_ref, k, outs):
    nz = outs[0].shape[1]
    rows = D // (2 * nz)
    for z in range(nz):
        for x in range(2):
            at = pl.multiple_of((info[0] ^ (2 * z + x)) * rows, 8)
            outs[x][k, z, :rows] = g_ref[pl.ds(at, rows), :].astype(BF)


def grad_outs(k, ys, nd, rows, fast, more=0):
    return [sds((k, nd // 2, rows + more, D), BF)] * (2 * ys) if fast else [sds((k, D, D), BF)] * ys


def store_grad(info, k, y, g, g_ref, outs):
    if len(outs[0].shape) == 4:
        g_ref[...] = g
        spread(info, g_ref, k, outs[2 * y : 2 * y + 2])
    else:
        outs[y][k] = g.astype(BF)


def sum_first_kernel(count, *refs):
    parts, (keep_ref, *send_refs) = refs[:count], refs[count:]
    for k in range(parts[0].shape[0]):
        for z in range(parts[0].shape[1]):
            total = parts[0][k, z].astype(F32)
            for r in parts[1:]:
                total = total + r[k, z].astype(F32)
            if z == 0:
                keep_ref[k] = total
            else:
                send_refs[z - 1][k] = total.astype(BF)


def sum_planes(parts):
    if len(parts) == 2:
        return list(parts)
    keep, x, y, xy = parts
    return [keep, hop(x, 1, 0), hop(y, 0, 2), hop(xy, 1, 2)]


def sum_lines(parts):
    nd = lax.axis_size("dp")
    if len(parts) == 2:
        me = lax.axis_index("dp")
        k = parts[0].shape[0]
        near, far = (
            relative(jnp.moveaxis(p.reshape(k, nd, D // nd, D), 0, 1), me) for p in parts
        )
        return scatter_chips(near, far)
    return finish_lines(sum_blocks(parts))


def sum_blocks(parts):
    if len(parts) == 2:
        return parts
    k, nz, rows, n = parts[0].shape
    return call(
        functools.partial(sum_first_kernel, len(parts)),
        [sds((k, rows, n))] + [sds((k, rows, n), BF)] * (nz - 1),
        list(parts),
        name="grad_sum",
    )


def finish_lines(sums):
    own, low, *high = sums
    if len(high) != 2:
        for z, piece in enumerate([low, *high], 1):
            own = own + hop(piece, 2 * z, 0).astype(F32)
        return own
    got = hop(jnp.stack([low, high[1]]), 2, 0)
    send = (high[0].astype(F32) + got[1].astype(F32)).astype(BF)
    return own + got[0].astype(F32) + hop(send, 4, 0).astype(F32)


def bias_rows(b, first, count, low, high):
    return jnp.concatenate([b[first + i : first + i + 1, low:high] for i in range(count)], axis=1)


def block(ref, i):
    return ref[:, 128 * i : 128 * i + 128]


def attn_fwd_kernel(nh, info, own_ref, sib_ref, bias_ref, aux_ref, *rest):
    *arrays, proj_ref, w_ref, ctx_ref, lse_ref, w_sems, o_ref, b_ref, b_sems = rest
    copies = load_pair(info, arrays, w_ref, w_sems)
    hw = nh * HS
    if len(arrays) == 2:
        wait(load_rows(info, arrays, 0, b_ref, b_sems))
        nd = b_ref.shape[0]
        w = 2 * HS // nd

        def bias_part(first):
            return [b_ref[a, h : h + 1, :w] for h in range(nh) for a in range(first, first + nd // 2)]

        q_part, v_part = (
            jnp.concatenate(bias_part(a), axis=1).astype(F32) for a in (0, nd // 2)
        )
    else:
        bias = bias_ref[...].astype(F32)
        q_part = bias_rows(bias, 0, nh, 0, HS)
        v_part = bias_rows(bias, 0, nh, HS, 2 * HS)
    row_bias = jnp.concatenate([q_part, jnp.zeros((1, hw), F32), v_part, jnp.zeros((1, HS), F32)], axis=1)
    wait(copies)
    half = own_ref.shape[0]
    n = 2 * half
    for i, ref in enumerate((own_ref, sib_ref)):
        for j in range(2):
            r = slice(j * half // 2, (j + 1) * half // 2)
            out = dot(ref[r], w_ref[:, : 10 * HS], 1, 0) + row_bias
            proj_ref[i * half + r.start : i * half + r.stop] = out.astype(BF)
    qt = [jnp.transpose(block(proj_ref, i).astype(F32)) * (HS**-0.5 * LOG2E) for i in (0, 1)]
    hi = [q.astype(BF) for q in qt]
    lo = [(q - h.astype(F32)).astype(BF) for q, h in zip(qt, hi)]
    vt = [jnp.transpose(block(proj_ref, i).astype(F32)).astype(BF) for i in (3, 4)]
    row = lax.broadcasted_iota(jnp.int32, (128, QB), 0)
    auxq = jnp.where(row == 0, 1.0, 0.0).astype(BF)
    o_ref[0:HS] = jnp.zeros((HS, n), F32)
    lse_ref[...] = jnp.zeros(lse_ref.shape, F32)
    for h in range(nh):
        kb, kh = ((1, 1), (2, 0), (2, 1))[h]
        lhs = jnp.concatenate([doubled(block(proj_ref, kb), kh), aux_ref[...]], axis=1)
        i, r = h // 2, slice(64 * (h % 2), 64 * (h % 2) + 64)
        vaug = jnp.concatenate([vt[i][r], jnp.ones((16, n), BF)], axis=0)
        to = slice(64 * h + 64, 64 * h + 128)
        for b in range(n // QB):
            s = slice(b * QB, b * QB + QB)
            rhs = jnp.concatenate([hi[i][r, s], lo[i][r, s], auxq], axis=0)
            sc = dot(lhs, rhs, 1, 0)
            m = jnp.max(sc, axis=0, keepdims=True)
            p = jnp.exp2(sc - m).astype(BF)
            o = dot(vaug, p, 1, 0)
            total = o[64:65]
            o_ref[to, s] = o[:64] / total
            lse_ref[h : h + 1, s] = m + jnp.log2(total)
    for j in range(2):
        ctx_ref[:, 128 * j : 128 * j + 128] = jnp.transpose(o_ref[128 * j : 128 * j + 128]).astype(BF)


def attn_fwd(nh, info, own, sib, bias, aux, arrays):
    n = 2 * own.shape[0]
    count = len(arrays) * arrays[0].shape[1] if len(arrays) == 2 else 1
    return call(
        functools.partial(attn_fwd_kernel, nh),
        [sds((n, 10 * HS), BF), sds((D, D), BF), sds((n, 4 * HS), BF), sds((8, n))],
        [info, own, sib, bias, aux, *arrays],
        [SMEM] + [None] * 4 + [ANY] * len(arrays),
        [
            pltpu.SemaphoreType.DMA((count,)),
            pltpu.VMEM((4 * HS, n), F32),
            pltpu.VMEM((count, 16, D), BF),
            pltpu.SemaphoreType.DMA((count,)),
        ],
        "attn_fwd",
        flops=11_000_000_000,
    )


def out_kernel(first, c0_ref, c1_ref, w0_ref, w1_ref, out_ref):
    rows, cols = slice(first, first + out_ref.shape[0]), slice(8 * HS, 12 * HS)
    part = dot(c0_ref[rows], w0_ref[:, cols], 1, 1) + dot(c1_ref[rows], w1_ref[:, cols], 1, 1)
    out_ref[...] = part.astype(out_ref.dtype)


def norm(values, gain, shift):
    center = values - jnp.mean(values, -1, keepdims=True)
    spread_ = jnp.mean(center * center, -1, keepdims=True)
    scale = lax.rsqrt(spread_ + EPSILON)
    normed = center * scale
    return normed * gain + shift, normed, scale


def live_rows(aux_ref):
    return jnp.where(aux_ref[:, 0:1].astype(F32) > -1.0, 1.0, 0.0)


def square(live, v):
    return jnp.sum(jnp.sum(v * v, -1, keepdims=True) * live, axis=0, keepdims=True)


def ln1_kernel(part_ref, got_ref, tok_ref, aux_ref, wide_ref, first_ref, low_ref, n_ref, s_ref, sq_ref):
    start_sums(sq_ref)
    tok = tok_ref[...].astype(F32)
    att = part_ref[...] + got_ref[...].astype(F32) + wide_ref[0:1]
    first, normed, scale = norm(tok + att, wide_ref[1:2], wide_ref[2:3])
    first_ref[...] = first
    low_ref[...] = first.astype(BF)
    n_ref[...] = normed
    s_ref[...] = scale
    live = live_rows(aux_ref)
    lane = lax.broadcasted_iota(jnp.int32, (1, 128), 1)
    out = jnp.zeros((1, 128), F32)
    for i, v in enumerate((tok, att, first)):
        out = jnp.where(lane == i, square(live, v), out)
    sq_ref[...] += out


def hidden_bias(b_ref, nr):
    nd = b_ref.shape[0]
    w = HS // nd
    first = jnp.concatenate([b_ref[a, 0:1, :128] for a in range(nd)], axis=0)
    i = lax.broadcasted_iota(jnp.int32, (128, nr * HS), 0)
    f = lax.broadcasted_iota(jnp.int32, (128, nr * HS), 1)
    place = jnp.where(i == (f // HS) * w + f % w, 1.0, 0.0).astype(BF)
    spread_ = dot(first, place, 1, 0)
    a = lax.broadcasted_iota(jnp.int32, (nd, nr * HS), 0)
    f = lax.broadcasted_iota(jnp.int32, (nd, nr * HS), 1)
    return jnp.sum(jnp.where((f % HS) // w == a, spread_, 0.0), axis=0, keepdims=True)


def ffn_up_kernel(nh, nr, info, x_ref, b0_ref, b1_ref, *rest):
    *up, act_ref, slope_ref, up_ref, sems, r0_ref, r1_ref, r_sems = rest
    copies = load_weight(info, up, 0, up_ref, sems)
    fw = nr * HS
    x = x_ref[...]
    if len(up) == 4:
        for i, r_ref in enumerate((r0_ref, r1_ref)):
            wait(load_rows(info, up[2 * i : 2 * i + 2], 0, r_ref, r_sems))
        biases = [hidden_bias(r_ref, nr) for r_ref in (r0_ref, r1_ref)]
    else:
        biases = [bias_rows(b_ref[...].astype(F32), nh, nr, 0, HS) for b_ref in (b0_ref, b1_ref)]
    wait(copies)
    for y in range(2):
        for j in range(fw // 256):
            s = slice(j * 256, (j + 1) * 256)
            t = slice(y * fw + j * 256, y * fw + (j + 1) * 256)
            pre = dot(x, up_ref[y, :, s], 1, 0) + biases[y][:, s]
            phi = 0.5 + 0.5 * lax.erf(pre * (0.5**0.5))
            act_ref[:, t] = (pre * phi).astype(BF)
            slope_ref[:, t] = (phi + pre * (jnp.exp(-0.5 * pre * pre) * (2 * np.pi) ** -0.5)).astype(BF)


def product_kernel(k, info, a_ref, *rest):
    *w, out_ref, w_ref, sems = rest
    wait(load_weight(info, w, k, w_ref, sems))
    fw = w_ref.shape[2]
    out_ref[...] = (dot(a_ref[:, :fw], w_ref[0], 1, 1) + dot(a_ref[:, fw:], w_ref[1], 1, 1)).astype(out_ref.dtype)


def head_ones():
    a = lax.broadcasted_iota(jnp.int32, (CW, CW), 0) // (CW // PH)
    b = lax.broadcasted_iota(jnp.int32, (CW, CW), 1) // (CW // PH)
    return jnp.where(a == b, 1.0, 0.0)


def fdot(a, b, ca=1, cb=0):
    return lax.dot_general(a, b, (((ca,), (cb,)), ((), ())), precision=HIGHEST, preferred_element_type=F32)


def ln2_kernel(
    part_ref, got_ref, first_ref, aux_ref, wide_ref, narrow_ref, sw_ref, low_ref, n_ref, s_ref, st_ref, lg_ref, stat_ref
):
    feed = part_ref[...] + got_ref[...].astype(F32) + wide_ref[3:4]
    second, normed, scale = norm(first_ref[...] + feed, wide_ref[4:5], wide_ref[5:6])
    low = second.astype(BF)
    low_ref[...] = low
    n_ref[...] = normed
    s_ref[...] = scale
    student = dot(low, sw_ref[...], 1, 0) + narrow_ref[0:1]
    st_ref[...] = student
    live = live_rows(aux_ref)
    logit = fdot(student * narrow_ref[1:2], head_ones()) * (CW // PH) ** -0.5
    logit = jnp.where(live > 0.0, logit, NEGATIVE)
    lg_ref[...] = logit

    @pl.when(pl.program_id(0) == 0)
    def _():
        stat_ref[...] = jnp.zeros((8, 128), F32)
        stat_ref[0:1] = jnp.full((1, 128), NEGATIVE, F32)

    old = stat_ref[0:1]
    top = jnp.maximum(old, jnp.max(logit, axis=0, keepdims=True))
    shrink = jnp.exp(old - top)
    weight = jnp.where(live > 0.0, jnp.exp(logit - top), 0.0)
    stat_ref[0:1] = top
    stat_ref[1:2] = stat_ref[1:2] * shrink + jnp.sum(weight, axis=0, keepdims=True)
    stat_ref[2:3] = stat_ref[2:3] * shrink + jnp.sum(weight * student, axis=0, keepdims=True)
    stat_ref[3:4] += jnp.broadcast_to(square(live, feed), (1, 128))


def norm_back(up, normed, scale, gain):
    scaled = up * gain
    inner = scaled - jnp.mean(scaled, -1, keepdims=True) - normed * jnp.mean(scaled * normed, -1, keepdims=True)
    return inner * scale


def colsum(x):
    return jnp.sum(x, axis=0, keepdims=True)


def head_kernel(
    info,
    st_ref,
    lg_ref,
    low_ref,
    cot_ref,
    n_ref,
    s_ref,
    stat_ref,
    sib_ref,
    sq_ref,
    pooler_ref,
    class_ref,
    cb_ref,
    narrow_ref,
    sw_ref,
    wide_ref,
    dr2_ref,
    dffn_ref,
    gst_ref,
    gpool_ref,
    gclass_ref,
    rep_ref,
    vec_ref,
    nvec_ref,
    keep_ref,
):
    scale = (CW // PH) ** -0.5
    once = jnp.where(info[1] == 0, 1.0, 0.0)

    @pl.when(pl.program_id(0) == 0)
    def _():
        top, top2 = stat_ref[0:1], sib_ref[0:1]
        best = jnp.maximum(top, top2)
        fa, fb = jnp.exp(top - best), jnp.exp(top2 - best)
        whole = stat_ref[1:2] * fa + sib_ref[1:2] * fb
        pooled = (stat_ref[2:3] * fa + sib_ref[2:3] * fb) / whole
        pooled = jnp.broadcast_to(pooled, (8, CW))
        z = jnp.tanh(fdot(pooled, pooler_ref[...]) + narrow_ref[2:3])
        lane = lax.broadcasted_iota(jnp.int32, (8, 128), 1)
        row = lax.broadcasted_iota(jnp.int32, (8, 128), 0)
        logit = fdot(z, class_ref[...]) + cb_ref[...]
        masked = jnp.where(lane < CLASSES, logit, NEGATIVE)
        e = jnp.exp(masked - jnp.max(masked, axis=1, keepdims=True))
        dlogit = e / jnp.sum(e, axis=1, keepdims=True) - jnp.where(lane == info[3], 1.0, 0.0)
        only = jnp.where(row == 0, once, 0.0)
        gclass_ref[...] = fdot(z * only, dlogit, 0, 0)
        dz = fdot(dlogit, class_ref[...], 1, 1)
        dzp = dz * (1.0 - z * z)
        gpool_ref[...] = fdot(pooled * only, dzp, 0, 0)
        dpooled = fdot(dzp, pooler_ref[...], 1, 1)
        sq = jnp.where(lane[0:1] == 3, stat_ref[3:4] + sib_ref[3:4] * 0.0, sq_ref[...])
        sq = jnp.where(info[1] == 0, pltpu.roll(sq, 2 * CLASSES, 1), pltpu.roll(sq, 2 * CLASSES + 4, 1))
        rep = jnp.where(lane < CLASSES, logit, pltpu.roll(jnp.where(lane < CLASSES, dlogit, 0.0), CLASSES, 1)) * once
        rep_ref[...] = jnp.where(lane < 2 * CLASSES, rep, sq)
        nvec_ref[...] = jnp.zeros((8, CW), F32)
        nvec_ref[2:3] = dzp[0:1] * once
        vec_ref[...] = jnp.zeros((8, D), F32)
        gst_ref[...] = jnp.zeros((D, CW), F32)
        keep_ref[0:1] = best
        keep_ref[1:2] = whole
        keep_ref[2:3] = dpooled[0:1]
        keep_ref[3:4] = fdot(pooled * dpooled, head_ones())[0:1]

    student = st_ref[...]
    dp = keep_ref[2:3]
    logit = lg_ref[...]
    weight = jnp.where(logit > 0.5 * NEGATIVE, jnp.exp(logit - keep_ref[0:1]), 0.0) / keep_ref[1:2]
    dq = scale * weight * (fdot(student * dp, head_ones()) - keep_ref[3:4])
    dstudent = (weight * dp + dq * narrow_ref[1:2]).astype(BF)
    nvec_ref[0:1] += colsum(dstudent.astype(F32))
    nvec_ref[1:2] += colsum(dq * student)
    gst_ref[...] += dot(low_ref[...], dstudent, 0, 0)
    dsecond = dot(dstudent, sw_ref[...], 1, 1) + cot_ref[...].astype(F32)
    normed = n_ref[...]
    dr2 = norm_back(dsecond, normed, s_ref[...], wide_ref[4:5])
    dr2_ref[...] = dr2
    dffn_ref[...] = dr2.astype(BF)
    vec_ref[0:1] += colsum(dr2)
    vec_ref[1:2] += colsum(dsecond * normed)
    vec_ref[2:3] += colsum(dsecond)


def ffn_back_kernel(info, g_ref, slope_ref, *rest):
    *down, dpre_ref, ub_ref, w_ref, sems = rest
    copies = load_weight(info, down, 1, w_ref, sems)
    fw = w_ref.shape[2]
    g = g_ref[...]
    ub_ref[...] = jnp.zeros(ub_ref.shape, F32)
    wait(copies)
    for y in range(2):
        for j in range(fw // 256):
            s = slice(j * 256, (j + 1) * 256)
            t = slice(y * fw + j * 256, y * fw + (j + 1) * 256)
            dpre = (dot(g, w_ref[y, :, s], 1, 0) * slope_ref[:, t].astype(F32)).astype(BF)
            dpre_ref[:, t] = dpre
            ub_ref[0:1, t] = colsum(dpre.astype(F32))


def ffn_grad_kernel(info, first, first2, dpre, dpre2, dffn, dffn2, act, act2, *rest):
    *outs, g_ref = rest
    fw = dpre.shape[1] // 2
    for k, (a0, a1, b0, b1) in enumerate(((first, first2, dpre, dpre2), (dffn, dffn2, act, act2))):
        for y in range(2):
            s = slice(y * fw, (y + 1) * fw)
            g = dot(a0[...], b0[:, s], 0, 0) + dot(a1[...], b1[:, s], 0, 0)
            if len(outs) == 2:
                outs[y][k] = g.astype(BF)
                continue
            g_ref[...] = g
            nz = outs[0].shape[1]
            rows = D // (2 * nz)
            for z in range(nz):
                for x in range(2):
                    at = pl.multiple_of((info[0] ^ (2 * z + x)) * rows, 8)
                    piece = g_ref[pl.ds(at, rows), :].astype(BF)
                    if k == 0:
                        outs[y][x, z] = piece
                    else:
                        outs[2 + x][y, z] = piece


def sum_half_kernel(a_ref, ga_ref, b_ref, gb_ref, keep_ref, sa_ref, sb_ref):
    for k, (r, g, send_ref) in enumerate(((a_ref, ga_ref, sa_ref), (b_ref, gb_ref, sb_ref))):
        for z in range(r.shape[1]):
            keep_ref[k, z] = (r[0, z].astype(F32) + g[0, z].astype(F32)).astype(BF)
            send_ref[z] = (r[1, z].astype(F32) + g[1, z].astype(F32)).astype(BF)


def sum_last_kernel(keep_ref, a_ref, b_ref, own_ref, *send_refs):
    for k, g in enumerate((a_ref, b_ref)):
        for z in range(keep_ref.shape[1]):
            total = keep_ref[k, z].astype(F32) + g[z].astype(F32)
            if z == 0:
                own_ref[k] = total
            else:
                send_refs[z - 1][k] = total.astype(BF)


def ln1_back_kernel(part_ref, got_ref, dr2_ref, n_ref, s_ref, wide_ref, dr1_ref, low_ref, vec_ref):
    start_sums(vec_ref)
    up = part_ref[...] + got_ref[...].astype(F32) + dr2_ref[...]
    normed = n_ref[...]
    dr1 = norm_back(up, normed, s_ref[...], wide_ref[1:2])
    dr1_ref[...] = dr1
    low_ref[...] = dr1.astype(BF)
    vec_ref[0:1] += colsum(dr1)
    vec_ref[1:2] += colsum(up * normed)
    vec_ref[2:3] += colsum(up)


def attn_bwd_kernel(nh, proj_ref, w_ref, aux_ref, ctx_ref, da_ref, db_ref, lse_ref, out_ref, sum_ref, do_ref, dqt_ref):
    n = proj_ref.shape[0]
    half = n // 2
    scale = HS**-0.5
    cols = slice(8 * HS, 12 * HS)
    for i, ref in enumerate((da_ref, db_ref)):
        do_ref[i * half : (i + 1) * half] = dot(ref[...], w_ref[:, cols], 1, 0).astype(BF)
    qb = [block(proj_ref, i) for i in (0, 1)]
    qt = [jnp.transpose(q.astype(F32)) * (scale * LOG2E) for q in qb]
    hi = [q.astype(BF) for q in qt]
    lo = [(q - h.astype(F32)).astype(BF) for q, h in zip(qt, hi)]
    kt = [jnp.transpose(block(proj_ref, i).astype(F32)).astype(BF) for i in (1, 2)]
    dob = [block(do_ref, i) for i in (0, 1)]
    dot_f = [jnp.transpose(d.astype(F32)) for d in dob]
    dot_b = [d.astype(BF) for d in dot_f]
    prod = [d * jnp.transpose(block(ctx_ref, i).astype(F32)) for i, d in enumerate(dot_f)]
    lane = lax.broadcasted_iota(jnp.int32, (n, 128), 1)
    row = lax.broadcasted_iota(jnp.int32, (128, QB), 0)
    zero = jnp.zeros((64, QB), BF)
    empty = jnp.zeros((n, 128), BF)
    dqt_ref[...] = jnp.zeros(dqt_ref.shape, F32)
    dk, dv = [], []
    for h in range(nh):
        kb, kh = ((1, 1), (2, 0), (2, 1))[h]
        i, ih = h // 2, h % 2
        vi, vh = ((3, 0), (3, 1), (4, 0))[h]
        oi, oh = ((0, 1), (1, 0), (1, 1))[h]
        lhs = jnp.concatenate([doubled(block(proj_ref, kb), kh), aux_ref[...]], axis=1)
        lhs_v = jnp.concatenate([block(proj_ref, vi), aux_ref[...]], axis=1)
        r = slice(64 * ih, 64 * ih + 64)
        ro = slice(64 * oh, 64 * oh + 64)
        rk = slice(64 * kh, 64 * kh + 64)
        qm = jnp.where((lane < 64) == (ih == 0), qb[i], empty)
        dom = jnp.where((lane < 64) == (oh == 0), dob[oi], empty)
        dsum = jnp.sum(prod[oi][ro], axis=0, keepdims=True)
        l1, l2, l3 = split3(-lse_ref[h : h + 1, :])
        d1, d2, d3 = split3(-dsum)
        dkh = jnp.zeros((n, 128), F32)
        dvh = jnp.zeros((n, 128), F32)
        for b in range(n // QB):
            s = slice(b * QB, b * QB + QB)

            def pieces(first, x1, x2, x3):
                z = jnp.where(row == 1, x1[:, s].astype(F32), jnp.where(row == 0, first, 0.0))
                z = jnp.where(row == 2, x2[:, s].astype(F32), z)
                return jnp.where(row == 3, x3[:, s].astype(F32), z).astype(BF)

            rhs = jnp.concatenate([hi[i][r, s], lo[i][r, s], pieces(1.0, l1, l2, l3)], axis=0)
            p = jnp.exp2(dot(lhs, rhs, 1, 0))
            g = dot_b[oi][ro, s]
            part = [g, zero] if vh == 0 else [zero, g]
            rhs_v = jnp.concatenate(part + [pieces(0.0, d1, d2, d3)], axis=0)
            ds = (p * dot(lhs_v, rhs_v, 1, 0)).astype(BF)
            dvh = dvh + dot(p.astype(BF), dom[s], 1, 0)
            dkh = dkh + dot(ds, qm[s], 1, 0)
            dqt_ref[64 * h : 64 * h + 64, s] = dot(kt[kb - 1][rk], ds, 1, 0)
        dk.append(dkh * scale)
        dv.append(dvh)

    def put(i, x):
        out_ref[:, 128 * i : 128 * i + 128] = x.astype(BF)
        sum_ref[:, 128 * i : 128 * i + 128] = jnp.broadcast_to(colsum(x.astype(BF).astype(F32)), (8, 128))

    left = lane < 64
    put(0, jnp.transpose(dqt_ref[0:128] * scale))
    put(1, jnp.where(left, jnp.transpose(dqt_ref[128:256] * scale), swap64(dk[0])))
    put(2, jnp.where(left, swap64(dk[1]), swap64(dk[2])))
    put(3, jnp.where(left, swap64(dv[0]), swap64(dv[1])))
    put(4, jnp.where(left, swap64(dv[2]), 0.0))


def attn_bwd(nh, proj, w, aux, ctx, da, db, lse):
    n = proj.shape[0]
    return call(
        functools.partial(attn_bwd_kernel, nh),
        [sds((n, 10 * HS), BF), sds((8, 10 * HS))],
        [proj, w, aux, ctx, da, db, lse],
        None,
        [pltpu.VMEM((n, 4 * HS), BF), pltpu.VMEM((4 * HS, n), F32)],
        "attn_bwd",
        flops=11_000_000_000,
    )


def token_grad_kernel(g0_ref, g1_ref, w0_ref, w1_ref, dr1_ref, send_ref, own_ref):
    n = g0_ref.shape[0]
    half = n // 2
    cols = slice(0, 10 * HS)
    for out_ref, s in ((send_ref, slice(half, n)), (own_ref, slice(0, half))):
        part = dot(g0_ref[s], w0_ref[:, cols], 1, 1) + dot(g1_ref[s], w1_ref[:, cols], 1, 1)
        if out_ref is own_ref:
            part = part + dr1_ref[...]
        out_ref[...] = part.astype(out_ref.dtype)


def qkv_grad_kernel(nh, info, x0, x1, g_in, da, db, ctx_ref, sum_ref, *rest):
    *outs, g_ref, t_ref = rest
    half = x0.shape[0]
    g = dot(x0[...], g_in[:half], 0, 0) + dot(x1[...], g_in[half:], 0, 0)
    o = dot(da[...], ctx_ref[:half], 0, 0) + dot(db[...], ctx_ref[half:], 0, 0)
    g = jnp.concatenate([g[:, : 8 * HS], g[:, 8 * HS :] + o[:, : 2 * HS], o[:, 2 * HS :]], axis=1)
    store_grad(info, 0, 0, g, g_ref, outs)
    if len(outs) == 2:
        nz = outs[0].shape[1]
        rows = D // (2 * nz)
        piece = HS // nz
        zero = jnp.zeros((1, 128 - nh * piece), F32)
        for a in range(2 * nz):
            base = (a % nz) * piece + (a // nz) * 2 * nh * HS
            cuts = [sum_ref[0:1, base + h * HS : base + h * HS + piece] for h in range(nh)]
            t_ref[a : a + 1] = jnp.concatenate([*cuts, zero], axis=1)
        for z in range(nz):
            for x in range(2):
                outs[x][0, z, rows:] = jnp.zeros((outs[x].shape[2] - rows, D), BF)
                row = t_ref[pl.ds(info[0] ^ (2 * z + x), 1), :]
                outs[x][0, z, rows : rows + 8, :128] = jnp.broadcast_to(row, (8, 128)).astype(BF)


def place_kernel(info, a_ref, b_ref, c_ref, d_ref, out_ref):
    c, y = info[1], info[2]
    out_ref[0, y, c] = a_ref[0]
    out_ref[0, 1 - y, c] = b_ref[0]
    out_ref[0, y, 1 - c] = c_ref[0]
    out_ref[0, 1 - y, 1 - c] = d_ref[0]


def lanes(x):
    x = x.reshape(1, -1) if x.ndim == 1 else x
    return jnp.pad(x, ((0, 0), (0, 128 - x.shape[1])))


def vectors_kernel(sizes, info, a0, a1, wide_ref, narrow_ref, b_ref, sems):
    rows, cr, nh, _ = sizes
    wait(load_rows(info, [a0, a1], 0, b_ref, sems))
    nd = b_ref.shape[0]
    for out_ref, row, count, width in ((wide_ref, nh, 6, rows), (narrow_ref, nh + 6, 3, cr)):
        out_ref[...] = jnp.zeros(out_ref.shape, F32)
        for i in range(count):
            cuts = [b_ref[a, row + i : row + i + 1, :width] for a in range(nd)]
            out_ref[i : i + 1] = jnp.concatenate(cuts, axis=1).astype(F32)


def matrices_kernel(info, a0, a1, sw_ref, pooler_ref, class_ref, b_ref, c_ref, sems):
    copies = load_rows(info, [a0, a1], 0, b_ref, sems.at[0])
    copies += load_rows(info, [a0, a1], 1, c_ref, sems.at[1])
    wait(copies)
    for a in range(b_ref.shape[0]):
        for i in range(2):
            at = slice(16 * a + 8 * i, 16 * a + 8 * i + 8)
            pooler_ref[at] = b_ref[a, 8:16, 128 * i : 128 * i + 128].astype(F32)
            class_ref[at] = b_ref[a, 8:16, 256 + 128 * i : 384 + 128 * i].astype(F32)
        for i in range(6):
            at = 96 * a + 16 * i
            sw_ref[at : at + 16] = c_ref[a, :, 128 * i : 128 * i + 128]


def unpack_kernel(sizes, in_ref, sw_ref, pooler_ref, class_ref, wide_ref, narrow_ref, bias_ref):
    rows, cr, nh, nr = sizes
    nd = in_ref.shape[0]
    blocks = [in_ref[d].astype(F32) for d in range(nd)]
    at = rows + 2 * cr

    def joined(first, count, width):
        return jnp.concatenate([b[first : first + count, :width] for b in blocks], axis=1)

    sw_ref[...] = jnp.concatenate([b[:rows] for b in blocks], axis=0).astype(BF)
    pooler_ref[...] = jnp.concatenate([b[rows : rows + cr] for b in blocks], axis=0)
    class_ref[...] = jnp.concatenate([b[rows + cr : at] for b in blocks], axis=0)
    wide_ref[...] = jnp.zeros(wide_ref.shape, F32)
    wide_ref[0:6] = joined(at, 6, rows)
    narrow_ref[...] = jnp.zeros(narrow_ref.shape, F32)
    narrow_ref[0:3] = joined(at + 6, 3, cr)
    bias_ref[...] = jnp.zeros(bias_ref.shape, F32)
    bias_ref[0:nh, :] = joined(at + 9, nh, 2 * HS // nd)
    bias_ref[nh : nh + nr, :HS] = joined(at + 9 + nh, nr, HS // nd)


def pack_grads_kernel(sizes, info, gst, gpool, gclass, v1, v2, nv, ub0, ub1, rep, out_ref):
    rows, cr, nh, nr = sizes
    nd = out_ref.shape[0]
    fw = nr * HS
    me = info[2] * 2 + info[1]
    ub = ub0[0:1] + ub1[0:1]
    pair = [
        jnp.concatenate([ub[:, y * fw + r * HS : y * fw + (r + 1) * HS] for r in range(nr)], axis=0) for y in range(2)
    ]
    quads = jnp.concatenate(
        [jnp.where(me == q, pair[0], jnp.where((me ^ 2) == q, pair[1], 0.0)) for q in range(4)], axis=0
    )
    wide = jnp.concatenate([v1[0:1], v1[1:2], v1[2:3], v2[0:1], v2[1:2], v2[2:3]], axis=0)

    def wider(x):
        return jnp.concatenate([x, jnp.zeros((x.shape[0], 128 - x.shape[1]), F32)], axis=1)

    total = 2 * nd
    row = lax.broadcasted_iota(jnp.int32, (total, 128), 0)
    high = rep[0:1].astype(BF).astype(F32)
    mine = row == 2 * info[0] + info[2]
    table = [jnp.where(mine, high, 0.0), jnp.where(mine, rep[0:1] - high, 0.0)]
    hs = HS // nd
    for d in range(nd):
        parts = [
            gst[d * rows : (d + 1) * rows],
            gpool[d * cr : (d + 1) * cr],
            gclass[d * cr : (d + 1) * cr],
            wider(wide[:, d * rows : (d + 1) * rows]),
            wider(nv[0:3, d * cr : (d + 1) * cr]),
            wider(quads[:, d * hs : (d + 1) * hs]),
            *table,
        ]
        parts = jnp.concatenate(parts, axis=0)
        out_ref[d, : parts.shape[0]] = parts
        if parts.shape[0] < out_ref.shape[1]:
            out_ref[d, parts.shape[0] :] = jnp.zeros((out_ref.shape[1] - parts.shape[0], 128), F32)


def body(
    hidden_in,
    cotangent,
    lengths,
    labels,
    qkv_weight,
    qv_bias,
    out_weight,
    out_bias,
    norm1_gain,
    norm1_bias,
    up_weight,
    up_bias,
    down_weight,
    down_bias,
    norm2_gain,
    norm2_bias,
    student_weight,
    student_bias,
    pool_query,
    pooler_weight,
    pooler_bias,
    class_weight,
    class_bias,
):
    nd = lax.axis_size("dp")
    me = lax.axis_index("dp")
    m = lax.axis_index("mp")
    c, y = m % 2, m // 2
    total, pd, _ = hidden_in.shape
    assert total == 2 * nd and lax.axis_size("mp") == 4
    hp = pd // 2
    half = nd * hp
    rows, cr = D // nd, CW // nd
    nh, nr = qv_bias.shape[0], up_bias.shape[0]
    hw, fw = nh * HS, nr * HS
    fast = nd == 8
    sizes = (rows, cr, nh, nr)
    seq = 2 * me + y
    length = lengths[seq]
    info = jnp.stack([me, c, y, labels[seq]]).astype(jnp.int32)

    def deal(x):
        x = x.reshape(nd, 2, 2, hp, D)
        x = lax.dynamic_slice(x, (0, y, c, 0, 0), (nd, 1, 1, hp, D)).reshape(nd, hp, D)
        return lax.all_to_all(x, "dp", 0, 0, tiled=True).reshape(half, D)

    def undeal(x):
        return lax.all_to_all(x.reshape(nd, hp, D), "dp", 0, 0, tiled=True)

    def place(a, b):
        one = pl.BlockSpec((1, hp, D), lambda d: (d, 0, 0))
        out = pl.pallas_call(
            place_kernel,
            grid=(nd,),
            in_specs=[SMEM] + [one] * 4,
            out_specs=pl.BlockSpec((1, 2, 2, hp, D), lambda d: (d, 0, 0, 0, 0)),
            out_shape=sds((nd, 2, 2, hp, D), BF),
            cost_estimate=cost(6_000_000),
            compiler_params=room(8),
            name="place",
        )(info, a, b, hop(a, 0, 1), hop(b, 0, 1))
        return out.reshape(total, pd, D)

    qo = jnp.concatenate([jnp.transpose(qkv_weight, (1, 0, 2)).reshape(rows, 3 * hw), out_weight.T], axis=1)
    if fast:
        vectors = [qv_bias]
        vectors += [v[None] for v in (out_bias, norm1_gain, norm1_bias, down_bias, norm2_gain, norm2_bias)]
        vectors += [v[None] for v in (student_bias, pool_query, pooler_bias)]
        vectors = [jnp.pad(v, ((0, 0), (0, 128 - v.shape[1]))) for v in vectors]
        vectors = jnp.concatenate([*vectors, jnp.zeros((7 - nh, 128), BF)], axis=0)
        qo = jnp.concatenate([qo, jnp.pad(vectors, ((0, 0), (0, D - 128)))], axis=0)
    qo_got = gather_lines(qo[None])
    qo_line = join_lines(qo_got)
    tokens = deal(after(hidden_in, qo_got[1:]))
    w_qo = gather_planes(qo_line, fast)
    w_qo = (w_qo[:2], w_qo[2:]) if fast else (w_qo[:1], w_qo[1:])
    up_pack, down_pack = up_weight, down_weight.T
    if fast:
        row = jnp.pad(up_bias.reshape(1, -1), ((0, 7), (0, D - up_bias.size)))
        cls = lanes(class_weight)
        more = jnp.concatenate([pooler_weight[:8], pooler_weight[8:], cls[:8], cls[8:]], axis=1)
        more = jnp.pad(more, ((0, 0), (0, D - 512)))
        up_pack = jnp.concatenate([up_pack, row, more], axis=0)
        more = jnp.concatenate([student_weight[16 * i : 16 * i + 16] for i in range(6)], axis=1)
        down_pack = jnp.concatenate([down_pack, more], axis=0)
    f_line, f_got = gather_doubling(after(jnp.stack([up_pack, down_pack]), qo_got[1:]))
    class_b = lanes(class_bias.astype(F32))
    cot = deal(after(cotangent, f_got))

    index = jnp.arange(half, dtype=jnp.int32)
    position = (index // hp) * pd + index % hp
    position = jnp.concatenate([position + c * hp, position + (1 - c) * hp])
    col = jnp.arange(128, dtype=jnp.int32)[None, :]
    aux = jnp.where(
        col == 0, jnp.where(position < length, 0.0, NEGATIVE)[:, None], jnp.where(col <= 3, 1.0, 0.0)
    ).astype(BF)
    aux_own = aux[:half]

    sib = hop(after(tokens, w_qo, f_got[0]), 0, 1)
    n = 2 * half
    biases = [aux, aux]
    if not fast:
        piece = jnp.broadcast_to(qv_bias[None], (nd, *qv_bias.shape))
        piece = lax.all_to_all(piece, "dp", 0, 0, tiled=True)
        piece = jnp.transpose(piece, (1, 0, 2)).reshape(nh, 2 * HS)
        piece = jnp.pad(piece, ((0, 16 - nh), (0, 0)))
        biases = [piece, hop(piece, 0, 2)]
    proj0, w0, ctx0, lse0 = attn_fwd(nh, info, tokens, sib, biases[0], aux, w_qo[0])
    if fast:
        wide, narrow = call(
            functools.partial(vectors_kernel, sizes),
            [sds((8, D)), sds((8, CW))],
            [info, *w_qo[0]],
            [SMEM, ANY, ANY],
            [pltpu.VMEM((nd, 16, D), BF), pltpu.SemaphoreType.DMA((nd,))],
            "vectors",
        )
        bias_near = bias_far = aux
    else:
        small = jnp.concatenate(
            [student_weight, pooler_weight]
            + [
                lanes(v)
                for v in (
                    class_weight,
                    out_bias,
                    norm1_gain,
                    norm1_bias,
                    down_bias,
                    norm2_gain,
                    norm2_bias,
                    student_bias,
                    pool_query,
                    pooler_bias,
                    qv_bias,
                    up_bias,
                )
            ],
            axis=0,
        )
        small = jnp.pad(small, ((0, -small.shape[0] % 16), (0, 0)))
        small = lax.all_to_all(jnp.broadcast_to(small[None], (nd, *small.shape)), "dp", 0, 0, tiled=True)
        student_w, pooler_f, class_f, wide, narrow, bias_near = call(
            functools.partial(unpack_kernel, sizes),
            [sds((D, CW), BF), sds((CW, CW)), sds((CW, CW)), sds((8, D)), sds((8, CW)), sds((16, 128))],
            [small],
            name="unpack",
        )
        bias_near = bias_near.astype(BF)
        bias_far = hop(bias_near, 0, 2)
    proj1, w1, ctx1, lse1 = attn_fwd(nh, info, tokens, sib, biases[1], after(aux, ctx0), w_qo[1])
    w_ffn = gather_planes(f_line, fast)

    if fast:
            ctx1 = after(ctx1, wide)

    def out(first, kind):
        return call(
            functools.partial(out_kernel, first), [sds((half, D), kind)], [ctx0, ctx1, w0, w1], name="out"
        )[0]

    att_got = hop(out(half, BF), 0, 1)
    att_part = out(0, F32)
    first, first_low, n1, s1, sq1 = by_rows(
        ln1_kernel,
        [sds((half, D)), sds((half, D), BF), sds((half, D)), sds((half, 1))],
        [sds((1, 128))],
        [att_part, att_got, tokens, aux_own],
        [wide],
        name="ln1",
    )
    first_sib = hop(after(first_low, w_ffn, cot), 0, 1)

    if fast:
        student_w, pooler_f, class_f = call(
            matrices_kernel,
            [sds((D, CW), BF), sds((CW, CW)), sds((CW, CW))],
            [info, *w_ffn[:2]],
            [SMEM, ANY, ANY],
            [pltpu.VMEM((nd, 16, D), BF)] * 2 + [pltpu.SemaphoreType.DMA((2, nd))],
            "matrices",
        )

    def ffn_up(x):
        return call(
            functools.partial(ffn_up_kernel, nh, nr),
            [sds((half, 2 * fw), BF), sds((half, 2 * fw), BF)],
            [info, x, bias_near, bias_far, *w_ffn],
            [SMEM] + [None] * 3 + [ANY] * len(w_ffn),
            weight_scratch(w_ffn)
            + [pltpu.VMEM((max(nd, 8), 8, D), BF)] * 2
            + [pltpu.SemaphoreType.DMA((nd,))],
            "ffn_up",
        )

    def product(a, k, kind):
        return call(
            functools.partial(product_kernel, k),
            [sds((half, D), kind)],
            [info, a, *w_ffn],
            [SMEM, None] + [ANY] * len(w_ffn),
            weight_scratch(w_ffn),
            "product",
        )[0]

    act, slope = ffn_up(first_low)
    act_sib, slope_sib = ffn_up(after(first_sib, act))
    ffn_got = hop(product(act_sib, 1, BF), 0, 1)
    ffn_part = product(act, 1, F32)
    second_low, n2, s2, student, pool_logit, stat = by_rows(
        ln2_kernel,
        [sds((half, D), BF), sds((half, D)), sds((half, 1)), sds((half, CW)), sds((half, CW))],
        [sds((8, 128))],
        [ffn_part, ffn_got, first, aux_own],
        [wide, narrow, student_w],
        name="ln2",
    )
    hidden_a = undeal(second_low)
    hidden_b = hop(hidden_a, 0, 2)

    dr2, dffn, g_st, g_pool, g_class, report, vec2, nvec, _ = by_rows(
        head_kernel,
        [sds((half, D)), sds((half, D), BF)],
        [
            sds((D, CW)),
            sds((CW, CW)),
            sds((CW, CW)),
            sds((8, 128)),
            sds((8, D)),
            sds((8, CW)),
            sds((8, 128)),
        ],
        [student, pool_logit, second_low, cot, n2, s2],
        [stat, hop(stat, 0, 1), sq1, pooler_f, class_f, class_b, narrow, student_w, wide],
        info,
        "head",
    )
    dffn_sib = hop(dffn, 0, 1)

    def ffn_back(g, s):
        return call(
            ffn_back_kernel,
            [sds((half, 2 * fw), BF), sds((8, 2 * fw))],
            [info, g, s, *w_ffn],
            [SMEM, None, None] + [ANY] * len(w_ffn),
            weight_scratch(w_ffn),
            "ffn_back",
        )

    dpre, ub0 = ffn_back(dffn, slope)
    dpre_sib, ub1 = ffn_back(after(dffn_sib, dpre, hidden_a), slope_sib)
    dfirst_got = hop(product(dpre_sib, 0, BF), 0, 1)
    dfirst_part = product(dpre, 0, F32)
    f_grads = call(
        ffn_grad_kernel,
        grad_outs(2, 2, nd, rows, fast),
        [info, first_low, first_sib, dpre, dpre_sib, dffn, dffn_sib, act, act_sib],
        [SMEM] + [None] * 8,
        [pltpu.VMEM((D, D), F32)],
        "ffn_grad",
    )
    dr1, dattn, vec1 = by_rows(
        ln1_back_kernel,
        [sds((half, D)), sds((half, D), BF)],
        [sds((8, D))],
        [dfirst_part, dfirst_got, after(dr2, hidden_b), n1, s1],
        [wide],
        name="ln1_back",
    )
    dattn_sib = hop(dattn, 0, 1)
    dattn_sib = after(dattn_sib, f_grads, hidden_b)
    if fast:
        up_keep, up_send, down_keep, down_send = f_grads
        up_got, down_got = hop(up_send, 0, 2), hop(down_send, 1, 0)
    count = rows + 2 * cr + 9 + 4 * nr + 2 * total
    (small_g,) = call(
        functools.partial(pack_grads_kernel, sizes),
        [sds((nd, count + -count % 16, 128))],
        [info, g_st, g_pool, g_class, vec1, vec2, nvec, ub0, ub1, report],
        [SMEM] + [None] * 9,
        name="pack",
    )
    small_g = small_g + hop(small_g.astype(BF), 0, 1).astype(F32)
    small_y = small_g + hop(small_g.astype(BF), 0, 2).astype(F32)


    def qkv_grad(g, ctx, sums):
        return call(
            functools.partial(qkv_grad_kernel, nh),
            grad_outs(1, 1, nd, rows, fast, 8),
            [info, tokens, sib, g, dattn, dattn_sib, ctx, sums],
            [SMEM] + [None] * 7,
            [pltpu.VMEM((D, D), F32), pltpu.VMEM((max(8, nd), 128), F32)],
            "qkv_grad",
        )

    g1, g1_sum = attn_bwd(nh, proj1, w1, aux, ctx1, dattn, after(dattn_sib, small_y), lse1)
    far_grad = qkv_grad(g1, ctx1, g1_sum)
    if fast:
        far_got = [hop(g, 0, 2) for g in far_grad]
    g0, g0_sum = attn_bwd(
        nh, proj0, w0, aux, ctx0, dattn, after(dattn_sib, g1, far_grad), lse0
    )
    if fast:
        g0, up_got, down_got = lax.optimization_barrier((g0, up_got, down_got))
    tok_send, tok_own = call(
        token_grad_kernel, [sds((half, D), BF), sds((half, D))], [g0, g1, w0, w1, dr1], name="token_grad"
    )
    near_grad = qkv_grad(g0, ctx0, g0_sum)
    tok_sum = after((tok_own + hop(tok_send, 0, 1).astype(F32)).astype(BF), near_grad)
    input_a = undeal(tok_sum)
    if fast:
        block_ = (nd // 2, rows, D)
        f_keep, up_half, down_half = call(
            sum_half_kernel,
            [sds((2, *block_), BF), sds(block_, BF), sds(block_, BF)],
            [up_keep, up_got, down_keep, down_got],
            name="grad_half",
        )
        f_sums = call(
            sum_last_kernel,
            [sds((2, rows, D))] + [sds((2, rows, D), BF)] * (nd // 2 - 1),
            [f_keep, hop(up_half, 1, 0), hop(down_half, 0, 2)],
            name="grad_sum",
        )
        f_sum = finish_lines(f_sums)
        near_part = (near_grad[1].astype(F32) + far_got[1].astype(F32)).astype(BF)
        qo_own = (near_grad[0], far_got[0], hop(near_part, 1, 0))
    else:
        qo_own = ()
        f_sums = f_sum = sum_lines(f_grads)
    hidden_out = place(hidden_a, hidden_b)
    input_b = hop(after(input_a, hidden_out, f_sums, qo_own[1:]), 0, 2)
    small_g = lax.all_to_all(after(small_y.astype(BF), input_b), "dp", 0, 0, tiled=True).astype(F32).sum(0)
    input_grad = place(input_a, input_b)
    up_sum, down_sum = f_sum
    if fast:
        qo_sum = finish_lines(sum_blocks(qo_own))[0]
    else:
        qo_sum = sum_lines([*near_grad, *far_grad])[0]

    width = 2 * HS // nd
    if fast:
        g_qv = qo_sum[rows, : nh * width].reshape(nh, width)
        qo_sum = qo_sum[:rows]
    else:
        g_qv = [
            jnp.concatenate([g[0, :hw].reshape(nh, HS), g[0, 2 * hw : 3 * hw].reshape(nh, HS)], axis=1)
            for g in (g0_sum, g1_sum)
        ]
        g_qv = g_qv[0] + hop(g_qv[1], 0, 2)
        bit = 1
        while bit < nd:
            g_qv = g_qv + hop(g_qv, bit, 0)
            bit *= 2
        g_qv = lax.dynamic_slice(g_qv, (0, width * me), (nh, width))

    at = rows + 2 * cr + 9 + 4 * nr
    table = small_g[at : at + total] + small_g[at + total : at + 2 * total]
    logit_all = table[:, :CLASSES]
    class_bias_grad = jnp.sum(table[:, CLASSES : 2 * CLASSES], 0)
    squares = jnp.sum(table[:, 2 * CLASSES : 2 * CLASSES + 8], 0).reshape(2, 4).sum(0)
    rms = jnp.sqrt(squares / (jnp.sum(lengths).astype(F32) * D))

    at = rows + 2 * cr
    g_wide = small_g[at : at + 6, :rows]
    g_narrow = small_g[at + 6 : at + 9, :cr]
    g_ub = lax.dynamic_slice(small_g, (at + 9 + nr * m, 0), (nr, HS // nd))
    return (
        hidden_out,
        logit_all,
        input_grad,
        jnp.transpose(qo_sum[:, : 3 * hw].reshape(rows, 3, hw), (1, 0, 2)),
        g_qv,
        qo_sum[:, 3 * hw :].T,
        g_wide[0],
        g_wide[1],
        g_wide[2],
        up_sum,
        g_ub,
        down_sum.T,
        g_wide[3],
        g_wide[4],
        g_wide[5],
        small_g[:rows],
        g_narrow[0],
        g_narrow[1],
        small_g[rows : rows + cr],
        g_narrow[2],
        small_g[rows + cr : at, :CLASSES],
        class_bias_grad,
        rms,
    )


def solution(mesh):
    rows = P(None, "dp", None)
    vec = P("dp")
    return jax.shard_map(
        body,
        mesh=mesh,
        in_specs=(
            rows,
            rows,
            P(),
            P(),
            P(None, "dp", "mp"),
            P("mp", "dp"),
            P("mp", "dp"),
            vec,
            vec,
            vec,
            P("dp", "mp"),
            P("mp", "dp"),
            P("mp", "dp"),
            vec,
            vec,
            vec,
            P("dp", None),
            vec,
            vec,
            P("dp", None),
            vec,
            P("dp", None),
            P(),
        ),
        out_specs=(
            rows,
            P(),
            rows,
            P(None, "dp", "mp"),
            P("mp", "dp"),
            P("mp", "dp"),
            vec,
            vec,
            vec,
            P("dp", "mp"),
            P("mp", "dp"),
            P("mp", "dp"),
            vec,
            vec,
            vec,
            P("dp", None),
            vec,
            vec,
            P("dp", None),
            vec,
            P("dp", None),
            P(),
            P(),
        ),
        check_vma=False,
    )
```

```python
import functools

import jax
import jax.numpy as jnp
import numpy as np
from jax import lax
from jax.experimental import pallas as pl
from jax.experimental.pallas import tpu as pltpu
from jax.sharding import PartitionSpec as P

D = 768
HS = 64
CW = 128
PH = 2
CLASSES = 14
EPSILON = 1e-06
NEGATIVE = -1e30
LOG2E = 1.4426950408889634
HIGHEST = lax.Precision.HIGHEST
BF = jnp.bfloat16
F32 = jnp.float32
AXES = ("dp", "mp")
QB = 512
RB = 128
SLOW = 1
ROOM = 16
ROOMS = {'product': 60, 'ffn_back': 60}


def dot(a, b, ca, cb):
    return lax.dot_general(a, b, (((ca,), (cb,)), ((), ())), preferred_element_type=F32)


def hop(x, dbit, mbit):
    nd, nm = lax.axis_size("dp"), lax.axis_size("mp")
    pairs = [(d * nm + m, (d ^ dbit) * nm + (m ^ mbit)) for d in range(nd) for m in range(nm)]
    return lax.ppermute(x, AXES, pairs)


def after(x, *others):
    return lax.optimization_barrier((x, *others))[0]


def bit_groups(nd):
    bits = []
    b = nd // 2
    while b > 1:
        bits.append(b)
        b //= 2
    groups = [bits[i : i + 2] for i in range(0, len(bits), 2)]
    out = []
    for g in groups:
        out.append([0, g[0]] if len(g) == 1 else [0, g[1], g[0], g[0] + g[1]])
    return out


def gather_chips(x):
    nd = lax.axis_size("dp")
    cur = x[None]
    for masks in bit_groups(nd):
        parts = [cur] + [hop(cur, k, 0) for k in masks[1:]]
        cur = jnp.stack(parts, 1).reshape(-1, *x.shape)
    near, far = (hop(cur, 1, 0), hop(cur, 0, 2))
    far2 = hop(cur, 1, 2)
    return (
        jnp.stack([cur, near], 1).reshape(nd, *x.shape),
        jnp.stack([far, far2], 1).reshape(nd, *x.shape),
    )


def scatter_chips(mine, other):
    nd = lax.axis_size("dp")
    tail = mine.shape[1:]
    a = mine.reshape(nd // 2, 2, *tail)
    b = other.reshape(nd // 2, 2, *tail)
    cur = (
        a[:, 0].astype(F32)
        + hop(a[:, 1], 1, 0).astype(F32)
        + hop(b[:, 0], 0, 2).astype(F32)
        + hop(b[:, 1], 1, 2).astype(F32)
    )
    for masks in reversed(bit_groups(nd)):
        low = cur.astype(BF).reshape(-1, len(masks), *tail)
        full = cur.reshape(-1, len(masks), *tail)
        cur = full[:, 0]
        for i, k in enumerate(masks[1:], 1):
            cur = cur + hop(low[:, i], k, 0).astype(F32)
    return cur[0]


def relative(x, me):
    return jnp.take(x, jnp.arange(x.shape[0], dtype=jnp.int32) ^ me, axis=0)


def split3(x):
    a = x.astype(BF)
    r = x - a.astype(F32)
    b = r.astype(BF)
    return a, b, (r - b.astype(F32)).astype(BF)


def swap64(x):
    return jnp.concatenate([x[:, 64:], x[:, :64]], axis=1)


def doubled(kp, head):
    lane = lax.broadcasted_iota(jnp.int32, kp.shape, 1)
    kr = swap64(kp)
    return jnp.where(lane < 64, kp, kr) if head == 0 else jnp.where(lane < 64, kr, kp)


ANY = pl.BlockSpec(memory_space=pl.ANY)
SMEM = pl.BlockSpec(memory_space=pltpu.SMEM)


def room(mib):
    return pltpu.CompilerParams(vmem_limit_bytes=mib << 20)


def call(kernel, outs, args, specs=None, scratch=(), name=None, flops=0, mib=ROOM):
    specs = [pl.BlockSpec(memory_space=pltpu.VMEM) if s is None else s for s in (specs or [None] * len(args))]
    size = sum(a.size * a.dtype.itemsize for a in args) + sum(
        int(np.prod(o.shape)) * np.dtype(o.dtype).itemsize for o in outs
    )
    return pl.pallas_call(
        kernel,
        in_specs=specs,
        out_specs=[pl.BlockSpec(memory_space=pltpu.VMEM)] * len(outs),
        out_shape=outs,
        scratch_shapes=list(scratch),
        cost_estimate=cost(size, flops),
        compiler_params=room(ROOMS.get(name, ROOM)),
        name=name,
    )(*args)


def cost(size, flops=0):
    return pl.CostEstimate(flops=int(flops) // SLOW, bytes_accessed=int(size) // SLOW, transcendentals=0)


def sds(shape, dtype=F32):
    return jax.ShapeDtypeStruct(shape, dtype)


def by_rows(kernel, outs, sums, args, consts, info=None, name=None):
    n = args[0].shape[0]

    def cut(a):
        return pl.BlockSpec((RB, a.shape[1]), lambda i: (i, 0))

    def whole(a):
        return pl.BlockSpec(a.shape, lambda i: (0,) * len(a.shape))

    head = [] if info is None else [info]
    size = sum(a.size * a.dtype.itemsize for a in [*args, *consts])
    return pl.pallas_call(
        kernel,
        grid=(n // RB,),
        in_specs=[SMEM] * len(head) + [cut(a) for a in args] + [whole(a) for a in consts],
        out_specs=[cut(o) for o in outs] + [whole(o) for o in sums],
        out_shape=[*outs, *sums],
        cost_estimate=cost(size),
        compiler_params=room(60),
        name=name,
    )(*head, *args, *consts)


def start_sums(*refs):
    @pl.when(pl.program_id(0) == 0)
    def _():
        for r in refs:
            r[...] = jnp.zeros(r.shape, F32)


def start(copies):
    for cp in copies:
        cp.start()
    return copies


def load_pair(info, arrays, w_ref, sems):
    if len(arrays) == 1:
        return start([pltpu.make_async_copy(arrays[0].at[0], w_ref, sems.at[0])])
    nz = arrays[0].shape[1]
    rows = D // (2 * nz)
    copies = []
    for x, a in enumerate(arrays):
        for z in range(nz):
            at = pl.multiple_of((info[0] ^ (2 * z + x)) * rows, 16)
            copies.append(
                pltpu.make_async_copy(a.at[0, z, pl.ds(0, rows), :], w_ref.at[pl.ds(at, rows), :], sems.at[len(copies)])
            )
    return start(copies)


def load_rows(info, arrays, k, b_ref, sems):
    nz = arrays[0].shape[1]
    rows = D // (2 * nz)
    copies = []
    for x, a in enumerate(arrays):
        for z in range(nz):
            copies.append(
                pltpu.make_async_copy(
                    a.at[k, z, pl.ds(rows, b_ref.shape[1]), :], b_ref.at[info[0] ^ (2 * z + x)], sems.at[len(copies)]
                )
            )
    return start(copies)


def load_weight(info, arrays, k, w_ref, sems):
    if len(arrays) == 2:
        return start([pltpu.make_async_copy(a.at[k], w_ref.at[i], sems.at[i]) for i, a in enumerate(arrays)])
    nz = arrays[0].shape[1]
    rows = D // (2 * nz)
    copies = []
    for i, a in enumerate(arrays):
        for z in range(nz):
            at = pl.multiple_of((info[0] ^ (2 * z + i % 2)) * rows, 16)
            copies.append(
                pltpu.make_async_copy(
                    a.at[k, z, pl.ds(0, rows), :], w_ref.at[i // 2, pl.ds(at, rows), :], sems.at[len(copies)]
                )
            )
    return start(copies)


def wait(copies):
    for cp in copies:
        cp.wait()


def weight_scratch(arrays):
    count = len(arrays) if len(arrays) == 2 else 4 * arrays[0].shape[1]
    return [pltpu.VMEM((2, D, arrays[0].shape[-1]), BF), pltpu.SemaphoreType.DMA((count,))]


def gather_lines(local):
    k, rows, n = local.shape
    cur = local[:, None]
    *groups, last = bit_groups(lax.axis_size("dp"))
    for masks in groups:
        parts = [cur] + [hop(cur, b, 0) for b in masks[1:]]
        cur = jnp.stack(parts, 2).reshape(k, -1, rows, n)
    return [cur] + [hop(cur, b, 0) for b in last[1:]]


def gather_doubling(local, *others):
    k, rows, n = local.shape
    cur, got = local[:, None], []
    bit = lax.axis_size("dp") // 2
    while bit > 1:
        got.append(hop(cur, bit, 0))
        cur = jnp.stack([cur, got[-1]], 2).reshape(k, -1, rows, n)
        bit //= 2
    return cur, got


def join_lines(parts):
    k, _, rows, n = parts[0].shape
    return jnp.stack(parts, 2).reshape(k, -1, rows, n)


def gather_planes(cur, fast):
    near, far, far2 = hop(cur, 1, 0), hop(cur, 0, 2), hop(cur, 1, 2)
    if fast:
        return cur, near, far, far2
    me = lax.axis_index("dp")
    k, half, rows, n = cur.shape

    def ordered(a, b):
        both = jnp.stack([a, b], 2).reshape(k, 2 * half, rows, n)
        return jnp.moveaxis(relative(jnp.moveaxis(both, 1, 0), me), 0, 1).reshape(k, 2 * half * rows, n)

    return ordered(cur, near), ordered(far, far2)


def spread(info, g_ref, k, outs):
    nz = outs[0].shape[1]
    rows = D // (2 * nz)
    for z in range(nz):
        for x in range(2):
            at = pl.multiple_of((info[0] ^ (2 * z + x)) * rows, 8)
            outs[x][k, z, :rows] = g_ref[pl.ds(at, rows), :].astype(BF)


def grad_outs(k, ys, nd, rows, fast, more=0):
    return [sds((k, nd // 2, rows + more, D), BF)] * (2 * ys) if fast else [sds((k, D, D), BF)] * ys


def store_grad(info, k, y, g, g_ref, outs):
    if len(outs[0].shape) == 4:
        g_ref[...] = g
        spread(info, g_ref, k, outs[2 * y : 2 * y + 2])
    else:
        outs[y][k] = g.astype(BF)


def sum_first_kernel(count, *refs):
    parts, (keep_ref, *send_refs) = refs[:count], refs[count:]
    for k in range(parts[0].shape[0]):
        for z in range(parts[0].shape[1]):
            total = parts[0][k, z].astype(F32)
            for r in parts[1:]:
                total = total + r[k, z].astype(F32)
            if z == 0:
                keep_ref[k] = total
            else:
                send_refs[z - 1][k] = total.astype(BF)


def sum_planes(parts):
    if len(parts) == 2:
        return list(parts)
    keep, x, y, xy = parts
    return [keep, hop(x, 1, 0), hop(y, 0, 2), hop(xy, 1, 2)]


def sum_lines(parts):
    nd = lax.axis_size("dp")
    if len(parts) == 2:
        me = lax.axis_index("dp")
        k = parts[0].shape[0]
        near, far = (
            relative(jnp.moveaxis(p.reshape(k, nd, D // nd, D), 0, 1), me) for p in parts
        )
        return scatter_chips(near, far)
    return finish_lines(sum_blocks(parts))


def sum_blocks(parts):
    if len(parts) == 2:
        return parts
    k, nz, rows, n = parts[0].shape
    return call(
        functools.partial(sum_first_kernel, len(parts)),
        [sds((k, rows, n))] + [sds((k, rows, n), BF)] * (nz - 1),
        list(parts),
        name="grad_sum",
    )


def finish_lines(sums):
    own, low, *high = sums
    if len(high) != 2:
        for z, piece in enumerate([low, *high], 1):
            own = own + hop(piece, 2 * z, 0).astype(F32)
        return own
    got = hop(jnp.stack([low, high[1]]), 2, 0)
    send = (high[0].astype(F32) + got[1].astype(F32)).astype(BF)
    return own + got[0].astype(F32) + hop(send, 4, 0).astype(F32)


def bias_rows(b, first, count, low, high):
    return jnp.concatenate([b[first + i : first + i + 1, low:high] for i in range(count)], axis=1)


def block(ref, i):
    return ref[:, 128 * i : 128 * i + 128]


def attn_fwd_kernel(nh, info, own_ref, sib_ref, bias_ref, aux_ref, *rest):
    *arrays, proj_ref, w_ref, ctx_ref, lse_ref, w_sems, o_ref, b_ref, b_sems = rest
    copies = load_pair(info, arrays, w_ref, w_sems)
    hw = nh * HS
    if len(arrays) == 2:
        wait(load_rows(info, arrays, 0, b_ref, b_sems))
        nd = b_ref.shape[0]
        w = 2 * HS // nd

        def bias_part(first):
            return [b_ref[a, h : h + 1, :w] for h in range(nh) for a in range(first, first + nd // 2)]

        q_part, v_part = (
            jnp.concatenate(bias_part(a), axis=1).astype(F32) for a in (0, nd // 2)
        )
    else:
        bias = bias_ref[...].astype(F32)
        q_part = bias_rows(bias, 0, nh, 0, HS)
        v_part = bias_rows(bias, 0, nh, HS, 2 * HS)
    row_bias = jnp.concatenate([q_part, jnp.zeros((1, hw), F32), v_part, jnp.zeros((1, HS), F32)], axis=1)
    wait(copies)
    half = own_ref.shape[0]
    n = 2 * half
    for i, ref in enumerate((own_ref, sib_ref)):
        for j in range(2):
            r = slice(j * half // 2, (j + 1) * half // 2)
            out = dot(ref[r], w_ref[:, : 10 * HS], 1, 0) + row_bias
            proj_ref[i * half + r.start : i * half + r.stop] = out.astype(BF)
    qt = [jnp.transpose(block(proj_ref, i).astype(F32)) * (HS**-0.5 * LOG2E) for i in (0, 1)]
    hi = [q.astype(BF) for q in qt]
    lo = [(q - h.astype(F32)).astype(BF) for q, h in zip(qt, hi)]
    vt = [jnp.transpose(block(proj_ref, i).astype(F32)).astype(BF) for i in (3, 4)]
    row = lax.broadcasted_iota(jnp.int32, (128, QB), 0)
    auxq = jnp.where(row == 0, 1.0, 0.0).astype(BF)
    o_ref[0:HS] = jnp.zeros((HS, n), F32)
    lse_ref[...] = jnp.zeros(lse_ref.shape, F32)
    for h in range(nh):
        kb, kh = ((1, 1), (2, 0), (2, 1))[h]
        lhs = jnp.concatenate([doubled(block(proj_ref, kb), kh), aux_ref[...]], axis=1)
        i, r = h // 2, slice(64 * (h % 2), 64 * (h % 2) + 64)
        vaug = jnp.concatenate([vt[i][r], jnp.ones((16, n), BF)], axis=0)
        to = slice(64 * h + 64, 64 * h + 128)
        for b in range(n // QB):
            s = slice(b * QB, b * QB + QB)
            rhs = jnp.concatenate([hi[i][r, s], lo[i][r, s], auxq], axis=0)
            sc = dot(lhs, rhs, 1, 0)
            m = jnp.max(sc, axis=0, keepdims=True)
            p = jnp.exp2(sc - m).astype(BF)
            o = dot(vaug, p, 1, 0)
            total = o[64:65]
            o_ref[to, s] = o[:64] / total
            lse_ref[h : h + 1, s] = m + jnp.log2(total)
    for j in range(2):
        ctx_ref[:, 128 * j : 128 * j + 128] = jnp.transpose(o_ref[128 * j : 128 * j + 128]).astype(BF)


def attn_fwd(nh, info, own, sib, bias, aux, arrays):
    n = 2 * own.shape[0]
    count = len(arrays) * arrays[0].shape[1] if len(arrays) == 2 else 1
    return call(
        functools.partial(attn_fwd_kernel, nh),
        [sds((n, 10 * HS), BF), sds((D, D), BF), sds((n, 4 * HS), BF), sds((8, n))],
        [info, own, sib, bias, aux, *arrays],
        [SMEM] + [None] * 4 + [ANY] * len(arrays),
        [
            pltpu.SemaphoreType.DMA((count,)),
            pltpu.VMEM((4 * HS, n), F32),
            pltpu.VMEM((count, 16, D), BF),
            pltpu.SemaphoreType.DMA((count,)),
        ],
        "attn_fwd",
        flops=11_000_000_000,
    )


def out_kernel(first, c0_ref, c1_ref, w0_ref, w1_ref, out_ref):
    rows, cols = slice(first, first + out_ref.shape[0]), slice(8 * HS, 12 * HS)
    part = dot(c0_ref[rows], w0_ref[:, cols], 1, 1) + dot(c1_ref[rows], w1_ref[:, cols], 1, 1)
    out_ref[...] = part.astype(out_ref.dtype)


def norm(values, gain, shift):
    center = values - jnp.mean(values, -1, keepdims=True)
    spread_ = jnp.mean(center * center, -1, keepdims=True)
    scale = lax.rsqrt(spread_ + EPSILON)
    normed = center * scale
    return normed * gain + shift, normed, scale


def live_rows(aux_ref):
    return jnp.where(aux_ref[:, 0:1].astype(F32) > -1.0, 1.0, 0.0)


def square(live, v):
    return jnp.sum(jnp.sum(v * v, -1, keepdims=True) * live, axis=0, keepdims=True)


def ln1_kernel(part_ref, got_ref, tok_ref, aux_ref, wide_ref, first_ref, low_ref, n_ref, s_ref, sq_ref):
    start_sums(sq_ref)
    tok = tok_ref[...].astype(F32)
    att = part_ref[...] + got_ref[...].astype(F32) + wide_ref[0:1]
    first, normed, scale = norm(tok + att, wide_ref[1:2], wide_ref[2:3])
    first_ref[...] = first
    low_ref[...] = first.astype(BF)
    n_ref[...] = normed
    s_ref[...] = scale
    live = live_rows(aux_ref)
    lane = lax.broadcasted_iota(jnp.int32, (1, 128), 1)
    out = jnp.zeros((1, 128), F32)
    for i, v in enumerate((tok, att, first)):
        out = jnp.where(lane == i, square(live, v), out)
    sq_ref[...] += out


def hidden_bias(b_ref, nr):
    nd = b_ref.shape[0]
    w = HS // nd
    first = jnp.concatenate([b_ref[a, 0:1, :128] for a in range(nd)], axis=0)
    i = lax.broadcasted_iota(jnp.int32, (128, nr * HS), 0)
    f = lax.broadcasted_iota(jnp.int32, (128, nr * HS), 1)
    place = jnp.where(i == (f // HS) * w + f % w, 1.0, 0.0).astype(BF)
    spread_ = dot(first, place, 1, 0)
    a = lax.broadcasted_iota(jnp.int32, (nd, nr * HS), 0)
    f = lax.broadcasted_iota(jnp.int32, (nd, nr * HS), 1)
    return jnp.sum(jnp.where((f % HS) // w == a, spread_, 0.0), axis=0, keepdims=True)


def ffn_up_kernel(nh, nr, info, x_ref, b0_ref, b1_ref, *rest):
    *up, act_ref, slope_ref, up_ref, sems, r0_ref, r1_ref, r_sems = rest
    copies = load_weight(info, up, 0, up_ref, sems)
    fw = nr * HS
    x = x_ref[...]
    if len(up) == 4:
        for i, r_ref in enumerate((r0_ref, r1_ref)):
            wait(load_rows(info, up[2 * i : 2 * i + 2], 0, r_ref, r_sems))
        biases = [hidden_bias(r_ref, nr) for r_ref in (r0_ref, r1_ref)]
    else:
        biases = [bias_rows(b_ref[...].astype(F32), nh, nr, 0, HS) for b_ref in (b0_ref, b1_ref)]
    wait(copies)
    for y in range(2):
        for j in range(fw // 256):
            s = slice(j * 256, (j + 1) * 256)
            t = slice(y * fw + j * 256, y * fw + (j + 1) * 256)
            pre = dot(x, up_ref[y, :, s], 1, 0) + biases[y][:, s]
            phi = 0.5 + 0.5 * lax.erf(pre * (0.5**0.5))
            act_ref[:, t] = (pre * phi).astype(BF)
            slope_ref[:, t] = (phi + pre * (jnp.exp(-0.5 * pre * pre) * (2 * np.pi) ** -0.5)).astype(BF)


def product_kernel(k, info, a_ref, *rest):
    *w, out_ref, w_ref, sems = rest
    wait(load_weight(info, w, k, w_ref, sems))
    fw = w_ref.shape[2]
    out_ref[...] = (dot(a_ref[:, :fw], w_ref[0], 1, 1) + dot(a_ref[:, fw:], w_ref[1], 1, 1)).astype(out_ref.dtype)


def head_ones():
    a = lax.broadcasted_iota(jnp.int32, (CW, CW), 0) // (CW // PH)
    b = lax.broadcasted_iota(jnp.int32, (CW, CW), 1) // (CW // PH)
    return jnp.where(a == b, 1.0, 0.0)


def fdot(a, b, ca=1, cb=0):
    return lax.dot_general(a, b, (((ca,), (cb,)), ((), ())), precision=HIGHEST, preferred_element_type=F32)


def ln2_kernel(
    part_ref, got_ref, first_ref, aux_ref, wide_ref, narrow_ref, sw_ref, low_ref, n_ref, s_ref, st_ref, lg_ref, stat_ref
):
    feed = part_ref[...] + got_ref[...].astype(F32) + wide_ref[3:4]
    second, normed, scale = norm(first_ref[...] + feed, wide_ref[4:5], wide_ref[5:6])
    low = second.astype(BF)
    low_ref[...] = low
    n_ref[...] = normed
    s_ref[...] = scale
    student = dot(low, sw_ref[...], 1, 0) + narrow_ref[0:1]
    st_ref[...] = student
    live = live_rows(aux_ref)
    logit = fdot(student * narrow_ref[1:2], head_ones()) * (CW // PH) ** -0.5
    logit = jnp.where(live > 0.0, logit, NEGATIVE)
    lg_ref[...] = logit

    @pl.when(pl.program_id(0) == 0)
    def _():
        stat_ref[...] = jnp.zeros((8, 128), F32)
        stat_ref[0:1] = jnp.full((1, 128), NEGATIVE, F32)

    old = stat_ref[0:1]
    top = jnp.maximum(old, jnp.max(logit, axis=0, keepdims=True))
    shrink = jnp.exp(old - top)
    weight = jnp.where(live > 0.0, jnp.exp(logit - top), 0.0)
    stat_ref[0:1] = top
    stat_ref[1:2] = stat_ref[1:2] * shrink + jnp.sum(weight, axis=0, keepdims=True)
    stat_ref[2:3] = stat_ref[2:3] * shrink + jnp.sum(weight * student, axis=0, keepdims=True)
    stat_ref[3:4] += jnp.broadcast_to(square(live, feed), (1, 128))


def norm_back(up, normed, scale, gain):
    scaled = up * gain
    inner = scaled - jnp.mean(scaled, -1, keepdims=True) - normed * jnp.mean(scaled * normed, -1, keepdims=True)
    return inner * scale


def colsum(x):
    return jnp.sum(x, axis=0, keepdims=True)


def head_kernel(
    info,
    st_ref,
    lg_ref,
    low_ref,
    cot_ref,
    n_ref,
    s_ref,
    stat_ref,
    sib_ref,
    sq_ref,
    pooler_ref,
    class_ref,
    cb_ref,
    narrow_ref,
    sw_ref,
    wide_ref,
    dr2_ref,
    dffn_ref,
    gst_ref,
    gpool_ref,
    gclass_ref,
    rep_ref,
    vec_ref,
    nvec_ref,
    keep_ref,
):
    scale = (CW // PH) ** -0.5
    once = jnp.where(info[1] == 0, 1.0, 0.0)

    @pl.when(pl.program_id(0) == 0)
    def _():
        top, top2 = stat_ref[0:1], sib_ref[0:1]
        best = jnp.maximum(top, top2)
        fa, fb = jnp.exp(top - best), jnp.exp(top2 - best)
        whole = stat_ref[1:2] * fa + sib_ref[1:2] * fb
        pooled = (stat_ref[2:3] * fa + sib_ref[2:3] * fb) / whole
        pooled = jnp.broadcast_to(pooled, (8, CW))
        z = jnp.tanh(fdot(pooled, pooler_ref[...]) + narrow_ref[2:3])
        lane = lax.broadcasted_iota(jnp.int32, (8, 128), 1)
        row = lax.broadcasted_iota(jnp.int32, (8, 128), 0)
        logit = fdot(z, class_ref[...]) + cb_ref[...]
        masked = jnp.where(lane < CLASSES, logit, NEGATIVE)
        e = jnp.exp(masked - jnp.max(masked, axis=1, keepdims=True))
        dlogit = e / jnp.sum(e, axis=1, keepdims=True) - jnp.where(lane == info[3], 1.0, 0.0)
        only = jnp.where(row == 0, once, 0.0)
        gclass_ref[...] = fdot(z * only, dlogit, 0, 0)
        dz = fdot(dlogit, class_ref[...], 1, 1)
        dzp = dz * (1.0 - z * z)
        gpool_ref[...] = fdot(pooled * only, dzp, 0, 0)
        dpooled = fdot(dzp, pooler_ref[...], 1, 1)
        sq = jnp.where(lane[0:1] == 3, stat_ref[3:4] + sib_ref[3:4] * 0.0, sq_ref[...])
        sq = jnp.where(info[1] == 0, pltpu.roll(sq, 2 * CLASSES, 1), pltpu.roll(sq, 2 * CLASSES + 4, 1))
        rep = jnp.where(lane < CLASSES, logit, pltpu.roll(jnp.where(lane < CLASSES, dlogit, 0.0), CLASSES, 1)) * once
        rep_ref[...] = jnp.where(lane < 2 * CLASSES, rep, sq)
        nvec_ref[...] = jnp.zeros((8, CW), F32)
        nvec_ref[2:3] = dzp[0:1] * once
        vec_ref[...] = jnp.zeros((8, D), F32)
        gst_ref[...] = jnp.zeros((D, CW), F32)
        keep_ref[0:1] = best
        keep_ref[1:2] = whole
        keep_ref[2:3] = dpooled[0:1]
        keep_ref[3:4] = fdot(pooled * dpooled, head_ones())[0:1]

    student = st_ref[...]
    dp = keep_ref[2:3]
    logit = lg_ref[...]
    weight = jnp.where(logit > 0.5 * NEGATIVE, jnp.exp(logit - keep_ref[0:1]), 0.0) / keep_ref[1:2]
    dq = scale * weight * (fdot(student * dp, head_ones()) - keep_ref[3:4])
    dstudent = (weight * dp + dq * narrow_ref[1:2]).astype(BF)
    nvec_ref[0:1] += colsum(dstudent.astype(F32))
    nvec_ref[1:2] += colsum(dq * student)
    gst_ref[...] += dot(low_ref[...], dstudent, 0, 0)
    dsecond = dot(dstudent, sw_ref[...], 1, 1) + cot_ref[...].astype(F32)
    normed = n_ref[...]
    dr2 = norm_back(dsecond, normed, s_ref[...], wide_ref[4:5])
    dr2_ref[...] = dr2
    dffn_ref[...] = dr2.astype(BF)
    vec_ref[0:1] += colsum(dr2)
    vec_ref[1:2] += colsum(dsecond * normed)
    vec_ref[2:3] += colsum(dsecond)


def ffn_back_kernel(info, g_ref, slope_ref, *rest):
    *down, dpre_ref, ub_ref, w_ref, sems = rest
    copies = load_weight(info, down, 1, w_ref, sems)
    fw = w_ref.shape[2]
    g = g_ref[...]
    ub_ref[...] = jnp.zeros(ub_ref.shape, F32)
    wait(copies)
    for y in range(2):
        for j in range(fw // 256):
            s = slice(j * 256, (j + 1) * 256)
            t = slice(y * fw + j * 256, y * fw + (j + 1) * 256)
            dpre = (dot(g, w_ref[y, :, s], 1, 0) * slope_ref[:, t].astype(F32)).astype(BF)
            dpre_ref[:, t] = dpre
            ub_ref[0:1, t] = colsum(dpre.astype(F32))


def ffn_grad_kernel(info, first, first2, dpre, dpre2, dffn, dffn2, act, act2, *rest):
    *outs, g_ref = rest
    fw = dpre.shape[1] // 2
    for k, (a0, a1, b0, b1) in enumerate(((first, first2, dpre, dpre2), (dffn, dffn2, act, act2))):
        for y in range(2):
            s = slice(y * fw, (y + 1) * fw)
            g = dot(a0[...], b0[:, s], 0, 0) + dot(a1[...], b1[:, s], 0, 0)
            if len(outs) == 2:
                outs[y][k] = g.astype(BF)
                continue
            g_ref[...] = g
            nz = outs[0].shape[1]
            rows = D // (2 * nz)
            for z in range(nz):
                for x in range(2):
                    at = pl.multiple_of((info[0] ^ (2 * z + x)) * rows, 8)
                    piece = g_ref[pl.ds(at, rows), :].astype(BF)
                    if k == 0:
                        outs[y][x, z] = piece
                    else:
                        outs[2 + x][y, z] = piece


def sum_half_kernel(a_ref, ga_ref, b_ref, gb_ref, keep_ref, sa_ref, sb_ref):
    for k, (r, g, send_ref) in enumerate(((a_ref, ga_ref, sa_ref), (b_ref, gb_ref, sb_ref))):
        for z in range(r.shape[1]):
            keep_ref[k, z] = (r[0, z].astype(F32) + g[0, z].astype(F32)).astype(BF)
            send_ref[z] = (r[1, z].astype(F32) + g[1, z].astype(F32)).astype(BF)


def sum_last_kernel(keep_ref, a_ref, b_ref, own_ref, *send_refs):
    for k, g in enumerate((a_ref, b_ref)):
        for z in range(keep_ref.shape[1]):
            total = keep_ref[k, z].astype(F32) + g[z].astype(F32)
            if z == 0:
                own_ref[k] = total
            else:
                send_refs[z - 1][k] = total.astype(BF)


def ln1_back_kernel(part_ref, got_ref, dr2_ref, n_ref, s_ref, wide_ref, dr1_ref, low_ref, vec_ref):
    start_sums(vec_ref)
    up = part_ref[...] + got_ref[...].astype(F32) + dr2_ref[...]
    normed = n_ref[...]
    dr1 = norm_back(up, normed, s_ref[...], wide_ref[1:2])
    dr1_ref[...] = dr1
    low_ref[...] = dr1.astype(BF)
    vec_ref[0:1] += colsum(dr1)
    vec_ref[1:2] += colsum(up * normed)
    vec_ref[2:3] += colsum(up)


def attn_bwd_kernel(nh, proj_ref, w_ref, aux_ref, ctx_ref, da_ref, db_ref, lse_ref, out_ref, sum_ref, do_ref, dqt_ref):
    n = proj_ref.shape[0]
    half = n // 2
    scale = HS**-0.5
    cols = slice(8 * HS, 12 * HS)
    for i, ref in enumerate((da_ref, db_ref)):
        do_ref[i * half : (i + 1) * half] = dot(ref[...], w_ref[:, cols], 1, 0).astype(BF)
    qb = [block(proj_ref, i) for i in (0, 1)]
    qt = [jnp.transpose(q.astype(F32)) * (scale * LOG2E) for q in qb]
    hi = [q.astype(BF) for q in qt]
    lo = [(q - h.astype(F32)).astype(BF) for q, h in zip(qt, hi)]
    kt = [jnp.transpose(block(proj_ref, i).astype(F32)).astype(BF) for i in (1, 2)]
    dob = [block(do_ref, i) for i in (0, 1)]
    dot_f = [jnp.transpose(d.astype(F32)) for d in dob]
    dot_b = [d.astype(BF) for d in dot_f]
    prod = [d * jnp.transpose(block(ctx_ref, i).astype(F32)) for i, d in enumerate(dot_f)]
    lane = lax.broadcasted_iota(jnp.int32, (n, 128), 1)
    row = lax.broadcasted_iota(jnp.int32, (128, QB), 0)
    zero = jnp.zeros((64, QB), BF)
    empty = jnp.zeros((n, 128), BF)
    dqt_ref[...] = jnp.zeros(dqt_ref.shape, F32)
    dk, dv = [], []
    for h in range(nh):
        kb, kh = ((1, 1), (2, 0), (2, 1))[h]
        i, ih = h // 2, h % 2
        vi, vh = ((3, 0), (3, 1), (4, 0))[h]
        oi, oh = ((0, 1), (1, 0), (1, 1))[h]
        lhs = jnp.concatenate([doubled(block(proj_ref, kb), kh), aux_ref[...]], axis=1)
        lhs_v = jnp.concatenate([block(proj_ref, vi), aux_ref[...]], axis=1)
        r = slice(64 * ih, 64 * ih + 64)
        ro = slice(64 * oh, 64 * oh + 64)
        rk = slice(64 * kh, 64 * kh + 64)
        qm = jnp.where((lane < 64) == (ih == 0), qb[i], empty)
        dom = jnp.where((lane < 64) == (oh == 0), dob[oi], empty)
        dsum = jnp.sum(prod[oi][ro], axis=0, keepdims=True)
        l1, l2, l3 = split3(-lse_ref[h : h + 1, :])
        d1, d2, d3 = split3(-dsum)
        dkh = jnp.zeros((n, 128), F32)
        dvh = jnp.zeros((n, 128), F32)
        for b in range(n // QB):
            s = slice(b * QB, b * QB + QB)

            def pieces(first, x1, x2, x3):
                z = jnp.where(row == 1, x1[:, s].astype(F32), jnp.where(row == 0, first, 0.0))
                z = jnp.where(row == 2, x2[:, s].astype(F32), z)
                return jnp.where(row == 3, x3[:, s].astype(F32), z).astype(BF)

            rhs = jnp.concatenate([hi[i][r, s], lo[i][r, s], pieces(1.0, l1, l2, l3)], axis=0)
            p = jnp.exp2(dot(lhs, rhs, 1, 0))
            g = dot_b[oi][ro, s]
            part = [g, zero] if vh == 0 else [zero, g]
            rhs_v = jnp.concatenate(part + [pieces(0.0, d1, d2, d3)], axis=0)
            ds = (p * dot(lhs_v, rhs_v, 1, 0)).astype(BF)
            dvh = dvh + dot(p.astype(BF), dom[s], 1, 0)
            dkh = dkh + dot(ds, qm[s], 1, 0)
            dqt_ref[64 * h : 64 * h + 64, s] = dot(kt[kb - 1][rk], ds, 1, 0)
        dk.append(dkh * scale)
        dv.append(dvh)

    def put(i, x):
        out_ref[:, 128 * i : 128 * i + 128] = x.astype(BF)
        sum_ref[:, 128 * i : 128 * i + 128] = jnp.broadcast_to(colsum(x.astype(BF).astype(F32)), (8, 128))

    left = lane < 64
    put(0, jnp.transpose(dqt_ref[0:128] * scale))
    put(1, jnp.where(left, jnp.transpose(dqt_ref[128:256] * scale), swap64(dk[0])))
    put(2, jnp.where(left, swap64(dk[1]), swap64(dk[2])))
    put(3, jnp.where(left, swap64(dv[0]), swap64(dv[1])))
    put(4, jnp.where(left, swap64(dv[2]), 0.0))


def attn_bwd(nh, proj, w, aux, ctx, da, db, lse):
    n = proj.shape[0]
    return call(
        functools.partial(attn_bwd_kernel, nh),
        [sds((n, 10 * HS), BF), sds((8, 10 * HS))],
        [proj, w, aux, ctx, da, db, lse],
        None,
        [pltpu.VMEM((n, 4 * HS), BF), pltpu.VMEM((4 * HS, n), F32)],
        "attn_bwd",
        flops=11_000_000_000,
    )


def token_grad_kernel(g0_ref, g1_ref, w0_ref, w1_ref, dr1_ref, send_ref, own_ref):
    n = g0_ref.shape[0]
    half = n // 2
    cols = slice(0, 10 * HS)
    for out_ref, s in ((send_ref, slice(half, n)), (own_ref, slice(0, half))):
        part = dot(g0_ref[s], w0_ref[:, cols], 1, 1) + dot(g1_ref[s], w1_ref[:, cols], 1, 1)
        if out_ref is own_ref:
            part = part + dr1_ref[...]
        out_ref[...] = part.astype(out_ref.dtype)


def qkv_grad_kernel(nh, info, x0, x1, g_in, da, db, ctx_ref, sum_ref, *rest):
    *outs, g_ref, t_ref = rest
    half = x0.shape[0]
    g = dot(x0[...], g_in[:half], 0, 0) + dot(x1[...], g_in[half:], 0, 0)
    o = dot(da[...], ctx_ref[:half], 0, 0) + dot(db[...], ctx_ref[half:], 0, 0)
    g = jnp.concatenate([g[:, : 8 * HS], g[:, 8 * HS :] + o[:, : 2 * HS], o[:, 2 * HS :]], axis=1)
    store_grad(info, 0, 0, g, g_ref, outs)
    if len(outs) == 2:
        nz = outs[0].shape[1]
        rows = D // (2 * nz)
        piece = HS // nz
        zero = jnp.zeros((1, 128 - nh * piece), F32)
        for a in range(2 * nz):
            base = (a % nz) * piece + (a // nz) * 2 * nh * HS
            cuts = [sum_ref[0:1, base + h * HS : base + h * HS + piece] for h in range(nh)]
            t_ref[a : a + 1] = jnp.concatenate([*cuts, zero], axis=1)
        for z in range(nz):
            for x in range(2):
                outs[x][0, z, rows:] = jnp.zeros((outs[x].shape[2] - rows, D), BF)
                row = t_ref[pl.ds(info[0] ^ (2 * z + x), 1), :]
                outs[x][0, z, rows : rows + 8, :128] = jnp.broadcast_to(row, (8, 128)).astype(BF)


def place_kernel(info, a_ref, b_ref, c_ref, d_ref, out_ref):
    c, y = info[1], info[2]
    out_ref[0, y, c] = a_ref[0]
    out_ref[0, 1 - y, c] = b_ref[0]
    out_ref[0, y, 1 - c] = c_ref[0]
    out_ref[0, 1 - y, 1 - c] = d_ref[0]


def lanes(x):
    x = x.reshape(1, -1) if x.ndim == 1 else x
    return jnp.pad(x, ((0, 0), (0, 128 - x.shape[1])))


def vectors_kernel(sizes, info, a0, a1, wide_ref, narrow_ref, b_ref, sems):
    rows, cr, nh, _ = sizes
    wait(load_rows(info, [a0, a1], 0, b_ref, sems))
    nd = b_ref.shape[0]
    for out_ref, row, count, width in ((wide_ref, nh, 6, rows), (narrow_ref, nh + 6, 3, cr)):
        out_ref[...] = jnp.zeros(out_ref.shape, F32)
        for i in range(count):
            cuts = [b_ref[a, row + i : row + i + 1, :width] for a in range(nd)]
            out_ref[i : i + 1] = jnp.concatenate(cuts, axis=1).astype(F32)


def matrices_kernel(info, a0, a1, sw_ref, pooler_ref, class_ref, b_ref, c_ref, sems):
    copies = load_rows(info, [a0, a1], 0, b_ref, sems.at[0])
    copies += load_rows(info, [a0, a1], 1, c_ref, sems.at[1])
    wait(copies)
    for a in range(b_ref.shape[0]):
        for i in range(2):
            at = slice(16 * a + 8 * i, 16 * a + 8 * i + 8)
            pooler_ref[at] = b_ref[a, 8:16, 128 * i : 128 * i + 128].astype(F32)
            class_ref[at] = b_ref[a, 8:16, 256 + 128 * i : 384 + 128 * i].astype(F32)
        for i in range(6):
            at = 96 * a + 16 * i
            sw_ref[at : at + 16] = c_ref[a, :, 128 * i : 128 * i + 128]


def unpack_kernel(sizes, in_ref, sw_ref, pooler_ref, class_ref, wide_ref, narrow_ref, bias_ref):
    rows, cr, nh, nr = sizes
    nd = in_ref.shape[0]
    blocks = [in_ref[d].astype(F32) for d in range(nd)]
    at = rows + 2 * cr

    def joined(first, count, width):
        return jnp.concatenate([b[first : first + count, :width] for b in blocks], axis=1)

    sw_ref[...] = jnp.concatenate([b[:rows] for b in blocks], axis=0).astype(BF)
    pooler_ref[...] = jnp.concatenate([b[rows : rows + cr] for b in blocks], axis=0)
    class_ref[...] = jnp.concatenate([b[rows + cr : at] for b in blocks], axis=0)
    wide_ref[...] = jnp.zeros(wide_ref.shape, F32)
    wide_ref[0:6] = joined(at, 6, rows)
    narrow_ref[...] = jnp.zeros(narrow_ref.shape, F32)
    narrow_ref[0:3] = joined(at + 6, 3, cr)
    bias_ref[...] = jnp.zeros(bias_ref.shape, F32)
    bias_ref[0:nh, :] = joined(at + 9, nh, 2 * HS // nd)
    bias_ref[nh : nh + nr, :HS] = joined(at + 9 + nh, nr, HS // nd)


def pack_grads_kernel(sizes, info, gst, gpool, gclass, v1, v2, nv, ub0, ub1, rep, out_ref):
    rows, cr, nh, nr = sizes
    nd = out_ref.shape[0]
    fw = nr * HS
    me = info[2] * 2 + info[1]
    ub = ub0[0:1] + ub1[0:1]
    pair = [
        jnp.concatenate([ub[:, y * fw + r * HS : y * fw + (r + 1) * HS] for r in range(nr)], axis=0) for y in range(2)
    ]
    quads = jnp.concatenate(
        [jnp.where(me == q, pair[0], jnp.where((me ^ 2) == q, pair[1], 0.0)) for q in range(4)], axis=0
    )
    wide = jnp.concatenate([v1[0:1], v1[1:2], v1[2:3], v2[0:1], v2[1:2], v2[2:3]], axis=0)

    def wider(x):
        return jnp.concatenate([x, jnp.zeros((x.shape[0], 128 - x.shape[1]), F32)], axis=1)

    total = 2 * nd
    row = lax.broadcasted_iota(jnp.int32, (total, 128), 0)
    high = rep[0:1].astype(BF).astype(F32)
    mine = row == 2 * info[0] + info[2]
    table = [jnp.where(mine, high, 0.0), jnp.where(mine, rep[0:1] - high, 0.0)]
    hs = HS // nd
    for d in range(nd):
        parts = [
            gst[d * rows : (d + 1) * rows],
            gpool[d * cr : (d + 1) * cr],
            gclass[d * cr : (d + 1) * cr],
            wider(wide[:, d * rows : (d + 1) * rows]),
            wider(nv[0:3, d * cr : (d + 1) * cr]),
            wider(quads[:, d * hs : (d + 1) * hs]),
            *table,
        ]
        parts = jnp.concatenate(parts, axis=0)
        out_ref[d, : parts.shape[0]] = parts
        if parts.shape[0] < out_ref.shape[1]:
            out_ref[d, parts.shape[0] :] = jnp.zeros((out_ref.shape[1] - parts.shape[0], 128), F32)


def body(
    hidden_in,
    cotangent,
    lengths,
    labels,
    qkv_weight,
    qv_bias,
    out_weight,
    out_bias,
    norm1_gain,
    norm1_bias,
    up_weight,
    up_bias,
    down_weight,
    down_bias,
    norm2_gain,
    norm2_bias,
    student_weight,
    student_bias,
    pool_query,
    pooler_weight,
    pooler_bias,
    class_weight,
    class_bias,
):
    nd = lax.axis_size("dp")
    me = lax.axis_index("dp")
    m = lax.axis_index("mp")
    c, y = m % 2, m // 2
    total, pd, _ = hidden_in.shape
    assert total == 2 * nd and lax.axis_size("mp") == 4
    hp = pd // 2
    half = nd * hp
    rows, cr = D // nd, CW // nd
    nh, nr = qv_bias.shape[0], up_bias.shape[0]
    hw, fw = nh * HS, nr * HS
    fast = nd == 8
    sizes = (rows, cr, nh, nr)
    seq = 2 * me + y
    length = lengths[seq]
    info = jnp.stack([me, c, y, labels[seq]]).astype(jnp.int32)

    def deal(x):
        x = x.reshape(nd, 2, 2, hp, D)
        x = lax.dynamic_slice(x, (0, y, c, 0, 0), (nd, 1, 1, hp, D)).reshape(nd, hp, D)
        return lax.all_to_all(x, "dp", 0, 0, tiled=True).reshape(half, D)

    def undeal(x):
        return lax.all_to_all(x.reshape(nd, hp, D), "dp", 0, 0, tiled=True)

    def place(a, b):
        one = pl.BlockSpec((1, hp, D), lambda d: (d, 0, 0))
        out = pl.pallas_call(
            place_kernel,
            grid=(nd,),
            in_specs=[SMEM] + [one] * 4,
            out_specs=pl.BlockSpec((1, 2, 2, hp, D), lambda d: (d, 0, 0, 0, 0)),
            out_shape=sds((nd, 2, 2, hp, D), BF),
            cost_estimate=cost(6_000_000),
            compiler_params=room(8),
            name="place",
        )(info, a, b, hop(a, 0, 1), hop(b, 0, 1))
        return out.reshape(total, pd, D)

    qo = jnp.concatenate([jnp.transpose(qkv_weight, (1, 0, 2)).reshape(rows, 3 * hw), out_weight.T], axis=1)
    if fast:
        vectors = [qv_bias]
        vectors += [v[None] for v in (out_bias, norm1_gain, norm1_bias, down_bias, norm2_gain, norm2_bias)]
        vectors += [v[None] for v in (student_bias, pool_query, pooler_bias)]
        vectors = [jnp.pad(v, ((0, 0), (0, 128 - v.shape[1]))) for v in vectors]
        vectors = jnp.concatenate([*vectors, jnp.zeros((7 - nh, 128), BF)], axis=0)
        qo = jnp.concatenate([qo, jnp.pad(vectors, ((0, 0), (0, D - 128)))], axis=0)
    qo_got = gather_lines(qo[None])
    qo_line = join_lines(qo_got)
    tokens = deal(after(hidden_in, qo_got[1:]))
    w_qo = gather_planes(qo_line, fast)
    w_qo = (w_qo[:2], w_qo[2:]) if fast else (w_qo[:1], w_qo[1:])
    up_pack, down_pack = up_weight, down_weight.T
    if fast:
        row = jnp.pad(up_bias.reshape(1, -1), ((0, 7), (0, D - up_bias.size)))
        cls = lanes(class_weight)
        more = jnp.concatenate([pooler_weight[:8], pooler_weight[8:], cls[:8], cls[8:]], axis=1)
        more = jnp.pad(more, ((0, 0), (0, D - 512)))
        up_pack = jnp.concatenate([up_pack, row, more], axis=0)
        more = jnp.concatenate([student_weight[16 * i : 16 * i + 16] for i in range(6)], axis=1)
        down_pack = jnp.concatenate([down_pack, more], axis=0)
    f_line, f_got = gather_doubling(after(jnp.stack([up_pack, down_pack]), qo_got[1:]))
    class_b = lanes(class_bias.astype(F32))
    cot = deal(after(cotangent, f_got))

    index = jnp.arange(half, dtype=jnp.int32)
    position = (index // hp) * pd + index % hp
    position = jnp.concatenate([position + c * hp, position + (1 - c) * hp])
    col = jnp.arange(128, dtype=jnp.int32)[None, :]
    aux = jnp.where(
        col == 0, jnp.where(position < length, 0.0, NEGATIVE)[:, None], jnp.where(col <= 3, 1.0, 0.0)
    ).astype(BF)
    aux_own = aux[:half]

    sib = hop(after(tokens, w_qo, f_got[0]), 0, 1)
    n = 2 * half
    biases = [aux, aux]
    if not fast:
        piece = jnp.broadcast_to(qv_bias[None], (nd, *qv_bias.shape))
        piece = lax.all_to_all(piece, "dp", 0, 0, tiled=True)
        piece = jnp.transpose(piece, (1, 0, 2)).reshape(nh, 2 * HS)
        piece = jnp.pad(piece, ((0, 16 - nh), (0, 0)))
        biases = [piece, hop(piece, 0, 2)]
    proj0, w0, ctx0, lse0 = attn_fwd(nh, info, tokens, sib, biases[0], aux, w_qo[0])
    if fast:
        wide, narrow = call(
            functools.partial(vectors_kernel, sizes),
            [sds((8, D)), sds((8, CW))],
            [info, *w_qo[0]],
            [SMEM, ANY, ANY],
            [pltpu.VMEM((nd, 16, D), BF), pltpu.SemaphoreType.DMA((nd,))],
            "vectors",
        )
        bias_near = bias_far = aux
    else:
        small = jnp.concatenate(
            [student_weight, pooler_weight]
            + [
                lanes(v)
                for v in (
                    class_weight,
                    out_bias,
                    norm1_gain,
                    norm1_bias,
                    down_bias,
                    norm2_gain,
                    norm2_bias,
                    student_bias,
                    pool_query,
                    pooler_bias,
                    qv_bias,
                    up_bias,
                )
            ],
            axis=0,
        )
        small = jnp.pad(small, ((0, -small.shape[0] % 16), (0, 0)))
        small = lax.all_to_all(jnp.broadcast_to(small[None], (nd, *small.shape)), "dp", 0, 0, tiled=True)
        student_w, pooler_f, class_f, wide, narrow, bias_near = call(
            functools.partial(unpack_kernel, sizes),
            [sds((D, CW), BF), sds((CW, CW)), sds((CW, CW)), sds((8, D)), sds((8, CW)), sds((16, 128))],
            [small],
            name="unpack",
        )
        bias_near = bias_near.astype(BF)
        bias_far = hop(bias_near, 0, 2)
    proj1, w1, ctx1, lse1 = attn_fwd(nh, info, tokens, sib, biases[1], after(aux, ctx0), w_qo[1])
    w_ffn = gather_planes(f_line, fast)

    if fast:
            ctx1 = after(ctx1, wide)

    def out(first, kind):
        return call(
            functools.partial(out_kernel, first), [sds((half, D), kind)], [ctx0, ctx1, w0, w1], name="out"
        )[0]

    att_got = hop(out(half, BF), 0, 1)
    att_part = out(0, F32)
    first, first_low, n1, s1, sq1 = by_rows(
        ln1_kernel,
        [sds((half, D)), sds((half, D), BF), sds((half, D)), sds((half, 1))],
        [sds((1, 128))],
        [att_part, att_got, tokens, aux_own],
        [wide],
        name="ln1",
    )
    first_sib = hop(after(first_low, w_ffn, cot), 0, 1)

    if fast:
        student_w, pooler_f, class_f = call(
            matrices_kernel,
            [sds((D, CW), BF), sds((CW, CW)), sds((CW, CW))],
            [info, *w_ffn[:2]],
            [SMEM, ANY, ANY],
            [pltpu.VMEM((nd, 16, D), BF)] * 2 + [pltpu.SemaphoreType.DMA((2, nd))],
            "matrices",
        )

    def ffn_up(x):
        return call(
            functools.partial(ffn_up_kernel, nh, nr),
            [sds((half, 2 * fw), BF), sds((half, 2 * fw), BF)],
            [info, x, bias_near, bias_far, *w_ffn],
            [SMEM] + [None] * 3 + [ANY] * len(w_ffn),
            weight_scratch(w_ffn)
            + [pltpu.VMEM((max(nd, 8), 8, D), BF)] * 2
            + [pltpu.SemaphoreType.DMA((nd,))],
            "ffn_up",
        )

    def product(a, k, kind):
        return call(
            functools.partial(product_kernel, k),
            [sds((half, D), kind)],
            [info, a, *w_ffn],
            [SMEM, None] + [ANY] * len(w_ffn),
            weight_scratch(w_ffn),
            "product",
        )[0]

    act, slope = ffn_up(first_low)
    act_sib, slope_sib = ffn_up(after(first_sib, act))
    ffn_got = hop(product(act_sib, 1, BF), 0, 1)
    ffn_part = product(act, 1, F32)
    second_low, n2, s2, student, pool_logit, stat = by_rows(
        ln2_kernel,
        [sds((half, D), BF), sds((half, D)), sds((half, 1)), sds((half, CW)), sds((half, CW))],
        [sds((8, 128))],
        [ffn_part, ffn_got, first, aux_own],
        [wide, narrow, student_w],
        name="ln2",
    )
    hidden_a = undeal(second_low)
    hidden_b = hop(hidden_a, 0, 2)

    dr2, dffn, g_st, g_pool, g_class, report, vec2, nvec, _ = by_rows(
        head_kernel,
        [sds((half, D)), sds((half, D), BF)],
        [
            sds((D, CW)),
            sds((CW, CW)),
            sds((CW, CW)),
            sds((8, 128)),
            sds((8, D)),
            sds((8, CW)),
            sds((8, 128)),
        ],
        [student, pool_logit, second_low, cot, n2, s2],
        [stat, hop(stat, 0, 1), sq1, pooler_f, class_f, class_b, narrow, student_w, wide],
        info,
        "head",
    )
    dffn_sib = hop(dffn, 0, 1)

    def ffn_back(g, s):
        return call(
            ffn_back_kernel,
            [sds((half, 2 * fw), BF), sds((8, 2 * fw))],
            [info, g, s, *w_ffn],
            [SMEM, None, None] + [ANY] * len(w_ffn),
            weight_scratch(w_ffn),
            "ffn_back",
        )

    dpre, ub0 = ffn_back(dffn, slope)
    dpre_sib, ub1 = ffn_back(after(dffn_sib, dpre, hidden_a), slope_sib)
    dfirst_got = hop(product(dpre_sib, 0, BF), 0, 1)
    dfirst_part = product(dpre, 0, F32)
    f_grads = call(
        ffn_grad_kernel,
        grad_outs(2, 2, nd, rows, fast),
        [info, first_low, first_sib, dpre, dpre_sib, dffn, dffn_sib, act, act_sib],
        [SMEM] + [None] * 8,
        [pltpu.VMEM((D, D), F32)],
        "ffn_grad",
    )
    dr1, dattn, vec1 = by_rows(
        ln1_back_kernel,
        [sds((half, D)), sds((half, D), BF)],
        [sds((8, D))],
        [dfirst_part, dfirst_got, after(dr2, hidden_b), n1, s1],
        [wide],
        name="ln1_back",
    )
    dattn_sib = hop(dattn, 0, 1)
    dattn_sib = after(dattn_sib, f_grads, hidden_b)
    if fast:
        up_keep, up_send, down_keep, down_send = f_grads
        up_got, down_got = hop(up_send, 0, 2), hop(down_send, 1, 0)
    count = rows + 2 * cr + 9 + 4 * nr + 2 * total
    (small_g,) = call(
        functools.partial(pack_grads_kernel, sizes),
        [sds((nd, count + -count % 16, 128))],
        [info, g_st, g_pool, g_class, vec1, vec2, nvec, ub0, ub1, report],
        [SMEM] + [None] * 9,
        name="pack",
    )
    small_g = small_g + hop(small_g.astype(BF), 0, 1).astype(F32)
    small_y = small_g + hop(small_g.astype(BF), 0, 2).astype(F32)


    def qkv_grad(g, ctx, sums):
        return call(
            functools.partial(qkv_grad_kernel, nh),
            grad_outs(1, 1, nd, rows, fast, 8),
            [info, tokens, sib, g, dattn, dattn_sib, ctx, sums],
            [SMEM] + [None] * 7,
            [pltpu.VMEM((D, D), F32), pltpu.VMEM((max(8, nd), 128), F32)],
            "qkv_grad",
        )

    g1, g1_sum = attn_bwd(nh, proj1, w1, aux, ctx1, dattn, after(dattn_sib, small_y), lse1)
    far_grad = qkv_grad(g1, ctx1, g1_sum)
    if fast:
        far_got = [hop(g, 0, 2) for g in far_grad]
    g0, g0_sum = attn_bwd(
        nh, proj0, w0, aux, ctx0, dattn, after(dattn_sib, g1, far_grad), lse0
    )
    if fast:
        g0, up_got, down_got = lax.optimization_barrier((g0, up_got, down_got))
    tok_send, tok_own = call(
        token_grad_kernel, [sds((half, D), BF), sds((half, D))], [g0, g1, w0, w1, dr1], name="token_grad"
    )
    near_grad = qkv_grad(g0, ctx0, g0_sum)
    tok_sum = after((tok_own + hop(tok_send, 0, 1).astype(F32)).astype(BF), near_grad)
    input_a = undeal(tok_sum)
    if fast:
        block_ = (nd // 2, rows, D)
        f_keep, up_half, down_half = call(
            sum_half_kernel,
            [sds((2, *block_), BF), sds(block_, BF), sds(block_, BF)],
            [up_keep, up_got, down_keep, down_got],
            name="grad_half",
        )
        f_sums = call(
            sum_last_kernel,
            [sds((2, rows, D))] + [sds((2, rows, D), BF)] * (nd // 2 - 1),
            [f_keep, hop(up_half, 1, 0), hop(down_half, 0, 2)],
            name="grad_sum",
        )
        f_sum = finish_lines(f_sums)
        near_part = (near_grad[1].astype(F32) + far_got[1].astype(F32)).astype(BF)
        qo_own = (near_grad[0], far_got[0], hop(near_part, 1, 0))
    else:
        qo_own = ()
        f_sums = f_sum = sum_lines(f_grads)
    hidden_out = place(hidden_a, hidden_b)
    input_b = hop(after(input_a, hidden_out, f_sums, qo_own[1:]), 0, 2)
    small_g = lax.all_to_all(after(small_y.astype(BF), input_b), "dp", 0, 0, tiled=True).astype(F32).sum(0)
    input_grad = place(input_a, input_b)
    up_sum, down_sum = f_sum
    if fast:
        qo_sum = finish_lines(sum_blocks(qo_own))[0]
    else:
        qo_sum = sum_lines([*near_grad, *far_grad])[0]

    width = 2 * HS // nd
    if fast:
        g_qv = qo_sum[rows, : nh * width].reshape(nh, width)
        qo_sum = qo_sum[:rows]
    else:
        g_qv = [
            jnp.concatenate([g[0, :hw].reshape(nh, HS), g[0, 2 * hw : 3 * hw].reshape(nh, HS)], axis=1)
            for g in (g0_sum, g1_sum)
        ]
        g_qv = g_qv[0] + hop(g_qv[1], 0, 2)
        bit = 1
        while bit < nd:
            g_qv = g_qv + hop(g_qv, bit, 0)
            bit *= 2
        g_qv = lax.dynamic_slice(g_qv, (0, width * me), (nh, width))

    at = rows + 2 * cr + 9 + 4 * nr
    table = small_g[at : at + total] + small_g[at + total : at + 2 * total]
    logit_all = table[:, :CLASSES]
    class_bias_grad = jnp.sum(table[:, CLASSES : 2 * CLASSES], 0)
    squares = jnp.sum(table[:, 2 * CLASSES : 2 * CLASSES + 8], 0).reshape(2, 4).sum(0)
    rms = jnp.sqrt(squares / (jnp.sum(lengths).astype(F32) * D))

    at = rows + 2 * cr
    g_wide = small_g[at : at + 6, :rows]
    g_narrow = small_g[at + 6 : at + 9, :cr]
    g_ub = lax.dynamic_slice(small_g, (at + 9 + nr * m, 0), (nr, HS // nd))
    return (
        hidden_out,
        logit_all,
        input_grad,
        jnp.transpose(qo_sum[:, : 3 * hw].reshape(rows, 3, hw), (1, 0, 2)),
        g_qv,
        qo_sum[:, 3 * hw :].T,
        g_wide[0],
        g_wide[1],
        g_wide[2],
        up_sum,
        g_ub,
        down_sum.T,
        g_wide[3],
        g_wide[4],
        g_wide[5],
        small_g[:rows],
        g_narrow[0],
        g_narrow[1],
        small_g[rows : rows + cr],
        g_narrow[2],
        small_g[rows + cr : at, :CLASSES],
        class_bias_grad,
        rms,
    )


def solution(mesh):
    rows = P(None, "dp", None)
    vec = P("dp")
    return jax.shard_map(
        body,
        mesh=mesh,
        in_specs=(
            rows,
            rows,
            P(),
            P(),
            P(None, "dp", "mp"),
            P("mp", "dp"),
            P("mp", "dp"),
            vec,
            vec,
            vec,
            P("dp", "mp"),
            P("mp", "dp"),
            P("mp", "dp"),
            vec,
            vec,
            vec,
            P("dp", None),
            vec,
            vec,
            P("dp", None),
            vec,
            P("dp", None),
            P(),
        ),
        out_specs=(
            rows,
            P(),
            rows,
            P(None, "dp", "mp"),
            P("mp", "dp"),
            P("mp", "dp"),
            vec,
            vec,
            vec,
            P("dp", "mp"),
            P("mp", "dp"),
            P("mp", "dp"),
            vec,
            vec,
            vec,
            P("dp", None),
            vec,
            vec,
            P("dp", None),
            vec,
            P("dp", None),
            P(),
            P(),
        ),
        check_vma=False,
    )
```
